128 devices in a mesh: row: 16 (over z_lo, y, core), col: 8 (over z_hi, x).
Axes of the slice: x: 4, y: 4, z: 4 (z_hi: 2, z_lo: 2; z = z_hi * 2 + z_lo), core: 2. Of those that a mesh axis runs over, the one named last changes fastest.
Arguments:
- activations: bfloat16 [3072, 16384], P(('row', 'col')), may hold values from -14 to 14
- tenant_ids: int32 [3072], P(('row', 'col')), may hold values from 0 to 63
- concept_labels: int32 [3072], P(('row', 'col')), may hold values from 0 to 1
Outputs:
- covariance: float32 [16384, 16384], P('row', 'col')
- cross: float32 [128, 16384], P(None, ('row', 'col'))
The draws below stay inside these ranges and needn't reach their ends.
All inputs are finite; a program needn't handle non-finite values.
Results may differ from the reference program's by a relative error of at most 0.0003.
Values may be sent and summed in bfloat16 or wider, within the bound.
A program may use at most 128 MiB of HBM per device.

```python
import math
import jax
import jax.numpy as jnp
import numpy as np

D = 16384
TENANTS = 64
LABELS = 2
TOKENS = 3072


def draw_activations(key, part):
    base_key = jax.random.fold_in(key, 11)
    key_base, key_scale, key_offset = jax.random.split(base_key, 3)
    scales = jnp.exp(jax.random.uniform(key_scale, (D,), jnp.float32, jnp.log(0.4), jnp.log(2.0)))
    offset = jax.random.uniform(key_offset, (D,), jnp.float32, -1.0, 1.0)
    base = jax.random.normal(key_base, (TOKENS, D), jnp.float32)
    values = base * scales[None, :] + offset[None, :]
    values = jnp.clip(values, -14.0, 14.0)
    return values.astype(jnp.bfloat16)


def plant(array, stream_key, low, largest):
    longest = array.shape.index(max(array.shape))
    spots = []
    for shift in (0, 1):
        where = [jax.random.randint(jax.random.fold_in(stream_key, axis), (), 0, length) for axis, length in enumerate(array.shape)]
        where[longest] = (where[longest] + shift) % array.shape[longest]
        spots.append(tuple(where))
    return array.at[spots[0]].set(low).at[spots[1]].set(largest)


def rank_table(amount, slope):
    portions = [(1 << 20) // math.isqrt(grade ** slope) + 1 for grade in range(1, amount + 1)]
    spread = 1 + sum(portions) // (1 << 30)
    return np.cumsum(np.array([max(1, weight // spread) for weight in portions]))


def ranked_ids(stream_key, dims, amount, slope):
    grid = rank_table(amount, slope)
    ticket = jax.random.randint(jax.random.fold_in(stream_key, 1), dims, 0, int(grid[amount - 1]))
    standing = jnp.searchsorted(jnp.asarray(grid, jnp.int32), ticket, side="right")
    return jax.random.permutation(jax.random.fold_in(stream_key, 2), amount)[standing].astype(jnp.int32)


def setup_inputs(seed: int = 0) -> dict:
    key_list = jax.random.split(jax.random.key(seed), 4)
    return {
        "activations": draw_activations(jax.random.fold_in(key_list[3], 71), 0),
        "tenant_ids": plant(ranked_ids(key_list[1], (TOKENS,), TENANTS, 2), jax.random.fold_in(key_list[1], 3), 0, TENANTS - 1).astype(jnp.int32),
        "concept_labels": plant(jax.random.randint(key_list[2], (TOKENS,), 0, LABELS), jax.random.fold_in(key_list[2], 1), 0, LABELS - 1).astype(jnp.int32),
    }


def reference(activations, tenant_ids, concept_labels):
    total = activations.shape[0]
    mean = jnp.sum(activations, axis=0, dtype=jnp.float32) / total
    gram = jnp.dot(activations.T, activations, preferred_element_type=jnp.float32)
    covariance = gram / total - mean[:, None] * mean[None, :]
    groups = TENANTS * LABELS
    codes = tenant_ids * LABELS + concept_labels
    onehot = codes[:, None] == jnp.arange(groups, dtype=jnp.int32)[None, :]
    counts = jnp.sum(onehot.astype(jnp.float32), axis=0)
    sums = jnp.dot(onehot.astype(jnp.bfloat16).T, activations, preferred_element_type=jnp.float32)
    cross = (groups / total) * (sums - counts[:, None] * mean[None, :])
    return covariance, cross
```

```python
import functools

import jax
import jax.numpy as jnp
from jax import lax
from jax.experimental import pallas as pl
from jax.experimental.pallas import tpu as pltpu
from jax.sharding import PartitionSpec as P

TENANTS = 64
LABELS = 2
MESH = pl.DeviceIdType.MESH


def _row_panel_kernel(n_row, n_col, x_ref, code_ref, p_ref, pc_ref,
                      sa, ra, sac, rac, sb, rb, sbc, rbc, lsem):
    r = lax.axis_index("row")
    c = lax.axis_index("col")
    width = p_ref.shape[-1]

    barrier = pltpu.get_barrier_semaphore()
    for k in range(1, n_row):
        pl.semaphore_signal(barrier, 1, device_id=(lax.rem(r + k, n_row), c), device_id_type=MESH)
    for k in range(1, n_col):
        pl.semaphore_signal(barrier, 1, device_id=(r, lax.rem(c + k, n_col)), device_id_type=MESH)
    pl.semaphore_wait(barrier, (n_row - 1) + (n_col - 1))

    own = pltpu.make_async_copy(
        x_ref.at[:, pl.ds(pl.multiple_of(r * width, width), width)], p_ref.at[c, r], lsem.at[0])
    own_codes = pltpu.make_async_copy(code_ref, pc_ref.at[c, r], lsem.at[1])
    own.start()
    own_codes.start()
    phase_a = []
    for k in range(1, n_row):
        dst = lax.rem(r + k, n_row)
        cp = pltpu.make_async_remote_copy(
            src_ref=x_ref.at[:, pl.ds(pl.multiple_of(dst * width, width), width)],
            dst_ref=p_ref.at[c, r],
            send_sem=sa.at[k - 1],
            recv_sem=ra.at[k - 1],
            device_id=(dst, c),
            device_id_type=MESH,
        )
        cc = pltpu.make_async_remote_copy(
            src_ref=code_ref,
            dst_ref=pc_ref.at[c, r],
            send_sem=sac.at[k - 1],
            recv_sem=rac.at[k - 1],
            device_id=(dst, c),
            device_id_type=MESH,
        )
        cp.start()
        cc.start()
        phase_a.append(cp)
        phase_a.append(cc)
    own.wait()
    own_codes.wait()
    for cp in phase_a:
        cp.wait()

    phase_b = []
    for k in range(1, n_col):
        dst = lax.rem(c + k, n_col)
        cp = pltpu.make_async_remote_copy(
            src_ref=p_ref.at[c],
            dst_ref=p_ref.at[c],
            send_sem=sb.at[k - 1],
            recv_sem=rb.at[k - 1],
            device_id=(r, dst),
            device_id_type=MESH,
        )
        cc = pltpu.make_async_remote_copy(
            src_ref=pc_ref.at[c],
            dst_ref=pc_ref.at[c],
            send_sem=sbc.at[k - 1],
            recv_sem=rbc.at[k - 1],
            device_id=(r, dst),
            device_id_type=MESH,
        )
        cp.start()
        cc.start()
        phase_b.append(cp)
        phase_b.append(cc)
    for cp in phase_b:
        cp.wait()


def _row_panel(activations, codes, n_row, n_col):
    tokens = activations.shape[0]
    width = activations.shape[1] // n_row
    any_spec = pl.BlockSpec(memory_space=pl.ANY)
    return pl.pallas_call(
        functools.partial(_row_panel_kernel, n_row, n_col),
        out_shape=(
            jax.ShapeDtypeStruct((n_col, n_row, tokens, width), activations.dtype),
            jax.ShapeDtypeStruct((n_col, n_row, 1, tokens), jnp.int32),
        ),
        in_specs=[any_spec, any_spec],
        out_specs=(any_spec, any_spec),
        scratch_shapes=[
            pltpu.SemaphoreType.DMA((n_row - 1,)),
            pltpu.SemaphoreType.DMA((n_row - 1,)),
            pltpu.SemaphoreType.DMA((n_row - 1,)),
            pltpu.SemaphoreType.DMA((n_row - 1,)),
            pltpu.SemaphoreType.DMA((n_col - 1,)),
            pltpu.SemaphoreType.DMA((n_col - 1,)),
            pltpu.SemaphoreType.DMA((n_col - 1,)),
            pltpu.SemaphoreType.DMA((n_col - 1,)),
            pltpu.SemaphoreType.DMA((2,)),
        ],
        compiler_params=pltpu.CompilerParams(collective_id=0, has_side_effects=True),
    )(activations, codes.reshape(1, tokens))


def shards(activations, tenant_ids, concept_labels):
    local_tokens = activations.shape[0]
    width = activations.shape[1]
    row_count = lax.axis_size("row")
    col_count = lax.axis_size("col")
    groups = TENANTS * LABELS
    codes = tenant_ids * LABELS + concept_labels
    col_piece = lax.all_to_all(activations, "col", split_axis=1, concat_axis=0, tiled=True)
    col_panel = lax.all_gather(col_piece, "row", axis=0, tiled=True)
    row_slots, code_slots = _row_panel(activations, codes, row_count, col_count)
    total = col_panel.shape[0]
    row_width = row_slots.shape[-1]
    row_panel = row_slots.reshape(total, row_width)
    codes_all = code_slots.reshape(total)
    row_view = row_slots
    col_view = col_panel.reshape(row_count, col_count, local_tokens, col_panel.shape[1])
    gram = jnp.einsum("abtf,batg->fg", row_view, col_view, preferred_element_type=jnp.float32)
    mean_row = jnp.sum(row_panel, axis=0, dtype=jnp.float32) / total
    mean_col = jnp.sum(col_panel, axis=0, dtype=jnp.float32) / total
    covariance = gram / total - mean_row[:, None] * mean_col[None, :]
    slice_width = width // (row_count * col_count)
    slice_start = lax.axis_index("col") * slice_width
    mean_slice = lax.dynamic_slice_in_dim(mean_row, slice_start, slice_width)
    group_ids = jnp.arange(groups, dtype=jnp.int32)
    onehot_all = codes_all[:, None] == group_ids[None, :]
    counts = jnp.sum(onehot_all.astype(jnp.float32), axis=0)
    panel_slice = lax.dynamic_slice_in_dim(row_panel, slice_start, slice_width, 1)
    sums = lax.dot_general(
        onehot_all.astype(jnp.bfloat16),
        panel_slice,
        (((0,), (0,)), ((), ())),
        preferred_element_type=jnp.float32,
    )
    cross = groups / total * (sums - counts[:, None] * mean_slice[None, :])
    return (covariance, cross)


def solution(mesh):
    placed = (P(("row", "col"), None), P(("row", "col")), P(("row", "col")))
    return jax.shard_map(
        shards,
        mesh=mesh,
        in_specs=placed,
        out_specs=(P("row", "col"), P(None, ("row", "col"))),
        check_vma=False,
    )
```

```python
import functools

import jax
import jax.numpy as jnp
from jax import lax
from jax.experimental import pallas as pl
from jax.experimental.pallas import tpu as pltpu
from jax.sharding import PartitionSpec as P

TENANTS = 64
LABELS = 2
MESH = pl.DeviceIdType.MESH
Z_HI = 2


def _row_panel_kernel(n_row, n_x, x_ref, code_ref, p_ref, pc_ref,
                      s1, r1, s1c, r1c, s2, r2, s2c, r2c, lsem):
    r = lax.axis_index("row")
    c = lax.axis_index("col")
    zh = c // n_x
    x = lax.rem(c, n_x)
    width = p_ref.shape[-1]
    group = Z_HI * n_row
    me_q = zh * n_row + r
    left = zh * n_x + lax.rem(x + n_x - 1, n_x)
    right = zh * n_x + lax.rem(x + 1, n_x)

    def peer(j):
        q = lax.rem(me_q + j, group)
        return q % n_row, (q // n_row) * n_x + x

    barrier = pltpu.get_barrier_semaphore()
    for j in range(1, group):
        pl.semaphore_signal(barrier, 1, device_id=peer(j), device_id_type=MESH)
    pl.semaphore_signal(barrier, 1, device_id=(r, left), device_id_type=MESH)
    pl.semaphore_signal(barrier, 1, device_id=(r, right), device_id_type=MESH)
    pl.semaphore_wait(barrier, group + 1)

    own = pltpu.make_async_copy(
        x_ref.at[:, pl.ds(pl.multiple_of(r * width, width), width)], p_ref.at[x, zh, r], lsem.at[0])
    own_codes = pltpu.make_async_copy(code_ref, pc_ref.at[x, zh, r], lsem.at[1])
    own.start()
    own_codes.start()
    stage1 = []
    for j in range(1, group):
        pr, pc = peer(j)
        cp = pltpu.make_async_remote_copy(
            src_ref=x_ref.at[:, pl.ds(pl.multiple_of(pr * width, width), width)],
            dst_ref=p_ref.at[x, zh, r],
            send_sem=s1.at[j - 1],
            recv_sem=r1.at[j - 1],
            device_id=(pr, pc),
            device_id_type=MESH,
        )
        cc = pltpu.make_async_remote_copy(
            src_ref=code_ref,
            dst_ref=pc_ref.at[x, zh, r],
            send_sem=s1c.at[j - 1],
            recv_sem=r1c.at[j - 1],
            device_id=(pr, pc),
            device_id_type=MESH,
        )
        cp.start()
        cc.start()
        stage1.append(cp)
        stage1.append(cc)
    own.wait()
    own_codes.wait()
    for cp in stage1:
        cp.wait()

    def send(src, dst, sems, idx, target):
        return pltpu.make_async_remote_copy(
            src_ref=src, dst_ref=dst, send_sem=sems[0].at[idx], recv_sem=sems[1].at[idx],
            device_id=(r, target), device_id_type=MESH)

    a_right = send(p_ref.at[x], p_ref.at[x], (s2, r2), 0, right)
    a_left = send(p_ref.at[x], p_ref.at[x], (s2, r2), 1, left)
    ac_right = send(pc_ref.at[x], pc_ref.at[x], (s2c, r2c), 0, right)
    ac_left = send(pc_ref.at[x], pc_ref.at[x], (s2c, r2c), 1, left)
    for cp in (a_right, a_left, ac_right, ac_left):
        cp.start()
    for cp in (a_right, a_left, ac_right, ac_left):
        cp.wait()

    from_left = lax.rem(x + n_x - 1, n_x)
    from_right = lax.rem(x + 1, n_x)
    b_right = send(p_ref.at[from_left, 0], p_ref.at[from_left, 0], (s2, r2), 2, right)
    b_left = send(p_ref.at[from_right, 1], p_ref.at[from_right, 1], (s2, r2), 3, left)
    bc_right = send(pc_ref.at[from_left, 0], pc_ref.at[from_left, 0], (s2c, r2c), 2, right)
    bc_left = send(pc_ref.at[from_right, 1], pc_ref.at[from_right, 1], (s2c, r2c), 3, left)
    for cp in (b_right, b_left, bc_right, bc_left):
        cp.start()
    for cp in (b_right, b_left, bc_right, bc_left):
        cp.wait()


def _row_panel(activations, codes, n_row, n_col):
    tokens = activations.shape[0]
    width = activations.shape[1] // n_row
    n_x = n_col // Z_HI
    assert n_x == 4
    group = Z_HI * n_row
    any_spec = pl.BlockSpec(memory_space=pl.ANY)
    return pl.pallas_call(
        functools.partial(_row_panel_kernel, n_row, n_x),
        out_shape=(
            jax.ShapeDtypeStruct((n_x, Z_HI, n_row, tokens, width), activations.dtype),
            jax.ShapeDtypeStruct((n_x, Z_HI, n_row, 1, tokens), jnp.int32),
        ),
        in_specs=[any_spec, any_spec],
        out_specs=(any_spec, any_spec),
        scratch_shapes=[
            pltpu.SemaphoreType.DMA((group - 1,)),
            pltpu.SemaphoreType.DMA((group - 1,)),
            pltpu.SemaphoreType.DMA((group - 1,)),
            pltpu.SemaphoreType.DMA((group - 1,)),
            pltpu.SemaphoreType.DMA((4,)),
            pltpu.SemaphoreType.DMA((4,)),
            pltpu.SemaphoreType.DMA((4,)),
            pltpu.SemaphoreType.DMA((4,)),
            pltpu.SemaphoreType.DMA((2,)),
        ],
        compiler_params=pltpu.CompilerParams(collective_id=0, has_side_effects=True),
    )(activations, codes.reshape(1, tokens))


def _col_piece_kernel(n_col, x_ref, o_ref, send_sem, recv_sem, lsem):
    r = lax.axis_index("row")
    c = lax.axis_index("col")
    width = o_ref.shape[-1]
    barrier = pltpu.get_barrier_semaphore()
    for k in range(1, n_col):
        pl.semaphore_signal(barrier, 1, device_id=(r, lax.rem(c + k, n_col)), device_id_type=MESH)
    pl.semaphore_wait(barrier, n_col - 1)
    own = pltpu.make_async_copy(
        x_ref.at[:, pl.ds(pl.multiple_of(c * width, width), width)], o_ref.at[c], lsem.at[0])
    own.start()
    copies = []
    for k in range(1, n_col):
        dst = lax.rem(c + k, n_col)
        cp = pltpu.make_async_remote_copy(
            src_ref=x_ref.at[:, pl.ds(pl.multiple_of(dst * width, width), width)],
            dst_ref=o_ref.at[c],
            send_sem=send_sem.at[k - 1],
            recv_sem=recv_sem.at[k - 1],
            device_id=(r, dst),
            device_id_type=MESH,
        )
        cp.start()
        copies.append(cp)
    own.wait()
    for cp in copies:
        cp.wait()


def _col_piece(activations, n_col):
    tokens = activations.shape[0]
    width = activations.shape[1] // n_col
    any_spec = pl.BlockSpec(memory_space=pl.ANY)
    return pl.pallas_call(
        functools.partial(_col_piece_kernel, n_col),
        out_shape=jax.ShapeDtypeStruct((n_col, tokens, width), activations.dtype),
        in_specs=[any_spec],
        out_specs=any_spec,
        scratch_shapes=[
            pltpu.SemaphoreType.DMA((n_col - 1,)),
            pltpu.SemaphoreType.DMA((n_col - 1,)),
            pltpu.SemaphoreType.DMA((1,)),
        ],
        compiler_params=pltpu.CompilerParams(collective_id=1, has_side_effects=True),
    )(activations)


def shards(activations, tenant_ids, concept_labels):
    local_tokens = activations.shape[0]
    width = activations.shape[1]
    row_count = lax.axis_size("row")
    col_count = lax.axis_size("col")
    n_x = col_count // Z_HI
    groups = TENANTS * LABELS
    codes = tenant_ids * LABELS + concept_labels
    col_piece = _col_piece(activations, col_count)
    col_piece = col_piece.reshape(col_count * local_tokens, col_piece.shape[-1])
    col_panel = lax.all_gather(col_piece, "row", axis=0, tiled=True)
    row_slots, code_slots = _row_panel(activations, codes, row_count, col_count)
    total = col_panel.shape[0]
    row_width = row_slots.shape[-1]
    row_panel = row_slots.reshape(total, row_width)
    codes_all = code_slots.reshape(total)
    col_view = col_panel.reshape(row_count, Z_HI, n_x, local_tokens, col_panel.shape[1])
    gram = jnp.einsum("xhrtf,rhxtg->fg", row_slots, col_view, preferred_element_type=jnp.float32)
    mean_row = jnp.sum(row_panel, axis=0, dtype=jnp.float32) / total
    mean_col = jnp.sum(col_panel, axis=0, dtype=jnp.float32) / total
    covariance = gram / total - mean_row[:, None] * mean_col[None, :]
    slice_width = width // (row_count * col_count)
    slice_start = lax.axis_index("col") * slice_width
    mean_slice = lax.dynamic_slice_in_dim(mean_row, slice_start, slice_width)
    group_ids = jnp.arange(groups, dtype=jnp.int32)
    onehot_all = codes_all[:, None] == group_ids[None, :]
    counts = jnp.sum(onehot_all.astype(jnp.float32), axis=0)
    panel_slice = lax.dynamic_slice_in_dim(row_panel, slice_start, slice_width, 1)
    sums = lax.dot_general(
        onehot_all.astype(jnp.bfloat16),
        panel_slice,
        (((0,), (0,)), ((), ())),
        preferred_element_type=jnp.float32,
    )
    cross = groups / total * (sums - counts[:, None] * mean_slice[None, :])
    return (covariance, cross)


def solution(mesh):
    placed = (P(("row", "col"), None), P(("row", "col")), P(("row", "col")))
    return jax.shard_map(
        shards,
        mesh=mesh,
        in_specs=placed,
        out_specs=(P("row", "col"), P(None, ("row", "col"))),
        check_vma=False,
    )
```

```python
import functools

import jax
import jax.numpy as jnp
from jax import lax
from jax.experimental import pallas as pl
from jax.experimental.pallas import tpu as pltpu
from jax.sharding import PartitionSpec as P

TENANTS = 64
LABELS = 2
MESH = pl.DeviceIdType.MESH
Z_HI = 2


def _row_panel_kernel(n_row, n_x, x_ref, code_ref, p_ref, pc_ref,
                      s1, r1, s1c, r1c, s2, r2, s2c, r2c, lsem):
    r = lax.axis_index("row")
    c = lax.axis_index("col")
    zh = c // n_x
    x = lax.rem(c, n_x)
    width = p_ref.shape[-1]
    left = zh * n_x + lax.rem(x + n_x - 1, n_x)
    right = zh * n_x + lax.rem(x + 1, n_x)
    sources = [(dz, dr) for dz in range(Z_HI) for dr in range(n_row) if dz or dr]

    def peer(dz, dr):
        return lax.rem(r + dr, n_row), lax.rem(zh + dz, Z_HI) * n_x + x

    barrier = pltpu.get_barrier_semaphore()
    for dz, dr in sources:
        pl.semaphore_signal(barrier, 1, device_id=peer(dz, dr), device_id_type=MESH)
    pl.semaphore_signal(barrier, 1, device_id=(r, left), device_id_type=MESH)
    pl.semaphore_signal(barrier, 1, device_id=(r, right), device_id_type=MESH)
    pl.semaphore_wait(barrier, len(sources) + 2)

    own = pltpu.make_async_copy(
        x_ref.at[:, pl.ds(pl.multiple_of(r * width, width), width)], p_ref.at[x, zh, r], lsem.at[0])
    own_codes = pltpu.make_async_copy(code_ref, pc_ref.at[x, zh, r], lsem.at[1])
    own.start()
    own_codes.start()
    stage1 = {0: [], 1: []}
    for i, (dz, dr) in enumerate(sources):
        pr, pc = peer(dz, dr)
        cp = pltpu.make_async_remote_copy(
            src_ref=x_ref.at[:, pl.ds(pl.multiple_of(pr * width, width), width)],
            dst_ref=p_ref.at[x, zh, r],
            send_sem=s1.at[i],
            recv_sem=r1.at[i],
            device_id=(pr, pc),
            device_id_type=MESH,
        )
        cc = pltpu.make_async_remote_copy(
            src_ref=code_ref,
            dst_ref=pc_ref.at[x, zh, r],
            send_sem=s1c.at[i],
            recv_sem=r1c.at[i],
            device_id=(pr, pc),
            device_id_type=MESH,
        )
        cp.start()
        cc.start()
        stage1[min(dz, 1)] += [cp, cc]

    def send(src, dst, sems, idx, target):
        return pltpu.make_async_remote_copy(
            src_ref=src, dst_ref=dst, send_sem=sems[0].at[idx], recv_sem=sems[1].at[idx],
            device_id=(r, target), device_id_type=MESH)

    own.wait()
    own_codes.wait()
    halves = []
    for h, plane in enumerate((zh, 1 - zh)):
        for cp in stage1[h]:
            cp.wait_recv()
        pair = [
            send(p_ref.at[x, plane], p_ref.at[x, plane], (s2, r2), 2 * h, right),
            send(p_ref.at[x, plane], p_ref.at[x, plane], (s2, r2), 2 * h + 1, left),
            send(pc_ref.at[x, plane], pc_ref.at[x, plane], (s2c, r2c), 2 * h, right),
            send(pc_ref.at[x, plane], pc_ref.at[x, plane], (s2c, r2c), 2 * h + 1, left),
        ]
        for cp in pair:
            cp.start()
        halves.append(pair)

    from_left = lax.rem(x + n_x - 1, n_x)
    from_right = lax.rem(x + 1, n_x)
    halves[0][0].wait_recv()
    halves[0][2].wait_recv()
    fwd = [
        send(p_ref.at[from_left, zh], p_ref.at[from_left, zh], (s2, r2), 4, right),
        send(pc_ref.at[from_left, zh], pc_ref.at[from_left, zh], (s2c, r2c), 4, right),
    ]
    for cp in fwd:
        cp.start()
    halves[1][1].wait_recv()
    halves[1][3].wait_recv()
    fwd2 = [
        send(p_ref.at[from_right, 1 - zh], p_ref.at[from_right, 1 - zh], (s2, r2), 5, left),
        send(pc_ref.at[from_right, 1 - zh], pc_ref.at[from_right, 1 - zh], (s2c, r2c), 5, left),
    ]
    for cp in fwd2:
        cp.start()

    for cp in stage1[0] + stage1[1]:
        cp.wait_send()
    for pair in halves:
        for cp in pair:
            cp.wait_send()
    halves[0][1].wait_recv()
    halves[0][3].wait_recv()
    halves[1][0].wait_recv()
    halves[1][2].wait_recv()
    for cp in fwd + fwd2:
        cp.wait()


def _row_panel(activations, codes, n_row, n_col):
    tokens = activations.shape[0]
    width = activations.shape[1] // n_row
    n_x = n_col // Z_HI
    assert n_x == 4
    group = Z_HI * n_row
    any_spec = pl.BlockSpec(memory_space=pl.ANY)
    return pl.pallas_call(
        functools.partial(_row_panel_kernel, n_row, n_x),
        out_shape=(
            jax.ShapeDtypeStruct((n_x, Z_HI, n_row, tokens, width), activations.dtype),
            jax.ShapeDtypeStruct((n_x, Z_HI, n_row, 1, tokens), jnp.int32),
        ),
        in_specs=[any_spec, any_spec],
        out_specs=(any_spec, any_spec),
        scratch_shapes=[
            pltpu.SemaphoreType.DMA((group - 1,)),
            pltpu.SemaphoreType.DMA((group - 1,)),
            pltpu.SemaphoreType.DMA((group - 1,)),
            pltpu.SemaphoreType.DMA((group - 1,)),
            pltpu.SemaphoreType.DMA((6,)),
            pltpu.SemaphoreType.DMA((6,)),
            pltpu.SemaphoreType.DMA((6,)),
            pltpu.SemaphoreType.DMA((6,)),
            pltpu.SemaphoreType.DMA((2,)),
        ],
        compiler_params=pltpu.CompilerParams(collective_id=0, has_side_effects=True),
    )(activations, codes.reshape(1, tokens))


def _col_piece_kernel(n_col, x_ref, o_ref, send_sem, recv_sem, lsem):
    r = lax.axis_index("row")
    c = lax.axis_index("col")
    width = o_ref.shape[-1]
    barrier = pltpu.get_barrier_semaphore()
    for k in range(1, n_col):
        pl.semaphore_signal(barrier, 1, device_id=(r, lax.rem(c + k, n_col)), device_id_type=MESH)
    pl.semaphore_wait(barrier, n_col - 1)
    own = pltpu.make_async_copy(
        x_ref.at[:, pl.ds(pl.multiple_of(c * width, width), width)], o_ref.at[c], lsem.at[0])
    own.start()
    copies = []
    for k in range(1, n_col):
        dst = lax.rem(c + k, n_col)
        cp = pltpu.make_async_remote_copy(
            src_ref=x_ref.at[:, pl.ds(pl.multiple_of(dst * width, width), width)],
            dst_ref=o_ref.at[c],
            send_sem=send_sem.at[k - 1],
            recv_sem=recv_sem.at[k - 1],
            device_id=(r, dst),
            device_id_type=MESH,
        )
        cp.start()
        copies.append(cp)
    own.wait()
    for cp in copies:
        cp.wait()


def _col_piece(activations, n_col):
    tokens = activations.shape[0]
    width = activations.shape[1] // n_col
    any_spec = pl.BlockSpec(memory_space=pl.ANY)
    return pl.pallas_call(
        functools.partial(_col_piece_kernel, n_col),
        out_shape=jax.ShapeDtypeStruct((n_col, tokens, width), activations.dtype),
        in_specs=[any_spec],
        out_specs=any_spec,
        scratch_shapes=[
            pltpu.SemaphoreType.DMA((n_col - 1,)),
            pltpu.SemaphoreType.DMA((n_col - 1,)),
            pltpu.SemaphoreType.DMA((1,)),
        ],
        compiler_params=pltpu.CompilerParams(collective_id=1, has_side_effects=True),
    )(activations)


def shards(activations, tenant_ids, concept_labels):
    local_tokens = activations.shape[0]
    width = activations.shape[1]
    row_count = lax.axis_size("row")
    col_count = lax.axis_size("col")
    n_x = col_count // Z_HI
    groups = TENANTS * LABELS
    codes = tenant_ids * LABELS + concept_labels
    col_piece = _col_piece(activations, col_count)
    col_piece = col_piece.reshape(col_count * local_tokens, col_piece.shape[-1])
    col_panel = lax.all_gather(col_piece, "row", axis=0, tiled=True)
    row_slots, code_slots = _row_panel(activations, codes, row_count, col_count)
    total = col_panel.shape[0]
    row_width = row_slots.shape[-1]
    row_panel = row_slots.reshape(total, row_width)
    codes_all = code_slots.reshape(total)
    col_view = col_panel.reshape(row_count, Z_HI, n_x, local_tokens, col_panel.shape[1])
    gram = jnp.einsum("xhrtf,rhxtg->fg", row_slots, col_view, preferred_element_type=jnp.float32)
    mean_row = jnp.sum(row_panel, axis=0, dtype=jnp.float32) / total
    mean_col = jnp.sum(col_panel, axis=0, dtype=jnp.float32) / total
    covariance = gram / total - mean_row[:, None] * mean_col[None, :]
    slice_width = width // (row_count * col_count)
    slice_start = lax.axis_index("col") * slice_width
    mean_slice = lax.dynamic_slice_in_dim(mean_row, slice_start, slice_width)
    group_ids = jnp.arange(groups, dtype=jnp.int32)
    onehot_all = codes_all[:, None] == group_ids[None, :]
    counts = jnp.sum(onehot_all.astype(jnp.float32), axis=0)
    panel_slice = lax.dynamic_slice_in_dim(row_panel, slice_start, slice_width, 1)
    sums = lax.dot_general(
        onehot_all.astype(jnp.bfloat16),
        panel_slice,
        (((0,), (0,)), ((), ())),
        preferred_element_type=jnp.float32,
    )
    cross = groups / total * (sums - counts[:, None] * mean_slice[None, :])
    return (covariance, cross)


def solution(mesh):
    placed = (P(("row", "col"), None), P(("row", "col")), P(("row", "col")))
    return jax.shard_map(
        shards,
        mesh=mesh,
        in_specs=placed,
        out_specs=(P("row", "col"), P(None, ("row", "col"))),
        check_vma=False,
    )
```

```python
import functools

import jax
import jax.numpy as jnp
from jax import lax
from jax.experimental import pallas as pl
from jax.experimental.pallas import tpu as pltpu
from jax.sharding import PartitionSpec as P

TENANTS = 64
LABELS = 2
MESH = pl.DeviceIdType.MESH
Z_HI = 2


def _row_panel_kernel(n_row, n_x, x_ref, code_ref, p_ref, pc_ref,
                      s1, r1, s1c, r1c, s2, r2, s2c, r2c, lsem):
    r = lax.axis_index("row")
    c = lax.axis_index("col")
    zh = c // n_x
    x = lax.rem(c, n_x)
    width = p_ref.shape[-1]
    left = zh * n_x + lax.rem(x + n_x - 1, n_x)
    right = zh * n_x + lax.rem(x + 1, n_x)
    sources = [(dz, dr) for dz in range(Z_HI) for dr in range(n_row) if dz or dr]

    def peer(dz, dr):
        return lax.rem(r + dr, n_row), lax.rem(zh + dz, Z_HI) * n_x + x

    barrier = pltpu.get_barrier_semaphore()
    for dz, dr in sources:
        pl.semaphore_signal(barrier, 1, device_id=peer(dz, dr), device_id_type=MESH)
    pl.semaphore_signal(barrier, 1, device_id=(r, left), device_id_type=MESH)
    pl.semaphore_signal(barrier, 1, device_id=(r, right), device_id_type=MESH)
    pl.semaphore_wait(barrier, len(sources) + 2)

    own = pltpu.make_async_copy(
        x_ref.at[:, pl.ds(pl.multiple_of(r * width, width), width)], p_ref.at[x, zh, r], lsem.at[0])
    own_codes = pltpu.make_async_copy(code_ref, pc_ref.at[x, zh, r], lsem.at[1])
    own.start()
    own_codes.start()
    stage1 = {0: [], 1: []}
    for i, (dz, dr) in enumerate(sources):
        pr, pc = peer(dz, dr)
        cp = pltpu.make_async_remote_copy(
            src_ref=x_ref.at[:, pl.ds(pl.multiple_of(pr * width, width), width)],
            dst_ref=p_ref.at[x, zh, r],
            send_sem=s1.at[i],
            recv_sem=r1.at[i],
            device_id=(pr, pc),
            device_id_type=MESH,
        )
        cc = pltpu.make_async_remote_copy(
            src_ref=code_ref,
            dst_ref=pc_ref.at[x, zh, r],
            send_sem=s1c.at[i],
            recv_sem=r1c.at[i],
            device_id=(pr, pc),
            device_id_type=MESH,
        )
        cp.start()
        cc.start()
        stage1[min(dz, 1)] += [cp, cc]

    def send(src, dst, sems, idx, target):
        return pltpu.make_async_remote_copy(
            src_ref=src, dst_ref=dst, send_sem=sems[0].at[idx], recv_sem=sems[1].at[idx],
            device_id=(r, target), device_id_type=MESH)

    own.wait()
    own_codes.wait()
    halves = []
    for h, plane in enumerate((zh, 1 - zh)):
        for cp in stage1[h]:
            cp.wait_recv()
        pair = [
            send(p_ref.at[x, plane], p_ref.at[x, plane], (s2, r2), 2 * h, right),
            send(p_ref.at[x, plane], p_ref.at[x, plane], (s2, r2), 2 * h + 1, left),
            send(pc_ref.at[x, plane], pc_ref.at[x, plane], (s2c, r2c), 2 * h, right),
            send(pc_ref.at[x, plane], pc_ref.at[x, plane], (s2c, r2c), 2 * h + 1, left),
        ]
        for cp in pair:
            cp.start()
        halves.append(pair)

    from_left = lax.rem(x + n_x - 1, n_x)
    from_right = lax.rem(x + 1, n_x)
    halves[0][0].wait_recv()
    halves[0][2].wait_recv()
    fwd = [
        send(p_ref.at[from_left, zh], p_ref.at[from_left, zh], (s2, r2), 4, right),
        send(pc_ref.at[from_left, zh], pc_ref.at[from_left, zh], (s2c, r2c), 4, right),
    ]
    for cp in fwd:
        cp.start()
    halves[1][1].wait_recv()
    halves[1][3].wait_recv()
    fwd2 = [
        send(p_ref.at[from_right, 1 - zh], p_ref.at[from_right, 1 - zh], (s2, r2), 5, left),
        send(pc_ref.at[from_right, 1 - zh], pc_ref.at[from_right, 1 - zh], (s2c, r2c), 5, left),
    ]
    for cp in fwd2:
        cp.start()

    for cp in stage1[0] + stage1[1]:
        cp.wait_send()
    for pair in halves:
        for cp in pair:
            cp.wait_send()
    halves[0][1].wait_recv()
    halves[0][3].wait_recv()
    halves[1][0].wait_recv()
    halves[1][2].wait_recv()
    for cp in fwd + fwd2:
        cp.wait()


def _row_panel(activations, codes, n_row, n_col):
    tokens = activations.shape[0]
    width = activations.shape[1] // n_row
    n_x = n_col // Z_HI
    assert n_x == 4
    group = Z_HI * n_row
    any_spec = pl.BlockSpec(memory_space=pl.ANY)
    return pl.pallas_call(
        functools.partial(_row_panel_kernel, n_row, n_x),
        out_shape=(
            jax.ShapeDtypeStruct((n_x, Z_HI, n_row, tokens, width), activations.dtype),
            jax.ShapeDtypeStruct((n_x, Z_HI, n_row, 1, tokens), jnp.int32),
        ),
        in_specs=[any_spec, any_spec],
        out_specs=(any_spec, any_spec),
        scratch_shapes=[
            pltpu.SemaphoreType.DMA((group - 1,)),
            pltpu.SemaphoreType.DMA((group - 1,)),
            pltpu.SemaphoreType.DMA((group - 1,)),
            pltpu.SemaphoreType.DMA((group - 1,)),
            pltpu.SemaphoreType.DMA((6,)),
            pltpu.SemaphoreType.DMA((6,)),
            pltpu.SemaphoreType.DMA((6,)),
            pltpu.SemaphoreType.DMA((6,)),
            pltpu.SemaphoreType.DMA((2,)),
        ],
        compiler_params=pltpu.CompilerParams(collective_id=0, has_side_effects=True),
    )(activations, codes)


def _col_piece_kernel(n_col, x_ref, code_ref, o_ref, code_out, send_sem, recv_sem, lsem):
    r = lax.axis_index("row")
    c = lax.axis_index("col")
    width = o_ref.shape[-1]
    barrier = pltpu.get_barrier_semaphore()
    for k in range(1, n_col):
        pl.semaphore_signal(barrier, 1, device_id=(r, lax.rem(c + k, n_col)), device_id_type=MESH)
    pl.semaphore_wait(barrier, n_col - 1)
    own = pltpu.make_async_copy(
        x_ref.at[:, pl.ds(pl.multiple_of(c * width, width), width)], o_ref.at[c], lsem.at[0])
    own.start()
    copies = []
    for k in range(1, n_col):
        dst = lax.rem(c + k, n_col)
        cp = pltpu.make_async_remote_copy(
            src_ref=x_ref.at[:, pl.ds(pl.multiple_of(dst * width, width), width)],
            dst_ref=o_ref.at[c],
            send_sem=send_sem.at[k - 1],
            recv_sem=recv_sem.at[k - 1],
            device_id=(r, dst),
            device_id_type=MESH,
        )
        cp.start()
        copies.append(cp)
    keep = pltpu.make_async_copy(code_ref, code_out, lsem.at[1])
    keep.start()
    own.wait()
    keep.wait()
    for cp in copies:
        cp.wait()


def _col_piece(activations, codes, n_col):
    tokens = activations.shape[0]
    width = activations.shape[1] // n_col
    any_spec = pl.BlockSpec(memory_space=pl.ANY)
    return pl.pallas_call(
        functools.partial(_col_piece_kernel, n_col),
        out_shape=(
            jax.ShapeDtypeStruct((n_col, tokens, width), activations.dtype),
            jax.ShapeDtypeStruct(codes.shape, codes.dtype),
        ),
        in_specs=[any_spec, any_spec],
        out_specs=(any_spec, any_spec),
        scratch_shapes=[
            pltpu.SemaphoreType.DMA((n_col - 1,)),
            pltpu.SemaphoreType.DMA((n_col - 1,)),
            pltpu.SemaphoreType.DMA((2,)),
        ],
        compiler_params=pltpu.CompilerParams(collective_id=1, has_side_effects=True),
    )(activations, codes)


def _column_sum(panel):
    rows = panel.shape[0]
    part = 32 if rows % 32 == 0 else 1
    first = jnp.sum(panel.reshape(rows // part, part, panel.shape[1]), axis=1, dtype=jnp.float32)
    first = lax.optimization_barrier(first)
    return jnp.sum(first, axis=0)


def shards(activations, tenant_ids, concept_labels):
    local_tokens = activations.shape[0]
    width = activations.shape[1]
    row_count = lax.axis_size("row")
    col_count = lax.axis_size("col")
    n_x = col_count // Z_HI
    groups = TENANTS * LABELS
    codes = tenant_ids * LABELS + concept_labels
    col_piece, codes = _col_piece(activations, codes.reshape(1, local_tokens), col_count)
    col_piece = col_piece.reshape(col_count * local_tokens, col_piece.shape[-1])
    col_panel = lax.all_gather(col_piece, "row", axis=0, tiled=True)
    row_slots, code_slots = _row_panel(activations, codes, row_count, col_count)
    total = col_panel.shape[0]
    row_width = row_slots.shape[-1]
    row_panel = row_slots.reshape(total, row_width)
    col_view = col_panel.reshape(row_count, Z_HI, n_x, local_tokens, col_panel.shape[1])
    gram = jnp.einsum("xhrtf,rhxtg->fg", row_slots, col_view, preferred_element_type=jnp.float32)
    mean_row = _column_sum(row_panel) / total
    mean_col = _column_sum(col_panel) / total
    covariance = gram / total - mean_row[:, None] * mean_col[None, :]
    slice_width = width // (row_count * col_count)
    slice_start = lax.axis_index("col") * slice_width
    mean_slice = lax.dynamic_slice_in_dim(mean_row, slice_start, slice_width)
    group_ids = jnp.arange(groups, dtype=jnp.int32)
    onehot_all = code_slots[..., None] == group_ids
    counts = jnp.sum(onehot_all.astype(jnp.float32), axis=(0, 1, 2, 3, 4))
    panel_slice = lax.dynamic_slice_in_dim(row_slots, slice_start, slice_width, 4)
    sums = jnp.einsum(
        "xhrotg,xhrtf->gf",
        onehot_all.astype(jnp.bfloat16),
        panel_slice,
        preferred_element_type=jnp.float32,
    )
    cross = groups / total * (sums - counts[:, None] * mean_slice[None, :])
    return (covariance, cross)


def solution(mesh):
    placed = (P(("row", "col"), None), P(("row", "col")), P(("row", "col")))
    return jax.shard_map(
        shards,
        mesh=mesh,
        in_specs=placed,
        out_specs=(P("row", "col"), P(None, ("row", "col"))),
        check_vma=False,
    )
```

```python
import functools

import jax
import jax.numpy as jnp
from jax import lax
from jax.experimental import pallas as pl
from jax.experimental.pallas import tpu as pltpu
from jax.sharding import PartitionSpec as P

TENANTS = 64
LABELS = 2
MESH = pl.DeviceIdType.MESH
Z_HI = 2


def _row_panel_kernel(n_row, n_x, x_ref, code_ref, p_ref, pc_ref,
                      s1, r1, s1c, r1c, s2, r2, s2c, r2c, lsem):
    r = lax.axis_index("row")
    c = lax.axis_index("col")
    zh = c // n_x
    x = lax.rem(c, n_x)
    width = p_ref.shape[-1]
    left = zh * n_x + lax.rem(x + n_x - 1, n_x)
    right = zh * n_x + lax.rem(x + 1, n_x)
    sources = [(dz, dr) for dz in range(Z_HI) for dr in range(n_row) if dz or dr]

    def peer(dz, dr):
        return lax.rem(r + dr, n_row), lax.rem(zh + dz, Z_HI) * n_x + x

    barrier = pltpu.get_barrier_semaphore()
    for dz, dr in sources:
        pl.semaphore_signal(barrier, 1, device_id=peer(dz, dr), device_id_type=MESH)
    pl.semaphore_signal(barrier, 1, device_id=(r, left), device_id_type=MESH)
    pl.semaphore_signal(barrier, 1, device_id=(r, right), device_id_type=MESH)
    pl.semaphore_wait(barrier, len(sources) + 2)

    own = pltpu.make_async_copy(
        x_ref.at[:, pl.ds(pl.multiple_of(r * width, width), width)], p_ref.at[x, zh, r], lsem.at[0])
    own_codes = pltpu.make_async_copy(code_ref, pc_ref.at[x, zh, r], lsem.at[1])
    own.start()
    own_codes.start()
    stage1 = {0: [], 1: []}
    for i, (dz, dr) in enumerate(sources):
        pr, pc = peer(dz, dr)
        cp = pltpu.make_async_remote_copy(
            src_ref=x_ref.at[:, pl.ds(pl.multiple_of(pr * width, width), width)],
            dst_ref=p_ref.at[x, zh, r],
            send_sem=s1.at[i],
            recv_sem=r1.at[i],
            device_id=(pr, pc),
            device_id_type=MESH,
        )
        cc = pltpu.make_async_remote_copy(
            src_ref=code_ref,
            dst_ref=pc_ref.at[x, zh, r],
            send_sem=s1c.at[i],
            recv_sem=r1c.at[i],
            device_id=(pr, pc),
            device_id_type=MESH,
        )
        cp.start()
        cc.start()
        stage1[min(dz, 1)] += [cp, cc]

    def send(src, dst, sems, idx, target):
        return pltpu.make_async_remote_copy(
            src_ref=src, dst_ref=dst, send_sem=sems[0].at[idx], recv_sem=sems[1].at[idx],
            device_id=(r, target), device_id_type=MESH)

    own.wait()
    own_codes.wait()
    halves = []
    for h, plane in enumerate((zh, 1 - zh)):
        for cp in stage1[h]:
            cp.wait_recv()
        pair = [
            send(p_ref.at[x, plane], p_ref.at[x, plane], (s2, r2), 2 * h, right),
            send(p_ref.at[x, plane], p_ref.at[x, plane], (s2, r2), 2 * h + 1, left),
            send(pc_ref.at[x, plane], pc_ref.at[x, plane], (s2c, r2c), 2 * h, right),
            send(pc_ref.at[x, plane], pc_ref.at[x, plane], (s2c, r2c), 2 * h + 1, left),
        ]
        for cp in pair:
            cp.start()
        halves.append(pair)

    from_left = lax.rem(x + n_x - 1, n_x)
    from_right = lax.rem(x + 1, n_x)
    halves[0][0].wait_recv()
    halves[0][2].wait_recv()
    fwd = [
        send(p_ref.at[from_left, zh], p_ref.at[from_left, zh], (s2, r2), 4, right),
        send(pc_ref.at[from_left, zh], pc_ref.at[from_left, zh], (s2c, r2c), 4, right),
    ]
    for cp in fwd:
        cp.start()
    halves[1][1].wait_recv()
    halves[1][3].wait_recv()
    fwd2 = [
        send(p_ref.at[from_right, 1 - zh], p_ref.at[from_right, 1 - zh], (s2, r2), 5, left),
        send(pc_ref.at[from_right, 1 - zh], pc_ref.at[from_right, 1 - zh], (s2c, r2c), 5, left),
    ]
    for cp in fwd2:
        cp.start()

    for cp in stage1[0] + stage1[1]:
        cp.wait_send()
    for pair in halves:
        for cp in pair:
            cp.wait_send()
    halves[0][1].wait_recv()
    halves[0][3].wait_recv()
    halves[1][0].wait_recv()
    halves[1][2].wait_recv()
    for cp in fwd + fwd2:
        cp.wait()


def _row_panel(activations, codes, n_row, n_col):
    tokens = activations.shape[0]
    width = activations.shape[1] // n_row
    n_x = n_col // Z_HI
    assert n_x == 4
    group = Z_HI * n_row
    any_spec = pl.BlockSpec(memory_space=pl.ANY)
    return pl.pallas_call(
        functools.partial(_row_panel_kernel, n_row, n_x),
        out_shape=(
            jax.ShapeDtypeStruct((n_x, Z_HI, n_row, tokens, width), activations.dtype),
            jax.ShapeDtypeStruct((n_x, Z_HI, n_row, 1, tokens), jnp.int32),
        ),
        in_specs=[any_spec, any_spec],
        out_specs=(any_spec, any_spec),
        scratch_shapes=[
            pltpu.SemaphoreType.DMA((group - 1,)),
            pltpu.SemaphoreType.DMA((group - 1,)),
            pltpu.SemaphoreType.DMA((group - 1,)),
            pltpu.SemaphoreType.DMA((group - 1,)),
            pltpu.SemaphoreType.DMA((6,)),
            pltpu.SemaphoreType.DMA((6,)),
            pltpu.SemaphoreType.DMA((6,)),
            pltpu.SemaphoreType.DMA((6,)),
            pltpu.SemaphoreType.DMA((2,)),
        ],
        compiler_params=pltpu.CompilerParams(collective_id=0, has_side_effects=True),
    )(activations, codes)


def _col_piece_kernel(n_col, x_ref, code_ref, o_ref, code_out, send_sem, recv_sem, lsem):
    r = lax.axis_index("row")
    c = lax.axis_index("col")
    width = o_ref.shape[-1]
    barrier = pltpu.get_barrier_semaphore()
    for k in range(1, n_col):
        pl.semaphore_signal(barrier, 1, device_id=(r, lax.rem(c + k, n_col)), device_id_type=MESH)
    pl.semaphore_wait(barrier, n_col - 1)
    own = pltpu.make_async_copy(
        x_ref.at[:, pl.ds(pl.multiple_of(c * width, width), width)], o_ref.at[c], lsem.at[0])
    own.start()
    copies = []
    for k in range(1, n_col):
        dst = lax.rem(c + k, n_col)
        cp = pltpu.make_async_remote_copy(
            src_ref=x_ref.at[:, pl.ds(pl.multiple_of(dst * width, width), width)],
            dst_ref=o_ref.at[c],
            send_sem=send_sem.at[k - 1],
            recv_sem=recv_sem.at[k - 1],
            device_id=(r, dst),
            device_id_type=MESH,
        )
        cp.start()
        copies.append(cp)
    keep = pltpu.make_async_copy(code_ref, code_out, lsem.at[1])
    keep.start()
    own.wait()
    keep.wait()
    for cp in copies:
        cp.wait()


def _col_piece(activations, codes, n_col):
    tokens = activations.shape[0]
    width = activations.shape[1] // n_col
    any_spec = pl.BlockSpec(memory_space=pl.ANY)
    return pl.pallas_call(
        functools.partial(_col_piece_kernel, n_col),
        out_shape=(
            jax.ShapeDtypeStruct((n_col, tokens, width), activations.dtype),
            jax.ShapeDtypeStruct(codes.shape, codes.dtype),
        ),
        in_specs=[any_spec, any_spec],
        out_specs=(any_spec, any_spec),
        scratch_shapes=[
            pltpu.SemaphoreType.DMA((n_col - 1,)),
            pltpu.SemaphoreType.DMA((n_col - 1,)),
            pltpu.SemaphoreType.DMA((2,)),
        ],
        compiler_params=pltpu.CompilerParams(collective_id=1, has_side_effects=True),
    )(activations, codes)


def _column_sum(panel):
    ones = jnp.ones((8, panel.shape[0]), panel.dtype)
    return jnp.dot(ones, panel, preferred_element_type=jnp.float32)[0]


def shards(activations, tenant_ids, concept_labels):
    local_tokens = activations.shape[0]
    width = activations.shape[1]
    row_count = lax.axis_size("row")
    col_count = lax.axis_size("col")
    n_x = col_count // Z_HI
    groups = TENANTS * LABELS
    codes = tenant_ids * LABELS + concept_labels
    col_piece, codes = _col_piece(activations, codes.reshape(1, local_tokens), col_count)
    col_piece = col_piece.reshape(col_count * local_tokens, col_piece.shape[-1])
    col_panel = lax.all_gather(col_piece, "row", axis=0, tiled=True)
    row_slots, code_slots = _row_panel(activations, codes, row_count, col_count)
    total = col_panel.shape[0]
    row_width = row_slots.shape[-1]
    row_panel = row_slots.reshape(total, row_width)
    col_view = col_panel.reshape(row_count, Z_HI, n_x, local_tokens, col_panel.shape[1])
    gram = jnp.einsum("xhrtf,rhxtg->fg", row_slots, col_view, preferred_element_type=jnp.float32)
    mean_row = _column_sum(row_panel) / total
    mean_col = _column_sum(col_panel) / total
    covariance = gram / total - mean_row[:, None] * mean_col[None, :]
    slice_width = width // (row_count * col_count)
    slice_start = lax.axis_index("col") * slice_width
    mean_slice = lax.dynamic_slice_in_dim(mean_row, slice_start, slice_width)
    group_ids = jnp.arange(groups, dtype=jnp.int32)
    onehot_all = code_slots[..., None] == group_ids
    counts = jnp.sum(onehot_all.astype(jnp.float32), axis=(0, 1, 2, 3, 4))
    panel_slice = lax.dynamic_slice_in_dim(row_slots, slice_start, slice_width, 4)
    sums = jnp.einsum(
        "xhrotg,xhrtf->gf",
        onehot_all.astype(jnp.bfloat16),
        panel_slice,
        preferred_element_type=jnp.float32,
    )
    cross = groups / total * (sums - counts[:, None] * mean_slice[None, :])
    return (covariance, cross)


def solution(mesh):
    placed = (P(("row", "col"), None), P(("row", "col")), P(("row", "col")))
    return jax.shard_map(
        shards,
        mesh=mesh,
        in_specs=placed,
        out_specs=(P("row", "col"), P(None, ("row", "col"))),
        check_vma=False,
    )
```

```python
import functools

import jax
import jax.numpy as jnp
from jax import lax
from jax.experimental import pallas as pl
from jax.experimental.pallas import tpu as pltpu
from jax.sharding import PartitionSpec as P

TENANTS = 64
LABELS = 2
MESH = pl.DeviceIdType.MESH
Z_HI = 2


def _row_panel_kernel(n_row, n_x, x_ref, code_ref, cs_ref, p_ref, pc_ref, cs_out,
                      s1, r1, s1c, r1c, s2, r2, s2c, r2c, s3, r3, lsem):
    r = lax.axis_index("row")
    c = lax.axis_index("col")
    zh = c // n_x
    x = lax.rem(c, n_x)
    width = p_ref.shape[-1]
    left = zh * n_x + lax.rem(x + n_x - 1, n_x)
    right = zh * n_x + lax.rem(x + 1, n_x)
    sources = [(dz, dr) for dz in range(Z_HI) for dr in range(n_row) if dz or dr]

    def peer(dz, dr):
        return lax.rem(r + dr, n_row), lax.rem(zh + dz, Z_HI) * n_x + x

    barrier = pltpu.get_barrier_semaphore()
    for dz, dr in sources:
        pl.semaphore_signal(barrier, 1, device_id=peer(dz, dr), device_id_type=MESH)
    pl.semaphore_signal(barrier, 1, device_id=(r, left), device_id_type=MESH)
    pl.semaphore_signal(barrier, 1, device_id=(r, right), device_id_type=MESH)
    pl.semaphore_wait(barrier, len(sources) + 2)

    own = pltpu.make_async_copy(
        x_ref.at[:, pl.ds(pl.multiple_of(r * width, width), width)], p_ref.at[x, zh, r], lsem.at[0])
    own_codes = pltpu.make_async_copy(code_ref, pc_ref.at[x, zh, r], lsem.at[1])
    own_sum = pltpu.make_async_copy(cs_ref, cs_out.at[r], lsem.at[2])
    own.start()
    own_codes.start()
    own_sum.start()
    stage1 = {0: [], 1: []}
    sums = []
    for i, (dz, dr) in enumerate(sources):
        pr, pc = peer(dz, dr)
        cp = pltpu.make_async_remote_copy(
            src_ref=x_ref.at[:, pl.ds(pl.multiple_of(pr * width, width), width)],
            dst_ref=p_ref.at[x, zh, r],
            send_sem=s1.at[i],
            recv_sem=r1.at[i],
            device_id=(pr, pc),
            device_id_type=MESH,
        )
        cc = pltpu.make_async_remote_copy(
            src_ref=code_ref,
            dst_ref=pc_ref.at[x, zh, r],
            send_sem=s1c.at[i],
            recv_sem=r1c.at[i],
            device_id=(pr, pc),
            device_id_type=MESH,
        )
        cp.start()
        cc.start()
        stage1[min(dz, 1)] += [cp, cc]
        if dz == 0:
            cs = pltpu.make_async_remote_copy(
                src_ref=cs_ref,
                dst_ref=cs_out.at[r],
                send_sem=s3.at[dr - 1],
                recv_sem=r3.at[dr - 1],
                device_id=(pr, pc),
                device_id_type=MESH,
            )
            cs.start()
            sums.append(cs)

    def send(src, dst, sems, idx, target):
        return pltpu.make_async_remote_copy(
            src_ref=src, dst_ref=dst, send_sem=sems[0].at[idx], recv_sem=sems[1].at[idx],
            device_id=(r, target), device_id_type=MESH)

    own.wait()
    own_codes.wait()
    halves = []
    for h, plane in enumerate((zh, 1 - zh)):
        for cp in stage1[h]:
            cp.wait_recv()
        pair = [
            send(p_ref.at[x, plane], p_ref.at[x, plane], (s2, r2), 2 * h, right),
            send(p_ref.at[x, plane], p_ref.at[x, plane], (s2, r2), 2 * h + 1, left),
            send(pc_ref.at[x, plane], pc_ref.at[x, plane], (s2c, r2c), 2 * h, right),
            send(pc_ref.at[x, plane], pc_ref.at[x, plane], (s2c, r2c), 2 * h + 1, left),
        ]
        for cp in pair:
            cp.start()
        halves.append(pair)

    from_left = lax.rem(x + n_x - 1, n_x)
    from_right = lax.rem(x + 1, n_x)
    halves[0][0].wait_recv()
    halves[0][2].wait_recv()
    fwd = [
        send(p_ref.at[from_left, zh], p_ref.at[from_left, zh], (s2, r2), 4, right),
        send(pc_ref.at[from_left, zh], pc_ref.at[from_left, zh], (s2c, r2c), 4, right),
    ]
    for cp in fwd:
        cp.start()
    halves[1][1].wait_recv()
    halves[1][3].wait_recv()
    fwd2 = [
        send(p_ref.at[from_right, 1 - zh], p_ref.at[from_right, 1 - zh], (s2, r2), 5, left),
        send(pc_ref.at[from_right, 1 - zh], pc_ref.at[from_right, 1 - zh], (s2c, r2c), 5, left),
    ]
    for cp in fwd2:
        cp.start()

    for cp in stage1[0] + stage1[1]:
        cp.wait_send()
    for pair in halves:
        for cp in pair:
            cp.wait_send()
    halves[0][1].wait_recv()
    halves[0][3].wait_recv()
    halves[1][0].wait_recv()
    halves[1][2].wait_recv()
    for cp in fwd + fwd2:
        cp.wait()
    own_sum.wait()
    for cp in sums:
        cp.wait()


def _row_panel(activations, codes, colsum, n_row, n_col):
    tokens = activations.shape[0]
    width = activations.shape[1] // n_row
    n_x = n_col // Z_HI
    assert n_x == 4
    group = Z_HI * n_row
    any_spec = pl.BlockSpec(memory_space=pl.ANY)
    return pl.pallas_call(
        functools.partial(_row_panel_kernel, n_row, n_x),
        out_shape=(
            jax.ShapeDtypeStruct((n_x, Z_HI, n_row, tokens, width), activations.dtype),
            jax.ShapeDtypeStruct((n_x, Z_HI, n_row, 1, tokens), jnp.int32),
            jax.ShapeDtypeStruct((n_row,) + colsum.shape, colsum.dtype),
        ),
        in_specs=[any_spec, any_spec, any_spec],
        out_specs=(any_spec, any_spec, any_spec),
        scratch_shapes=[
            pltpu.SemaphoreType.DMA((group - 1,)),
            pltpu.SemaphoreType.DMA((group - 1,)),
            pltpu.SemaphoreType.DMA((group - 1,)),
            pltpu.SemaphoreType.DMA((group - 1,)),
            pltpu.SemaphoreType.DMA((6,)),
            pltpu.SemaphoreType.DMA((6,)),
            pltpu.SemaphoreType.DMA((6,)),
            pltpu.SemaphoreType.DMA((6,)),
            pltpu.SemaphoreType.DMA((n_row - 1,)),
            pltpu.SemaphoreType.DMA((n_row - 1,)),
            pltpu.SemaphoreType.DMA((3,)),
        ],
        compiler_params=pltpu.CompilerParams(collective_id=0, has_side_effects=True),
    )(activations, codes, colsum)


def _col_piece_kernel(n_col, x_ref, code_ref, o_ref, code_out, send_sem, recv_sem, lsem):
    r = lax.axis_index("row")
    c = lax.axis_index("col")
    width = o_ref.shape[-1]
    barrier = pltpu.get_barrier_semaphore()
    for k in range(1, n_col):
        pl.semaphore_signal(barrier, 1, device_id=(r, lax.rem(c + k, n_col)), device_id_type=MESH)
    pl.semaphore_wait(barrier, n_col - 1)
    own = pltpu.make_async_copy(
        x_ref.at[:, pl.ds(pl.multiple_of(c * width, width), width)], o_ref.at[c], lsem.at[0])
    own.start()
    copies = []
    for k in range(1, n_col):
        dst = lax.rem(c + k, n_col)
        cp = pltpu.make_async_remote_copy(
            src_ref=x_ref.at[:, pl.ds(pl.multiple_of(dst * width, width), width)],
            dst_ref=o_ref.at[c],
            send_sem=send_sem.at[k - 1],
            recv_sem=recv_sem.at[k - 1],
            device_id=(r, dst),
            device_id_type=MESH,
        )
        cp.start()
        copies.append(cp)
    keep = pltpu.make_async_copy(code_ref, code_out, lsem.at[1])
    keep.start()
    own.wait()
    keep.wait()
    for cp in copies:
        cp.wait()


def _col_piece(activations, codes, n_col):
    tokens = activations.shape[0]
    width = activations.shape[1] // n_col
    any_spec = pl.BlockSpec(memory_space=pl.ANY)
    return pl.pallas_call(
        functools.partial(_col_piece_kernel, n_col),
        out_shape=(
            jax.ShapeDtypeStruct((n_col, tokens, width), activations.dtype),
            jax.ShapeDtypeStruct(codes.shape, codes.dtype),
        ),
        in_specs=[any_spec, any_spec],
        out_specs=(any_spec, any_spec),
        scratch_shapes=[
            pltpu.SemaphoreType.DMA((n_col - 1,)),
            pltpu.SemaphoreType.DMA((n_col - 1,)),
            pltpu.SemaphoreType.DMA((2,)),
        ],
        compiler_params=pltpu.CompilerParams(collective_id=1, has_side_effects=True),
    )(activations, codes)


def _column_sum(panel):
    ones = jnp.ones((8, panel.shape[0]), panel.dtype)
    return jnp.dot(ones, panel, preferred_element_type=jnp.float32)[0]


def shards(activations, tenant_ids, concept_labels):
    local_tokens = activations.shape[0]
    width = activations.shape[1]
    row_count = lax.axis_size("row")
    col_count = lax.axis_size("col")
    n_x = col_count // Z_HI
    groups = TENANTS * LABELS
    codes = tenant_ids * LABELS + concept_labels
    col_piece, codes = _col_piece(activations, codes.reshape(1, local_tokens), col_count)
    col_piece = col_piece.reshape(col_count * local_tokens, col_piece.shape[-1])
    col_panel = lax.all_gather(col_piece, "row", axis=0, tiled=True)
    colsum = jnp.dot(jnp.ones((8, col_piece.shape[0]), col_piece.dtype), col_piece,
                     preferred_element_type=jnp.float32)[0:1]
    row_slots, code_slots, col_sums = _row_panel(activations, codes, colsum, row_count, col_count)
    total = col_panel.shape[0]
    row_width = row_slots.shape[-1]
    row_panel = row_slots.reshape(total, row_width)
    col_view = col_panel.reshape(row_count, Z_HI, n_x, local_tokens, col_panel.shape[1])
    gram = jnp.einsum("xhrtf,rhxtg->fg", row_slots, col_view, preferred_element_type=jnp.float32)
    mean_row = _column_sum(row_panel) / total
    mean_col = jnp.sum(col_sums, axis=(0, 1)) / total
    covariance = gram / total - mean_row[:, None] * mean_col[None, :]
    slice_width = width // (row_count * col_count)
    slice_start = lax.axis_index("col") * slice_width
    mean_slice = lax.dynamic_slice_in_dim(mean_row, slice_start, slice_width)
    group_ids = jnp.arange(groups, dtype=jnp.int32)
    onehot_all = code_slots[..., None] == group_ids
    counts = jnp.sum(onehot_all.astype(jnp.float32), axis=(0, 1, 2, 3, 4))
    panel_slice = lax.dynamic_slice_in_dim(row_slots, slice_start, slice_width, 4)
    sums = jnp.einsum(
        "xhrotg,xhrtf->gf",
        onehot_all.astype(jnp.bfloat16),
        panel_slice,
        preferred_element_type=jnp.float32,
    )
    cross = groups / total * (sums - counts[:, None] * mean_slice[None, :])
    return (covariance, cross)


def solution(mesh):
    placed = (P(("row", "col"), None), P(("row", "col")), P(("row", "col")))
    return jax.shard_map(
        shards,
        mesh=mesh,
        in_specs=placed,
        out_specs=(P("row", "col"), P(None, ("row", "col"))),
        check_vma=False,
    )
```

```python
import functools

import jax
import jax.numpy as jnp
from jax import lax
from jax.experimental import pallas as pl
from jax.experimental.pallas import tpu as pltpu
from jax.sharding import PartitionSpec as P

TENANTS = 64
LABELS = 2
MESH = pl.DeviceIdType.MESH
Z_HI = 2


def _row_panel_kernel(n_row, n_x, x_ref, code_ref, p_ref, pc_ref, pair, cpair,
                      s0, r0, s1, r1, s1c, r1c, s2, r2, s2c, r2c, lsem):
    r = lax.axis_index("row")
    c = lax.axis_index("col")
    zh = c // n_x
    x = lax.rem(c, n_x)
    core = lax.rem(r, 2)
    j = r // 2
    n_j = n_row // 2
    partner = r + 1 - 2 * core
    width = p_ref.shape[-1]
    left = zh * n_x + lax.rem(x + n_x - 1, n_x)
    right = zh * n_x + lax.rem(x + 1, n_x)
    sources = [(dz, dj) for dz in range(Z_HI) for dj in range(n_j) if dz or dj]

    def peer(dz, dj):
        return 2 * lax.rem(j + dj, n_j) + core, lax.rem(zh + dz, Z_HI) * n_x + x

    barrier = pltpu.get_barrier_semaphore()
    for dz, dj in sources:
        pl.semaphore_signal(barrier, 1, device_id=peer(dz, dj), device_id_type=MESH)
    pl.semaphore_signal(barrier, 1, device_id=(partner, c), device_id_type=MESH)
    pl.semaphore_signal(barrier, 1, device_id=(r, left), device_id_type=MESH)
    pl.semaphore_signal(barrier, 1, device_id=(r, right), device_id_type=MESH)
    pl.semaphore_wait(barrier, len(sources) + 3)

    mine = pltpu.make_async_copy(x_ref, pair.at[core], lsem.at[0])
    mine_codes = pltpu.make_async_copy(code_ref, cpair.at[core], lsem.at[1])
    swap = pltpu.make_async_remote_copy(
        src_ref=x_ref, dst_ref=pair.at[core], send_sem=s0.at[0], recv_sem=r0.at[0],
        device_id=(partner, c), device_id_type=MESH)
    swap_codes = pltpu.make_async_remote_copy(
        src_ref=code_ref, dst_ref=cpair.at[core], send_sem=s0.at[1], recv_sem=r0.at[1],
        device_id=(partner, c), device_id_type=MESH)
    for cp in (swap, swap_codes, mine, mine_codes):
        cp.start()
    for cp in (swap, swap_codes, mine, mine_codes):
        cp.wait()

    block = pl.ds(pl.multiple_of(2 * j, 2), 2)
    own = pltpu.make_async_copy(
        pair.at[:, :, pl.ds(pl.multiple_of(r * width, width), width)], p_ref.at[x, zh, block], lsem.at[2])
    own_codes = pltpu.make_async_copy(cpair, pc_ref.at[x, zh, block], lsem.at[3])
    own.start()
    own_codes.start()
    stage1 = {0: [], 1: []}
    for i, (dz, dj) in enumerate(sources):
        pr, pc = peer(dz, dj)
        cp = pltpu.make_async_remote_copy(
            src_ref=pair.at[:, :, pl.ds(pl.multiple_of(pr * width, width), width)],
            dst_ref=p_ref.at[x, zh, block],
            send_sem=s1.at[i],
            recv_sem=r1.at[i],
            device_id=(pr, pc),
            device_id_type=MESH,
        )
        cc = pltpu.make_async_remote_copy(
            src_ref=cpair,
            dst_ref=pc_ref.at[x, zh, block],
            send_sem=s1c.at[i],
            recv_sem=r1c.at[i],
            device_id=(pr, pc),
            device_id_type=MESH,
        )
        cp.start()
        cc.start()
        stage1[min(dz, 1)] += [cp, cc]

    def send(src, dst, sems, idx, target):
        return pltpu.make_async_remote_copy(
            src_ref=src, dst_ref=dst, send_sem=sems[0].at[idx], recv_sem=sems[1].at[idx],
            device_id=(r, target), device_id_type=MESH)

    own.wait()
    own_codes.wait()
    halves = []
    for h, plane in enumerate((zh, 1 - zh)):
        for cp in stage1[h]:
            cp.wait_recv()
        pair = [
            send(p_ref.at[x, plane], p_ref.at[x, plane], (s2, r2), 2 * h, right),
            send(p_ref.at[x, plane], p_ref.at[x, plane], (s2, r2), 2 * h + 1, left),
            send(pc_ref.at[x, plane], pc_ref.at[x, plane], (s2c, r2c), 2 * h, right),
            send(pc_ref.at[x, plane], pc_ref.at[x, plane], (s2c, r2c), 2 * h + 1, left),
        ]
        for cp in pair:
            cp.start()
        halves.append(pair)

    from_left = lax.rem(x + n_x - 1, n_x)
    from_right = lax.rem(x + 1, n_x)
    halves[0][0].wait_recv()
    halves[0][2].wait_recv()
    fwd = [
        send(p_ref.at[from_left, zh], p_ref.at[from_left, zh], (s2, r2), 4, right),
        send(pc_ref.at[from_left, zh], pc_ref.at[from_left, zh], (s2c, r2c), 4, right),
    ]
    for cp in fwd:
        cp.start()
    halves[1][1].wait_recv()
    halves[1][3].wait_recv()
    fwd2 = [
        send(p_ref.at[from_right, 1 - zh], p_ref.at[from_right, 1 - zh], (s2, r2), 5, left),
        send(pc_ref.at[from_right, 1 - zh], pc_ref.at[from_right, 1 - zh], (s2c, r2c), 5, left),
    ]
    for cp in fwd2:
        cp.start()

    for cp in stage1[0] + stage1[1]:
        cp.wait_send()
    for pair in halves:
        for cp in pair:
            cp.wait_send()
    halves[0][1].wait_recv()
    halves[0][3].wait_recv()
    halves[1][0].wait_recv()
    halves[1][2].wait_recv()
    for cp in fwd + fwd2:
        cp.wait()


def _row_panel(activations, codes, n_row, n_col):
    tokens = activations.shape[0]
    width = activations.shape[1] // n_row
    n_x = n_col // Z_HI
    assert n_x == 4
    group = Z_HI * n_row
    any_spec = pl.BlockSpec(memory_space=pl.ANY)
    return pl.pallas_call(
        functools.partial(_row_panel_kernel, n_row, n_x),
        out_shape=(
            jax.ShapeDtypeStruct((n_x, Z_HI, n_row, tokens, width), activations.dtype),
            jax.ShapeDtypeStruct((n_x, Z_HI, n_row, 1, tokens), jnp.int32),
            jax.ShapeDtypeStruct((2,) + activations.shape, activations.dtype),
            jax.ShapeDtypeStruct((2,) + codes.shape, codes.dtype),
        ),
        in_specs=[any_spec, any_spec],
        out_specs=(any_spec, any_spec, any_spec, any_spec),
        scratch_shapes=[
            pltpu.SemaphoreType.DMA((2,)),
            pltpu.SemaphoreType.DMA((2,)),
            pltpu.SemaphoreType.DMA((group // 2 - 1,)),
            pltpu.SemaphoreType.DMA((group // 2 - 1,)),
            pltpu.SemaphoreType.DMA((group // 2 - 1,)),
            pltpu.SemaphoreType.DMA((group // 2 - 1,)),
            pltpu.SemaphoreType.DMA((6,)),
            pltpu.SemaphoreType.DMA((6,)),
            pltpu.SemaphoreType.DMA((6,)),
            pltpu.SemaphoreType.DMA((6,)),
            pltpu.SemaphoreType.DMA((4,)),
        ],
        compiler_params=pltpu.CompilerParams(collective_id=0, has_side_effects=True),
    )(activations, codes)


def _col_piece_kernel(n_col, x_ref, code_ref, o_ref, code_out, send_sem, recv_sem, lsem):
    r = lax.axis_index("row")
    c = lax.axis_index("col")
    width = o_ref.shape[-1]
    barrier = pltpu.get_barrier_semaphore()
    for k in range(1, n_col):
        pl.semaphore_signal(barrier, 1, device_id=(r, lax.rem(c + k, n_col)), device_id_type=MESH)
    pl.semaphore_wait(barrier, n_col - 1)
    own = pltpu.make_async_copy(
        x_ref.at[:, pl.ds(pl.multiple_of(c * width, width), width)], o_ref.at[c], lsem.at[0])
    own.start()
    copies = []
    for k in range(1, n_col):
        dst = lax.rem(c + k, n_col)
        cp = pltpu.make_async_remote_copy(
            src_ref=x_ref.at[:, pl.ds(pl.multiple_of(dst * width, width), width)],
            dst_ref=o_ref.at[c],
            send_sem=send_sem.at[k - 1],
            recv_sem=recv_sem.at[k - 1],
            device_id=(r, dst),
            device_id_type=MESH,
        )
        cp.start()
        copies.append(cp)
    keep = pltpu.make_async_copy(code_ref, code_out, lsem.at[1])
    keep.start()
    own.wait()
    keep.wait()
    for cp in copies:
        cp.wait()


def _col_piece(activations, codes, n_col):
    tokens = activations.shape[0]
    width = activations.shape[1] // n_col
    any_spec = pl.BlockSpec(memory_space=pl.ANY)
    return pl.pallas_call(
        functools.partial(_col_piece_kernel, n_col),
        out_shape=(
            jax.ShapeDtypeStruct((n_col, tokens, width), activations.dtype),
            jax.ShapeDtypeStruct(codes.shape, codes.dtype),
        ),
        in_specs=[any_spec, any_spec],
        out_specs=(any_spec, any_spec),
        scratch_shapes=[
            pltpu.SemaphoreType.DMA((n_col - 1,)),
            pltpu.SemaphoreType.DMA((n_col - 1,)),
            pltpu.SemaphoreType.DMA((2,)),
        ],
        compiler_params=pltpu.CompilerParams(collective_id=1, has_side_effects=True),
    )(activations, codes)


def _column_sum(panel):
    ones = jnp.ones((8, panel.shape[0]), panel.dtype)
    return jnp.dot(ones, panel, preferred_element_type=jnp.float32)[0]


def shards(activations, tenant_ids, concept_labels):
    local_tokens = activations.shape[0]
    width = activations.shape[1]
    row_count = lax.axis_size("row")
    col_count = lax.axis_size("col")
    n_x = col_count // Z_HI
    groups = TENANTS * LABELS
    codes = tenant_ids * LABELS + concept_labels
    col_piece, codes = _col_piece(activations, codes.reshape(1, local_tokens), col_count)
    col_piece = col_piece.reshape(col_count * local_tokens, col_piece.shape[-1])
    col_panel = lax.all_gather(col_piece, "row", axis=0, tiled=True)
    row_slots, code_slots, _, _ = _row_panel(activations, codes, row_count, col_count)
    total = col_panel.shape[0]
    row_width = row_slots.shape[-1]
    row_panel = row_slots.reshape(total, row_width)
    col_view = col_panel.reshape(row_count, Z_HI, n_x, local_tokens, col_panel.shape[1])
    gram = jnp.einsum("xhrtf,rhxtg->fg", row_slots, col_view, preferred_element_type=jnp.float32)
    mean_row = _column_sum(row_panel) / total
    mean_col = _column_sum(col_panel) / total
    covariance = gram / total - mean_row[:, None] * mean_col[None, :]
    slice_width = width // (row_count * col_count)
    slice_start = lax.axis_index("col") * slice_width
    mean_slice = lax.dynamic_slice_in_dim(mean_row, slice_start, slice_width)
    group_ids = jnp.arange(groups, dtype=jnp.int32)
    onehot_all = code_slots[..., None] == group_ids
    counts = jnp.sum(onehot_all.astype(jnp.float32), axis=(0, 1, 2, 3, 4))
    panel_slice = lax.dynamic_slice_in_dim(row_slots, slice_start, slice_width, 4)
    sums = jnp.einsum(
        "xhrotg,xhrtf->gf",
        onehot_all.astype(jnp.bfloat16),
        panel_slice,
        preferred_element_type=jnp.float32,
    )
    cross = groups / total * (sums - counts[:, None] * mean_slice[None, :])
    return (covariance, cross)


def solution(mesh):
    placed = (P(("row", "col"), None), P(("row", "col")), P(("row", "col")))
    return jax.shard_map(
        shards,
        mesh=mesh,
        in_specs=placed,
        out_specs=(P("row", "col"), P(None, ("row", "col"))),
        check_vma=False,
    )
```

```python
import functools

import jax
import jax.numpy as jnp
from jax import lax
from jax.experimental import pallas as pl
from jax.experimental.pallas import tpu as pltpu
from jax.sharding import PartitionSpec as P

TENANTS = 64
LABELS = 2
MESH = pl.DeviceIdType.MESH
Z_HI = 2


def _row_panel_kernel(n_row, n_x, x_ref, code_ref, cs_ref, p_ref, pc_ref, cs_out,
                      s1, r1, s1c, r1c, s2, r2, s2c, r2c, s3, r3, lsem):
    r = lax.axis_index("row")
    c = lax.axis_index("col")
    zh = c // n_x
    x = lax.rem(c, n_x)
    width = p_ref.shape[-1]
    left = zh * n_x + lax.rem(x + n_x - 1, n_x)
    right = zh * n_x + lax.rem(x + 1, n_x)
    sources = [(dz, dr) for dz in range(Z_HI) for dr in range(n_row) if dz or dr]

    def peer(dz, dr):
        return lax.rem(r + dr, n_row), lax.rem(zh + dz, Z_HI) * n_x + x

    barrier = pltpu.get_barrier_semaphore()
    for dz, dr in sources:
        pl.semaphore_signal(barrier, 1, device_id=peer(dz, dr), device_id_type=MESH)
    pl.semaphore_signal(barrier, 1, device_id=(r, left), device_id_type=MESH)
    pl.semaphore_signal(barrier, 1, device_id=(r, right), device_id_type=MESH)
    pl.semaphore_wait(barrier, len(sources) + 2)

    own = pltpu.make_async_copy(
        x_ref.at[:, pl.ds(pl.multiple_of(r * width, width), width)], p_ref.at[x, zh, r], lsem.at[0])
    own_codes = pltpu.make_async_copy(code_ref, pc_ref.at[x, zh, r], lsem.at[1])
    own_sum = pltpu.make_async_copy(cs_ref, cs_out.at[r], lsem.at[2])
    own.start()
    own_codes.start()
    own_sum.start()
    stage1 = {0: [], 1: []}
    sums = []
    for i, (dz, dr) in enumerate(sources):
        pr, pc = peer(dz, dr)
        cp = pltpu.make_async_remote_copy(
            src_ref=x_ref.at[:, pl.ds(pl.multiple_of(pr * width, width), width)],
            dst_ref=p_ref.at[x, zh, r],
            send_sem=s1.at[i],
            recv_sem=r1.at[i],
            device_id=(pr, pc),
            device_id_type=MESH,
        )
        cc = pltpu.make_async_remote_copy(
            src_ref=code_ref,
            dst_ref=pc_ref.at[x, zh, r],
            send_sem=s1c.at[i],
            recv_sem=r1c.at[i],
            device_id=(pr, pc),
            device_id_type=MESH,
        )
        cp.start()
        cc.start()
        stage1[min(dz, 1)] += [cp, cc]
        if dz == 0:
            cs = pltpu.make_async_remote_copy(
                src_ref=cs_ref,
                dst_ref=cs_out.at[r],
                send_sem=s3.at[dr - 1],
                recv_sem=r3.at[dr - 1],
                device_id=(pr, pc),
                device_id_type=MESH,
            )
            cs.start()
            sums.append(cs)

    def send(src, dst, sems, idx, target):
        return pltpu.make_async_remote_copy(
            src_ref=src, dst_ref=dst, send_sem=sems[0].at[idx], recv_sem=sems[1].at[idx],
            device_id=(r, target), device_id_type=MESH)

    own.wait()
    own_codes.wait()
    halves = []
    for h, plane in enumerate((zh, 1 - zh)):
        for cp in stage1[h]:
            cp.wait_recv()
        pair = [
            send(p_ref.at[x, plane], p_ref.at[x, plane], (s2, r2), 2 * h, right),
            send(p_ref.at[x, plane], p_ref.at[x, plane], (s2, r2), 2 * h + 1, left),
            send(pc_ref.at[x, plane], pc_ref.at[x, plane], (s2c, r2c), 2 * h, right),
            send(pc_ref.at[x, plane], pc_ref.at[x, plane], (s2c, r2c), 2 * h + 1, left),
        ]
        for cp in pair:
            cp.start()
        halves.append(pair)

    from_left = lax.rem(x + n_x - 1, n_x)
    from_right = lax.rem(x + 1, n_x)
    halves[0][0].wait_recv()
    halves[0][2].wait_recv()
    fwd = [
        send(p_ref.at[from_left, zh], p_ref.at[from_left, zh], (s2, r2), 4, right),
        send(pc_ref.at[from_left, zh], pc_ref.at[from_left, zh], (s2c, r2c), 4, right),
    ]
    for cp in fwd:
        cp.start()
    halves[1][1].wait_recv()
    halves[1][3].wait_recv()
    fwd2 = [
        send(p_ref.at[from_right, 1 - zh], p_ref.at[from_right, 1 - zh], (s2, r2), 5, left),
        send(pc_ref.at[from_right, 1 - zh], pc_ref.at[from_right, 1 - zh], (s2c, r2c), 5, left),
    ]
    for cp in fwd2:
        cp.start()

    for cp in stage1[0] + stage1[1]:
        cp.wait_send()
    for pair in halves:
        for cp in pair:
            cp.wait_send()
    halves[0][1].wait_recv()
    halves[0][3].wait_recv()
    halves[1][0].wait_recv()
    halves[1][2].wait_recv()
    for cp in fwd + fwd2:
        cp.wait()
    own_sum.wait()
    for cp in sums:
        cp.wait()


def _row_panel(activations, codes, colsum, n_row, n_col):
    tokens = activations.shape[0]
    width = activations.shape[1] // n_row
    n_x = n_col // Z_HI
    assert n_x == 4
    group = Z_HI * n_row
    any_spec = pl.BlockSpec(memory_space=pl.ANY)
    return pl.pallas_call(
        functools.partial(_row_panel_kernel, n_row, n_x),
        out_shape=(
            jax.ShapeDtypeStruct((n_x, Z_HI, n_row, tokens, width), activations.dtype),
            jax.ShapeDtypeStruct((n_x, Z_HI, n_row, 1, tokens), jnp.int32),
            jax.ShapeDtypeStruct((n_row,) + colsum.shape, colsum.dtype),
        ),
        in_specs=[any_spec, any_spec, any_spec],
        out_specs=(any_spec, any_spec, any_spec),
        scratch_shapes=[
            pltpu.SemaphoreType.DMA((group - 1,)),
            pltpu.SemaphoreType.DMA((group - 1,)),
            pltpu.SemaphoreType.DMA((group - 1,)),
            pltpu.SemaphoreType.DMA((group - 1,)),
            pltpu.SemaphoreType.DMA((6,)),
            pltpu.SemaphoreType.DMA((6,)),
            pltpu.SemaphoreType.DMA((6,)),
            pltpu.SemaphoreType.DMA((6,)),
            pltpu.SemaphoreType.DMA((n_row - 1,)),
            pltpu.SemaphoreType.DMA((n_row - 1,)),
            pltpu.SemaphoreType.DMA((3,)),
        ],
        compiler_params=pltpu.CompilerParams(collective_id=0, has_side_effects=True),
    )(activations, codes, colsum)


def _col_piece_kernel(n_col, x_ref, code_ref, o_ref, code_out, send_sem, recv_sem, lsem):
    r = lax.axis_index("row")
    c = lax.axis_index("col")
    width = o_ref.shape[-1]
    barrier = pltpu.get_barrier_semaphore()
    for k in range(1, n_col):
        pl.semaphore_signal(barrier, 1, device_id=(r, lax.rem(c + k, n_col)), device_id_type=MESH)
    pl.semaphore_wait(barrier, n_col - 1)
    own = pltpu.make_async_copy(
        x_ref.at[:, pl.ds(pl.multiple_of(c * width, width), width)], o_ref.at[c], lsem.at[0])
    own.start()
    copies = []
    for k in range(1, n_col):
        dst = lax.rem(c + k, n_col)
        cp = pltpu.make_async_remote_copy(
            src_ref=x_ref.at[:, pl.ds(pl.multiple_of(dst * width, width), width)],
            dst_ref=o_ref.at[c],
            send_sem=send_sem.at[k - 1],
            recv_sem=recv_sem.at[k - 1],
            device_id=(r, dst),
            device_id_type=MESH,
        )
        cp.start()
        copies.append(cp)
    keep = pltpu.make_async_copy(code_ref, code_out, lsem.at[1])
    keep.start()
    own.wait()
    keep.wait()
    for cp in copies:
        cp.wait()


def _col_piece(activations, codes, n_col):
    tokens = activations.shape[0]
    width = activations.shape[1] // n_col
    any_spec = pl.BlockSpec(memory_space=pl.ANY)
    return pl.pallas_call(
        functools.partial(_col_piece_kernel, n_col),
        out_shape=(
            jax.ShapeDtypeStruct((n_col, tokens, width), activations.dtype),
            jax.ShapeDtypeStruct(codes.shape, codes.dtype),
        ),
        in_specs=[any_spec, any_spec],
        out_specs=(any_spec, any_spec),
        scratch_shapes=[
            pltpu.SemaphoreType.DMA((n_col - 1,)),
            pltpu.SemaphoreType.DMA((n_col - 1,)),
            pltpu.SemaphoreType.DMA((2,)),
        ],
        compiler_params=pltpu.CompilerParams(collective_id=1, has_side_effects=True),
    )(activations, codes)


def _column_sum(panel):
    ones = jnp.ones((8, panel.shape[0]), panel.dtype)
    return jnp.dot(ones, panel, preferred_element_type=jnp.float32)[0]


def shards(activations, tenant_ids, concept_labels):
    local_tokens = activations.shape[0]
    width = activations.shape[1]
    row_count = lax.axis_size("row")
    col_count = lax.axis_size("col")
    n_x = col_count // Z_HI
    groups = TENANTS * LABELS
    codes = tenant_ids * LABELS + concept_labels
    col_piece, codes = _col_piece(activations, codes.reshape(1, local_tokens), col_count)
    col_piece = col_piece.reshape(col_count * local_tokens, col_piece.shape[-1])
    col_panel = lax.all_gather(col_piece, "row", axis=0, tiled=True)
    colsum = jnp.sum(col_piece, axis=0, dtype=jnp.float32, keepdims=True)
    row_slots, code_slots, col_sums = _row_panel(activations, codes, colsum, row_count, col_count)
    total = col_panel.shape[0]
    row_width = row_slots.shape[-1]
    row_panel = row_slots.reshape(total, row_width)
    col_view = col_panel.reshape(row_count, Z_HI, n_x, local_tokens, col_panel.shape[1])
    gram = jnp.einsum("xhrtf,rhxtg->fg", row_slots, col_view, preferred_element_type=jnp.float32)
    mean_row = _column_sum(row_panel) / total
    mean_col = jnp.sum(col_sums, axis=(0, 1)) / total
    covariance = gram / total - mean_row[:, None] * mean_col[None, :]
    slice_width = width // (row_count * col_count)
    slice_start = lax.axis_index("col") * slice_width
    mean_slice = lax.dynamic_slice_in_dim(mean_row, slice_start, slice_width)
    group_ids = jnp.arange(groups, dtype=jnp.int32)
    onehot_all = code_slots[..., None] == group_ids
    counts = jnp.sum(onehot_all.astype(jnp.float32), axis=(0, 1, 2, 3, 4))
    panel_slice = lax.dynamic_slice_in_dim(row_slots, slice_start, slice_width, 4)
    sums = jnp.einsum(
        "xhrotg,xhrtf->gf",
        onehot_all.astype(jnp.bfloat16),
        panel_slice,
        preferred_element_type=jnp.float32,
    )
    cross = groups / total * (sums - counts[:, None] * mean_slice[None, :])
    return (covariance, cross)


def solution(mesh):
    placed = (P(("row", "col"), None), P(("row", "col")), P(("row", "col")))
    return jax.shard_map(
        shards,
        mesh=mesh,
        in_specs=placed,
        out_specs=(P("row", "col"), P(None, ("row", "col"))),
        check_vma=False,
    )
```

```python
import functools

import jax
import jax.numpy as jnp
from jax import lax
from jax.experimental import pallas as pl
from jax.experimental.pallas import tpu as pltpu
from jax.sharding import PartitionSpec as P

TENANTS = 64
LABELS = 2
MESH = pl.DeviceIdType.MESH
Z_HI = 2


def _row_panel_kernel(n_row, n_x, x_ref, code_ref, cs_ref, p_ref, pc_ref, cs_out, rs_out,
                      s1, r1, s1c, r1c, s2, r2, s2c, r2c, s3, r3, lsem, vbuf, vsem):
    r = lax.axis_index("row")
    c = lax.axis_index("col")
    zh = c // n_x
    x = lax.rem(c, n_x)
    width = p_ref.shape[-1]
    left = zh * n_x + lax.rem(x + n_x - 1, n_x)
    right = zh * n_x + lax.rem(x + 1, n_x)
    sources = [(dz, dr) for dz in range(Z_HI) for dr in range(n_row) if dz or dr]

    def peer(dz, dr):
        return lax.rem(r + dr, n_row), lax.rem(zh + dz, Z_HI) * n_x + x

    barrier = pltpu.get_barrier_semaphore()
    for dz, dr in sources:
        pl.semaphore_signal(barrier, 1, device_id=peer(dz, dr), device_id_type=MESH)
    pl.semaphore_signal(barrier, 1, device_id=(r, left), device_id_type=MESH)
    pl.semaphore_signal(barrier, 1, device_id=(r, right), device_id_type=MESH)
    pl.semaphore_wait(barrier, len(sources) + 2)

    own = pltpu.make_async_copy(
        x_ref.at[:, pl.ds(pl.multiple_of(r * width, width), width)], p_ref.at[x, zh, r], lsem.at[0])
    own_codes = pltpu.make_async_copy(code_ref, pc_ref.at[x, zh, r], lsem.at[1])
    own_sum = pltpu.make_async_copy(cs_ref, cs_out.at[r], lsem.at[2])
    own.start()
    own_codes.start()
    own_sum.start()
    stage1 = {0: [], 1: []}
    sums = []
    for i, (dz, dr) in enumerate(sources):
        pr, pc = peer(dz, dr)
        cp = pltpu.make_async_remote_copy(
            src_ref=x_ref.at[:, pl.ds(pl.multiple_of(pr * width, width), width)],
            dst_ref=p_ref.at[x, zh, r],
            send_sem=s1.at[i],
            recv_sem=r1.at[i],
            device_id=(pr, pc),
            device_id_type=MESH,
        )
        cc = pltpu.make_async_remote_copy(
            src_ref=code_ref,
            dst_ref=pc_ref.at[x, zh, r],
            send_sem=s1c.at[i],
            recv_sem=r1c.at[i],
            device_id=(pr, pc),
            device_id_type=MESH,
        )
        cp.start()
        cc.start()
        stage1[min(dz, 1)] += [cp, cc]
        if dz == 0:
            cs = pltpu.make_async_remote_copy(
                src_ref=cs_ref,
                dst_ref=cs_out.at[r],
                send_sem=s3.at[dr - 1],
                recv_sem=r3.at[dr - 1],
                device_id=(pr, pc),
                device_id_type=MESH,
            )
            cs.start()
            sums.append(cs)

    def send(src, dst, sems, idx, target):
        return pltpu.make_async_remote_copy(
            src_ref=src, dst_ref=dst, send_sem=sems[0].at[idx], recv_sem=sems[1].at[idx],
            device_id=(r, target), device_id_type=MESH)

    own.wait()
    own_codes.wait()
    halves = []
    for h, plane in enumerate((zh, 1 - zh)):
        for cp in stage1[h]:
            cp.wait_recv()
        pair = [
            send(p_ref.at[x, plane], p_ref.at[x, plane], (s2, r2), 2 * h, right),
            send(p_ref.at[x, plane], p_ref.at[x, plane], (s2, r2), 2 * h + 1, left),
            send(pc_ref.at[x, plane], pc_ref.at[x, plane], (s2c, r2c), 2 * h, right),
            send(pc_ref.at[x, plane], pc_ref.at[x, plane], (s2c, r2c), 2 * h + 1, left),
        ]
        for cp in pair:
            cp.start()
        halves.append(pair)

    from_left = lax.rem(x + n_x - 1, n_x)
    from_right = lax.rem(x + 1, n_x)
    halves[0][0].wait_recv()
    halves[0][2].wait_recv()
    fwd = [
        send(p_ref.at[from_left, zh], p_ref.at[from_left, zh], (s2, r2), 4, right),
        send(pc_ref.at[from_left, zh], pc_ref.at[from_left, zh], (s2c, r2c), 4, right),
    ]
    for cp in fwd:
        cp.start()
    halves[1][1].wait_recv()
    halves[1][3].wait_recv()
    fwd2 = [
        send(p_ref.at[from_right, 1 - zh], p_ref.at[from_right, 1 - zh], (s2, r2), 5, left),
        send(pc_ref.at[from_right, 1 - zh], pc_ref.at[from_right, 1 - zh], (s2c, r2c), 5, left),
    ]
    for cp in fwd2:
        cp.start()

    rs_out[...] = jnp.zeros_like(rs_out)

    def add_part(slot, xp):
        load = pltpu.make_async_copy(p_ref.at[xp], vbuf.at[slot], vsem.at[slot])
        load.start()
        load.wait()

        def body(i, carry):
            block = vbuf[slot, i // n_row, lax.rem(i, n_row)].astype(jnp.float32)
            return carry + jnp.sum(block, axis=0, keepdims=True)

        rs_out[...] += lax.fori_loop(0, Z_HI * n_row, body, jnp.zeros(rs_out.shape, jnp.float32))

    add_part(0, x)
    halves[0][1].wait_recv()
    halves[0][3].wait_recv()
    halves[1][0].wait_recv()
    halves[1][2].wait_recv()
    add_part(1, from_left)
    add_part(2, from_right)
    for cp in stage1[0] + stage1[1]:
        cp.wait_send()
    for pair in halves:
        for cp in pair:
            cp.wait_send()
    for cp in fwd + fwd2:
        cp.wait()
    add_part(3, lax.rem(x + 2, n_x))
    own_sum.wait()
    for cp in sums:
        cp.wait()


def _row_panel(activations, codes, colsum, n_row, n_col):
    tokens = activations.shape[0]
    width = activations.shape[1] // n_row
    n_x = n_col // Z_HI
    assert n_x == 4
    group = Z_HI * n_row
    any_spec = pl.BlockSpec(memory_space=pl.ANY)
    return pl.pallas_call(
        functools.partial(_row_panel_kernel, n_row, n_x),
        out_shape=(
            jax.ShapeDtypeStruct((n_x, Z_HI, n_row, tokens, width), activations.dtype),
            jax.ShapeDtypeStruct((n_x, Z_HI, n_row, 1, tokens), jnp.int32),
            jax.ShapeDtypeStruct((n_row,) + colsum.shape, colsum.dtype),
            jax.ShapeDtypeStruct((1, width), jnp.float32),
        ),
        in_specs=[any_spec, any_spec, any_spec],
        out_specs=(any_spec, any_spec, any_spec, pl.BlockSpec(memory_space=pltpu.VMEM)),
        scratch_shapes=[
            pltpu.SemaphoreType.DMA((group - 1,)),
            pltpu.SemaphoreType.DMA((group - 1,)),
            pltpu.SemaphoreType.DMA((group - 1,)),
            pltpu.SemaphoreType.DMA((group - 1,)),
            pltpu.SemaphoreType.DMA((6,)),
            pltpu.SemaphoreType.DMA((6,)),
            pltpu.SemaphoreType.DMA((6,)),
            pltpu.SemaphoreType.DMA((6,)),
            pltpu.SemaphoreType.DMA((n_row - 1,)),
            pltpu.SemaphoreType.DMA((n_row - 1,)),
            pltpu.SemaphoreType.DMA((3,)),
            pltpu.VMEM((4, Z_HI, n_row, tokens, width), activations.dtype),
            pltpu.SemaphoreType.DMA((4,)),
        ],
        compiler_params=pltpu.CompilerParams(collective_id=0, has_side_effects=True),
    )(activations, codes, colsum)


def _col_piece_kernel(n_col, x_ref, code_ref, o_ref, code_out, send_sem, recv_sem, lsem):
    r = lax.axis_index("row")
    c = lax.axis_index("col")
    width = o_ref.shape[-1]
    barrier = pltpu.get_barrier_semaphore()
    for k in range(1, n_col):
        pl.semaphore_signal(barrier, 1, device_id=(r, lax.rem(c + k, n_col)), device_id_type=MESH)
    pl.semaphore_wait(barrier, n_col - 1)
    own = pltpu.make_async_copy(
        x_ref.at[:, pl.ds(pl.multiple_of(c * width, width), width)], o_ref.at[c], lsem.at[0])
    own.start()
    copies = []
    for k in range(1, n_col):
        dst = lax.rem(c + k, n_col)
        cp = pltpu.make_async_remote_copy(
            src_ref=x_ref.at[:, pl.ds(pl.multiple_of(dst * width, width), width)],
            dst_ref=o_ref.at[c],
            send_sem=send_sem.at[k - 1],
            recv_sem=recv_sem.at[k - 1],
            device_id=(r, dst),
            device_id_type=MESH,
        )
        cp.start()
        copies.append(cp)
    keep = pltpu.make_async_copy(code_ref, code_out, lsem.at[1])
    keep.start()
    own.wait()
    keep.wait()
    for cp in copies:
        cp.wait()


def _col_piece(activations, codes, n_col):
    tokens = activations.shape[0]
    width = activations.shape[1] // n_col
    any_spec = pl.BlockSpec(memory_space=pl.ANY)
    return pl.pallas_call(
        functools.partial(_col_piece_kernel, n_col),
        out_shape=(
            jax.ShapeDtypeStruct((n_col, tokens, width), activations.dtype),
            jax.ShapeDtypeStruct(codes.shape, codes.dtype),
        ),
        in_specs=[any_spec, any_spec],
        out_specs=(any_spec, any_spec),
        scratch_shapes=[
            pltpu.SemaphoreType.DMA((n_col - 1,)),
            pltpu.SemaphoreType.DMA((n_col - 1,)),
            pltpu.SemaphoreType.DMA((2,)),
        ],
        compiler_params=pltpu.CompilerParams(collective_id=1, has_side_effects=True),
    )(activations, codes)


def _column_sum(panel):
    ones = jnp.ones((8, panel.shape[0]), panel.dtype)
    return jnp.dot(ones, panel, preferred_element_type=jnp.float32)[0]


def shards(activations, tenant_ids, concept_labels):
    local_tokens = activations.shape[0]
    width = activations.shape[1]
    row_count = lax.axis_size("row")
    col_count = lax.axis_size("col")
    n_x = col_count // Z_HI
    groups = TENANTS * LABELS
    codes = tenant_ids * LABELS + concept_labels
    col_piece, codes = _col_piece(activations, codes.reshape(1, local_tokens), col_count)
    col_piece = col_piece.reshape(col_count * local_tokens, col_piece.shape[-1])
    col_panel = lax.all_gather(col_piece, "row", axis=0, tiled=True)
    colsum = jnp.sum(col_piece, axis=0, dtype=jnp.float32, keepdims=True)
    row_slots, code_slots, col_sums, row_sums = _row_panel(activations, codes, colsum, row_count, col_count)
    total = col_panel.shape[0]
    row_width = row_slots.shape[-1]
    row_panel = row_slots.reshape(total, row_width)
    col_view = col_panel.reshape(row_count, Z_HI, n_x, local_tokens, col_panel.shape[1])
    gram = jnp.einsum("xhrtf,rhxtg->fg", row_slots, col_view, preferred_element_type=jnp.float32)
    mean_row = row_sums[0] / total
    mean_col = jnp.sum(col_sums, axis=(0, 1)) / total
    covariance = gram / total - mean_row[:, None] * mean_col[None, :]
    slice_width = width // (row_count * col_count)
    slice_start = lax.axis_index("col") * slice_width
    mean_slice = lax.dynamic_slice_in_dim(mean_row, slice_start, slice_width)
    group_ids = jnp.arange(groups, dtype=jnp.int32)
    onehot_all = code_slots[..., None] == group_ids
    counts = jnp.sum(onehot_all.astype(jnp.float32), axis=(0, 1, 2, 3, 4))
    panel_slice = lax.dynamic_slice_in_dim(row_slots, slice_start, slice_width, 4)
    sums = jnp.einsum(
        "xhrotg,xhrtf->gf",
        onehot_all.astype(jnp.bfloat16),
        panel_slice,
        preferred_element_type=jnp.float32,
    )
    cross = groups / total * (sums - counts[:, None] * mean_slice[None, :])
    return (covariance, cross)


def solution(mesh):
    placed = (P(("row", "col"), None), P(("row", "col")), P(("row", "col")))
    return jax.shard_map(
        shards,
        mesh=mesh,
        in_specs=placed,
        out_specs=(P("row", "col"), P(None, ("row", "col"))),
        check_vma=False,
    )
```

```python
import functools

import jax
import jax.numpy as jnp
from jax import lax
from jax.experimental import pallas as pl
from jax.experimental.pallas import tpu as pltpu
from jax.sharding import PartitionSpec as P

TENANTS = 64
LABELS = 2
MESH = pl.DeviceIdType.MESH
Z_HI = 2


def _row_panel_kernel(n_row, n_x, x_ref, code_ref, cs_ref, p_ref, pc_ref, cs_out,
                      s1, r1, s1c, r1c, s2, r2, s2c, r2c, s3, r3, lsem):
    r = lax.axis_index("row")
    c = lax.axis_index("col")
    zh = c // n_x
    x = lax.rem(c, n_x)
    width = p_ref.shape[-1]
    left = zh * n_x + lax.rem(x + n_x - 1, n_x)
    right = zh * n_x + lax.rem(x + 1, n_x)
    sources = [(dz, dr) for dz in range(Z_HI) for dr in range(n_row) if dz or dr]

    def peer(dz, dr):
        return lax.rem(r + dr, n_row), lax.rem(zh + dz, Z_HI) * n_x + x

    barrier = pltpu.get_barrier_semaphore()
    for dz, dr in sources:
        pl.semaphore_signal(barrier, 1, device_id=peer(dz, dr), device_id_type=MESH)
    pl.semaphore_signal(barrier, 1, device_id=(r, left), device_id_type=MESH)
    pl.semaphore_signal(barrier, 1, device_id=(r, right), device_id_type=MESH)
    pl.semaphore_wait(barrier, len(sources) + 2)

    own = pltpu.make_async_copy(
        x_ref.at[:, pl.ds(pl.multiple_of(r * width, width), width)], p_ref.at[x, zh, r], lsem.at[0])
    own_codes = pltpu.make_async_copy(code_ref, pc_ref.at[x, zh, r], lsem.at[1])
    own_sum = pltpu.make_async_copy(cs_ref, cs_out.at[r], lsem.at[2])
    own.start()
    own_codes.start()
    own_sum.start()
    stage1 = {0: [], 1: []}
    sums = []
    for i, (dz, dr) in enumerate(sources):
        pr, pc = peer(dz, dr)
        cp = pltpu.make_async_remote_copy(
            src_ref=x_ref.at[:, pl.ds(pl.multiple_of(pr * width, width), width)],
            dst_ref=p_ref.at[x, zh, r],
            send_sem=s1.at[i],
            recv_sem=r1.at[i],
            device_id=(pr, pc),
            device_id_type=MESH,
        )
        cc = pltpu.make_async_remote_copy(
            src_ref=code_ref,
            dst_ref=pc_ref.at[x, zh, r],
            send_sem=s1c.at[i],
            recv_sem=r1c.at[i],
            device_id=(pr, pc),
            device_id_type=MESH,
        )
        cp.start()
        cc.start()
        stage1[min(dz, 1)] += [cp, cc]
        if dz == 0:
            cs = pltpu.make_async_remote_copy(
                src_ref=cs_ref,
                dst_ref=cs_out.at[r],
                send_sem=s3.at[dr - 1],
                recv_sem=r3.at[dr - 1],
                device_id=(pr, pc),
                device_id_type=MESH,
            )
            cs.start()
            sums.append(cs)

    def send(src, dst, sems, idx, target):
        return pltpu.make_async_remote_copy(
            src_ref=src, dst_ref=dst, send_sem=sems[0].at[idx], recv_sem=sems[1].at[idx],
            device_id=(r, target), device_id_type=MESH)

    own.wait()
    own_codes.wait()
    halves = []
    for h, plane in enumerate((zh, 1 - zh)):
        for cp in stage1[h]:
            cp.wait_recv()
        pair = [
            send(p_ref.at[x, plane], p_ref.at[x, plane], (s2, r2), 2 * h, right),
            send(p_ref.at[x, plane], p_ref.at[x, plane], (s2, r2), 2 * h + 1, left),
            send(pc_ref.at[x, plane], pc_ref.at[x, plane], (s2c, r2c), 2 * h, right),
            send(pc_ref.at[x, plane], pc_ref.at[x, plane], (s2c, r2c), 2 * h + 1, left),
        ]
        for cp in pair:
            cp.start()
        halves.append(pair)

    from_left = lax.rem(x + n_x - 1, n_x)
    from_right = lax.rem(x + 1, n_x)
    halves[0][0].wait_recv()
    halves[0][2].wait_recv()
    fwd = [
        send(p_ref.at[from_left, zh], p_ref.at[from_left, zh], (s2, r2), 4, right),
        send(pc_ref.at[from_left, zh], pc_ref.at[from_left, zh], (s2c, r2c), 4, right),
    ]
    for cp in fwd:
        cp.start()
    halves[1][1].wait_recv()
    halves[1][3].wait_recv()
    fwd2 = [
        send(p_ref.at[from_right, 1 - zh], p_ref.at[from_right, 1 - zh], (s2, r2), 5, left),
        send(pc_ref.at[from_right, 1 - zh], pc_ref.at[from_right, 1 - zh], (s2c, r2c), 5, left),
    ]
    for cp in fwd2:
        cp.start()

    for cp in stage1[0] + stage1[1]:
        cp.wait_send()
    for pair in halves:
        for cp in pair:
            cp.wait_send()
    halves[0][1].wait_recv()
    halves[0][3].wait_recv()
    halves[1][0].wait_recv()
    halves[1][2].wait_recv()
    for cp in fwd + fwd2:
        cp.wait()
    own_sum.wait()
    for cp in sums:
        cp.wait()


def _row_panel(activations, codes, colsum, n_row, n_col):
    tokens = activations.shape[0]
    width = activations.shape[1] // n_row
    n_x = n_col // Z_HI
    assert n_x == 4
    group = Z_HI * n_row
    any_spec = pl.BlockSpec(memory_space=pl.ANY)
    return pl.pallas_call(
        functools.partial(_row_panel_kernel, n_row, n_x),
        out_shape=(
            jax.ShapeDtypeStruct((n_x, Z_HI, n_row, tokens, width), activations.dtype),
            jax.ShapeDtypeStruct((n_x, Z_HI, n_row, 1, tokens), jnp.int32),
            jax.ShapeDtypeStruct((n_row,) + colsum.shape, colsum.dtype),
        ),
        in_specs=[any_spec, any_spec, any_spec],
        out_specs=(any_spec, any_spec, any_spec),
        scratch_shapes=[
            pltpu.SemaphoreType.DMA((group - 1,)),
            pltpu.SemaphoreType.DMA((group - 1,)),
            pltpu.SemaphoreType.DMA((group - 1,)),
            pltpu.SemaphoreType.DMA((group - 1,)),
            pltpu.SemaphoreType.DMA((6,)),
            pltpu.SemaphoreType.DMA((6,)),
            pltpu.SemaphoreType.DMA((6,)),
            pltpu.SemaphoreType.DMA((6,)),
            pltpu.SemaphoreType.DMA((n_row - 1,)),
            pltpu.SemaphoreType.DMA((n_row - 1,)),
            pltpu.SemaphoreType.DMA((3,)),
        ],
        compiler_params=pltpu.CompilerParams(collective_id=0, has_side_effects=True),
    )(activations, codes, colsum)


def _col_piece_kernel(n_col, x_ref, code_ref, o_ref, code_out, send_sem, recv_sem, lsem):
    r = lax.axis_index("row")
    c = lax.axis_index("col")
    width = o_ref.shape[-1]
    barrier = pltpu.get_barrier_semaphore()
    for k in range(1, n_col):
        pl.semaphore_signal(barrier, 1, device_id=(r, lax.rem(c + k, n_col)), device_id_type=MESH)
    pl.semaphore_wait(barrier, n_col - 1)
    own = pltpu.make_async_copy(
        x_ref.at[:, pl.ds(pl.multiple_of(c * width, width), width)], o_ref.at[c], lsem.at[0])
    own.start()
    copies = []
    for k in range(1, n_col):
        dst = lax.rem(c + k, n_col)
        cp = pltpu.make_async_remote_copy(
            src_ref=x_ref.at[:, pl.ds(pl.multiple_of(dst * width, width), width)],
            dst_ref=o_ref.at[c],
            send_sem=send_sem.at[k - 1],
            recv_sem=recv_sem.at[k - 1],
            device_id=(r, dst),
            device_id_type=MESH,
        )
        cp.start()
        copies.append(cp)
    keep = pltpu.make_async_copy(code_ref, code_out, lsem.at[1])
    keep.start()
    own.wait()
    keep.wait()
    for cp in copies:
        cp.wait()


def _col_piece(activations, codes, n_col):
    tokens = activations.shape[0]
    width = activations.shape[1] // n_col
    any_spec = pl.BlockSpec(memory_space=pl.ANY)
    return pl.pallas_call(
        functools.partial(_col_piece_kernel, n_col),
        out_shape=(
            jax.ShapeDtypeStruct((n_col, tokens, width), activations.dtype),
            jax.ShapeDtypeStruct(codes.shape, codes.dtype),
        ),
        in_specs=[any_spec, any_spec],
        out_specs=(any_spec, any_spec),
        scratch_shapes=[
            pltpu.SemaphoreType.DMA((n_col - 1,)),
            pltpu.SemaphoreType.DMA((n_col - 1,)),
            pltpu.SemaphoreType.DMA((2,)),
        ],
        compiler_params=pltpu.CompilerParams(collective_id=1, has_side_effects=True),
    )(activations, codes)


def _column_sum(panel):
    ones = jnp.ones((8, panel.shape[0]), panel.dtype)
    return jnp.dot(ones, panel, preferred_element_type=jnp.float32)[0]


def _col_exchange(activations, n_col):
    tokens = activations.shape[0]
    c = lax.axis_index("col")
    blocks = activations.reshape(tokens, n_col, activations.shape[1] // n_col)
    order = lax.rem(c + jnp.arange(n_col, dtype=jnp.int32), n_col)
    outgoing = jnp.take(blocks, order, axis=1)
    pieces = [outgoing[:, 0]]
    for k in range(1, n_col):
        perm = [(i, (i + k) % n_col) for i in range(n_col)]
        pieces.append(lax.ppermute(outgoing[:, k], "col", perm))
    stacked = jnp.stack(pieces, axis=0)
    back = lax.rem(c - jnp.arange(n_col, dtype=jnp.int32) + n_col, n_col)
    piece = jnp.take(stacked, back, axis=0)
    return piece.reshape(n_col * tokens, piece.shape[-1])


def shards(activations, tenant_ids, concept_labels):
    local_tokens = activations.shape[0]
    width = activations.shape[1]
    row_count = lax.axis_size("row")
    col_count = lax.axis_size("col")
    n_x = col_count // Z_HI
    groups = TENANTS * LABELS
    codes = tenant_ids * LABELS + concept_labels
    codes = codes.reshape(1, local_tokens)
    col_piece = _col_exchange(activations, col_count)
    col_panel = lax.all_gather(col_piece, "row", axis=0, tiled=True)
    colsum = jnp.sum(col_piece, axis=0, dtype=jnp.float32, keepdims=True)
    row_slots, code_slots, col_sums = _row_panel(activations, codes, colsum, row_count, col_count)
    total = col_panel.shape[0]
    row_width = row_slots.shape[-1]
    row_panel = row_slots.reshape(total, row_width)
    col_view = col_panel.reshape(row_count, Z_HI, n_x, local_tokens, col_panel.shape[1])
    gram = jnp.einsum("xhrtf,rhxtg->fg", row_slots, col_view, preferred_element_type=jnp.float32)
    mean_row = _column_sum(row_panel) / total
    mean_col = jnp.sum(col_sums, axis=(0, 1)) / total
    covariance = gram / total - mean_row[:, None] * mean_col[None, :]
    slice_width = width // (row_count * col_count)
    slice_start = lax.axis_index("col") * slice_width
    mean_slice = lax.dynamic_slice_in_dim(mean_row, slice_start, slice_width)
    group_ids = jnp.arange(groups, dtype=jnp.int32)
    onehot_all = code_slots[..., None] == group_ids
    counts = jnp.sum(onehot_all.astype(jnp.float32), axis=(0, 1, 2, 3, 4))
    panel_slice = lax.dynamic_slice_in_dim(row_slots, slice_start, slice_width, 4)
    sums = jnp.einsum(
        "xhrotg,xhrtf->gf",
        onehot_all.astype(jnp.bfloat16),
        panel_slice,
        preferred_element_type=jnp.float32,
    )
    cross = groups / total * (sums - counts[:, None] * mean_slice[None, :])
    return (covariance, cross)


def solution(mesh):
    placed = (P(("row", "col"), None), P(("row", "col")), P(("row", "col")))
    return jax.shard_map(
        shards,
        mesh=mesh,
        in_specs=placed,
        out_specs=(P("row", "col"), P(None, ("row", "col"))),
        check_vma=False,
    )
```

```python
import functools

import jax
import jax.numpy as jnp
from jax import lax
from jax.experimental import pallas as pl
from jax.experimental.pallas import tpu as pltpu
from jax.sharding import PartitionSpec as P

TENANTS = 64
LABELS = 2
MESH = pl.DeviceIdType.MESH
Z_HI = 2
SIDE_CODES = 128


def _row_panel_kernel(n_row, n_x, x_ref, code_ref, p_ref, pc_ref,
                      s1, r1, s1c, r1c, s2, r2, s2c, r2c, lsem):
    r = lax.axis_index("row")
    c = lax.axis_index("col")
    zh = c // n_x
    x = lax.rem(c, n_x)
    width = p_ref.shape[-1]
    left = zh * n_x + lax.rem(x + n_x - 1, n_x)
    right = zh * n_x + lax.rem(x + 1, n_x)
    sources = [(dz, dr) for dz in range(Z_HI) for dr in range(n_row) if dz or dr]

    def peer(dz, dr):
        return lax.rem(r + dr, n_row), lax.rem(zh + dz, Z_HI) * n_x + x

    barrier = pltpu.get_barrier_semaphore()
    for dz, dr in sources:
        pl.semaphore_signal(barrier, 1, device_id=peer(dz, dr), device_id_type=MESH)
    pl.semaphore_signal(barrier, 1, device_id=(r, left), device_id_type=MESH)
    pl.semaphore_signal(barrier, 1, device_id=(r, right), device_id_type=MESH)
    pl.semaphore_wait(barrier, len(sources) + 2)

    own = pltpu.make_async_copy(
        x_ref.at[:, pl.ds(pl.multiple_of(r * width, width), width)], p_ref.at[x, zh, r], lsem.at[0])
    own_codes = pltpu.make_async_copy(code_ref, pc_ref.at[x, zh, r], lsem.at[1])
    own.start()
    own_codes.start()
    stage1 = {0: [], 1: []}
    for i, (dz, dr) in enumerate(sources):
        pr, pc = peer(dz, dr)
        cp = pltpu.make_async_remote_copy(
            src_ref=x_ref.at[:, pl.ds(pl.multiple_of(pr * width, width), width)],
            dst_ref=p_ref.at[x, zh, r],
            send_sem=s1.at[i],
            recv_sem=r1.at[i],
            device_id=(pr, pc),
            device_id_type=MESH,
        )
        cc = pltpu.make_async_remote_copy(
            src_ref=code_ref,
            dst_ref=pc_ref.at[x, zh, r],
            send_sem=s1c.at[i],
            recv_sem=r1c.at[i],
            device_id=(pr, pc),
            device_id_type=MESH,
        )
        cp.start()
        cc.start()
        stage1[min(dz, 1)] += [cp, cc]

    def lanes(ref):
        return ref.at[:, :, pl.ds(0, SIDE_CODES)]

    def send(src, dst, sems, idx, target):
        return pltpu.make_async_remote_copy(
            src_ref=src, dst_ref=dst, send_sem=sems[0].at[idx], recv_sem=sems[1].at[idx],
            device_id=(r, target), device_id_type=MESH)

    own.wait()
    own_codes.wait()
    halves = []
    for h, plane in enumerate((zh, 1 - zh)):
        for cp in stage1[h]:
            cp.wait_recv()
        pair = [
            send(p_ref.at[x, plane], p_ref.at[x, plane], (s2, r2), 2 * h, right),
            send(p_ref.at[x, plane], p_ref.at[x, plane], (s2, r2), 2 * h + 1, left),
            send(lanes(pc_ref.at[x, plane]), lanes(pc_ref.at[x, plane]), (s2c, r2c), 2 * h, right),
            send(lanes(pc_ref.at[x, plane]), lanes(pc_ref.at[x, plane]), (s2c, r2c), 2 * h + 1, left),
        ]
        for cp in pair:
            cp.start()
        halves.append(pair)

    from_left = lax.rem(x + n_x - 1, n_x)
    from_right = lax.rem(x + 1, n_x)
    halves[0][0].wait_recv()
    halves[0][2].wait_recv()
    fwd = [
        send(p_ref.at[from_left, zh], p_ref.at[from_left, zh], (s2, r2), 4, right),
        send(lanes(pc_ref.at[from_left, zh]), lanes(pc_ref.at[from_left, zh]), (s2c, r2c), 4, right),
    ]
    for cp in fwd:
        cp.start()
    halves[1][1].wait_recv()
    halves[1][3].wait_recv()
    fwd2 = [
        send(p_ref.at[from_right, 1 - zh], p_ref.at[from_right, 1 - zh], (s2, r2), 5, left),
        send(lanes(pc_ref.at[from_right, 1 - zh]), lanes(pc_ref.at[from_right, 1 - zh]), (s2c, r2c), 5, left),
    ]
    for cp in fwd2:
        cp.start()

    for cp in stage1[0] + stage1[1]:
        cp.wait_send()
    for pair in halves:
        for cp in pair:
            cp.wait_send()
    halves[0][1].wait_recv()
    halves[0][3].wait_recv()
    halves[1][0].wait_recv()
    halves[1][2].wait_recv()
    for cp in fwd + fwd2:
        cp.wait()


def _row_panel(activations, side, n_row, n_col):
    tokens = activations.shape[0]
    width = activations.shape[1] // n_row
    n_x = n_col // Z_HI
    assert n_x == 4
    group = Z_HI * n_row
    any_spec = pl.BlockSpec(memory_space=pl.ANY)
    return pl.pallas_call(
        functools.partial(_row_panel_kernel, n_row, n_x),
        out_shape=(
            jax.ShapeDtypeStruct((n_x, Z_HI, n_row, tokens, width), activations.dtype),
            jax.ShapeDtypeStruct((n_x, Z_HI, n_row) + side.shape, side.dtype),
        ),
        in_specs=[any_spec, any_spec],
        out_specs=(any_spec, any_spec),
        scratch_shapes=[
            pltpu.SemaphoreType.DMA((group - 1,)),
            pltpu.SemaphoreType.DMA((group - 1,)),
            pltpu.SemaphoreType.DMA((group - 1,)),
            pltpu.SemaphoreType.DMA((group - 1,)),
            pltpu.SemaphoreType.DMA((6,)),
            pltpu.SemaphoreType.DMA((6,)),
            pltpu.SemaphoreType.DMA((6,)),
            pltpu.SemaphoreType.DMA((6,)),
            pltpu.SemaphoreType.DMA((2,)),
        ],
        compiler_params=pltpu.CompilerParams(collective_id=0, has_side_effects=True),
    )(activations, side)


def _col_piece_kernel(n_col, x_ref, code_ref, o_ref, code_out, send_sem, recv_sem, lsem):
    r = lax.axis_index("row")
    c = lax.axis_index("col")
    width = o_ref.shape[-1]
    barrier = pltpu.get_barrier_semaphore()
    for k in range(1, n_col):
        pl.semaphore_signal(barrier, 1, device_id=(r, lax.rem(c + k, n_col)), device_id_type=MESH)
    pl.semaphore_wait(barrier, n_col - 1)
    own = pltpu.make_async_copy(
        x_ref.at[:, pl.ds(pl.multiple_of(c * width, width), width)], o_ref.at[c], lsem.at[0])
    own.start()
    copies = []
    for k in range(1, n_col):
        dst = lax.rem(c + k, n_col)
        cp = pltpu.make_async_remote_copy(
            src_ref=x_ref.at[:, pl.ds(pl.multiple_of(dst * width, width), width)],
            dst_ref=o_ref.at[c],
            send_sem=send_sem.at[k - 1],
            recv_sem=recv_sem.at[k - 1],
            device_id=(r, dst),
            device_id_type=MESH,
        )
        cp.start()
        copies.append(cp)
    keep = pltpu.make_async_copy(code_ref, code_out, lsem.at[1])
    keep.start()
    own.wait()
    keep.wait()
    for cp in copies:
        cp.wait()


def _col_piece(activations, codes, n_col):
    tokens = activations.shape[0]
    width = activations.shape[1] // n_col
    any_spec = pl.BlockSpec(memory_space=pl.ANY)
    return pl.pallas_call(
        functools.partial(_col_piece_kernel, n_col),
        out_shape=(
            jax.ShapeDtypeStruct((n_col, tokens, width), activations.dtype),
            jax.ShapeDtypeStruct(codes.shape, codes.dtype),
        ),
        in_specs=[any_spec, any_spec],
        out_specs=(any_spec, any_spec),
        scratch_shapes=[
            pltpu.SemaphoreType.DMA((n_col - 1,)),
            pltpu.SemaphoreType.DMA((n_col - 1,)),
            pltpu.SemaphoreType.DMA((2,)),
        ],
        compiler_params=pltpu.CompilerParams(collective_id=1, has_side_effects=True),
    )(activations, codes)


def _column_sum(panel):
    ones = jnp.ones((8, panel.shape[0]), panel.dtype)
    return jnp.dot(ones, panel, preferred_element_type=jnp.float32)[0]


def shards(activations, tenant_ids, concept_labels):
    local_tokens = activations.shape[0]
    width = activations.shape[1]
    row_count = lax.axis_size("row")
    col_count = lax.axis_size("col")
    n_x = col_count // Z_HI
    groups = TENANTS * LABELS
    codes = tenant_ids * LABELS + concept_labels
    col_piece, codes = _col_piece(activations, codes.reshape(1, local_tokens), col_count)
    col_piece = col_piece.reshape(col_count * local_tokens, col_piece.shape[-1])
    col_panel = lax.all_gather(col_piece, "row", axis=0, tiled=True)
    colsum = jnp.sum(col_piece, axis=0, dtype=jnp.float32, keepdims=True)
    side = jnp.concatenate(
        [jnp.pad(codes.astype(jnp.float32), ((0, 0), (0, SIDE_CODES - local_tokens))), colsum], axis=1)
    row_slots, side_slots = _row_panel(activations, side, row_count, col_count)
    code_slots = side_slots[:, :, :, :, :local_tokens].astype(jnp.int32)
    col_sums = side_slots[lax.rem(lax.axis_index("col"), n_x), lax.axis_index("col") // n_x, :, :, SIDE_CODES:]
    total = col_panel.shape[0]
    row_width = row_slots.shape[-1]
    row_panel = row_slots.reshape(total, row_width)
    col_view = col_panel.reshape(row_count, Z_HI, n_x, local_tokens, col_panel.shape[1])
    gram = jnp.einsum("xhrtf,rhxtg->fg", row_slots, col_view, preferred_element_type=jnp.float32)
    mean_row = _column_sum(row_panel) / total
    mean_col = jnp.sum(col_sums, axis=(0, 1)) / total
    covariance = gram / total - mean_row[:, None] * mean_col[None, :]
    slice_width = width // (row_count * col_count)
    slice_start = lax.axis_index("col") * slice_width
    mean_slice = lax.dynamic_slice_in_dim(mean_row, slice_start, slice_width)
    group_ids = jnp.arange(groups, dtype=jnp.int32)
    onehot_all = code_slots[..., None] == group_ids
    counts = jnp.sum(onehot_all.astype(jnp.float32), axis=(0, 1, 2, 3, 4))
    panel_slice = lax.dynamic_slice_in_dim(row_slots, slice_start, slice_width, 4)
    sums = jnp.einsum(
        "xhrotg,xhrtf->gf",
        onehot_all.astype(jnp.bfloat16),
        panel_slice,
        preferred_element_type=jnp.float32,
    )
    cross = groups / total * (sums - counts[:, None] * mean_slice[None, :])
    return (covariance, cross)


def solution(mesh):
    placed = (P(("row", "col"), None), P(("row", "col")), P(("row", "col")))
    return jax.shard_map(
        shards,
        mesh=mesh,
        in_specs=placed,
        out_specs=(P("row", "col"), P(None, ("row", "col"))),
        check_vma=False,
    )
```

```python
import functools

import jax
import jax.numpy as jnp
from jax import lax
from jax.experimental import pallas as pl
from jax.experimental.pallas import tpu as pltpu
from jax.sharding import PartitionSpec as P

TENANTS = 64
LABELS = 2
MESH = pl.DeviceIdType.MESH
Z_HI = 2


def _row_panel_kernel(n_row, n_x, x_ref, code_ref, cs_ref, p_ref, pc_ref, cs_out,
                      s1, r1, s1c, r1c, s2, r2, s2c, r2c, s3, r3, lsem):
    r = lax.axis_index("row")
    c = lax.axis_index("col")
    zh = c // n_x
    x = lax.rem(c, n_x)
    width = p_ref.shape[-1]
    left = zh * n_x + lax.rem(x + n_x - 1, n_x)
    right = zh * n_x + lax.rem(x + 1, n_x)
    sources = [(dz, dr) for dz in range(Z_HI) for dr in range(n_row) if dz or dr]

    def peer(dz, dr):
        return lax.rem(r + dr, n_row), lax.rem(zh + dz, Z_HI) * n_x + x

    barrier = pltpu.get_barrier_semaphore()
    for dz, dr in sources:
        pl.semaphore_signal(barrier, 1, device_id=peer(dz, dr), device_id_type=MESH)
    pl.semaphore_signal(barrier, 1, device_id=(r, left), device_id_type=MESH)
    pl.semaphore_signal(barrier, 1, device_id=(r, right), device_id_type=MESH)
    pl.semaphore_wait(barrier, len(sources) + 2)

    own = pltpu.make_async_copy(
        x_ref.at[:, pl.ds(pl.multiple_of(r * width, width), width)], p_ref.at[r, zh, x], lsem.at[0])
    own_codes = pltpu.make_async_copy(code_ref, pc_ref.at[r, zh, x], lsem.at[1])
    own_sum = pltpu.make_async_copy(cs_ref, cs_out.at[r], lsem.at[2])
    own.start()
    own_codes.start()
    own_sum.start()
    stage1 = {0: [], 1: []}
    sums = []
    for i, (dz, dr) in enumerate(sources):
        pr, pc = peer(dz, dr)
        cp = pltpu.make_async_remote_copy(
            src_ref=x_ref.at[:, pl.ds(pl.multiple_of(pr * width, width), width)],
            dst_ref=p_ref.at[r, zh, x],
            send_sem=s1.at[i],
            recv_sem=r1.at[i],
            device_id=(pr, pc),
            device_id_type=MESH,
        )
        cc = pltpu.make_async_remote_copy(
            src_ref=code_ref,
            dst_ref=pc_ref.at[r, zh, x],
            send_sem=s1c.at[i],
            recv_sem=r1c.at[i],
            device_id=(pr, pc),
            device_id_type=MESH,
        )
        cp.start()
        cc.start()
        stage1[min(dz, 1)] += [cp, cc]
        if dz == 0:
            cs = pltpu.make_async_remote_copy(
                src_ref=cs_ref,
                dst_ref=cs_out.at[r],
                send_sem=s3.at[dr - 1],
                recv_sem=r3.at[dr - 1],
                device_id=(pr, pc),
                device_id_type=MESH,
            )
            cs.start()
            sums.append(cs)

    def send(src, dst, sems, idx, target):
        return pltpu.make_async_remote_copy(
            src_ref=src, dst_ref=dst, send_sem=sems[0].at[idx], recv_sem=sems[1].at[idx],
            device_id=(r, target), device_id_type=MESH)

    own.wait()
    own_codes.wait()
    halves = []
    for h, plane in enumerate((zh, 1 - zh)):
        for cp in stage1[h]:
            cp.wait_recv()
        pair = [
            send(p_ref.at[:, plane, x], p_ref.at[:, plane, x], (s2, r2), 2 * h, right),
            send(p_ref.at[:, plane, x], p_ref.at[:, plane, x], (s2, r2), 2 * h + 1, left),
            send(pc_ref.at[:, plane, x], pc_ref.at[:, plane, x], (s2c, r2c), 2 * h, right),
            send(pc_ref.at[:, plane, x], pc_ref.at[:, plane, x], (s2c, r2c), 2 * h + 1, left),
        ]
        for cp in pair:
            cp.start()
        halves.append(pair)

    from_left = lax.rem(x + n_x - 1, n_x)
    from_right = lax.rem(x + 1, n_x)
    halves[0][0].wait_recv()
    halves[0][2].wait_recv()
    fwd = [
        send(p_ref.at[:, zh, from_left], p_ref.at[:, zh, from_left], (s2, r2), 4, right),
        send(pc_ref.at[:, zh, from_left], pc_ref.at[:, zh, from_left], (s2c, r2c), 4, right),
    ]
    for cp in fwd:
        cp.start()
    halves[1][1].wait_recv()
    halves[1][3].wait_recv()
    fwd2 = [
        send(p_ref.at[:, 1 - zh, from_right], p_ref.at[:, 1 - zh, from_right], (s2, r2), 5, left),
        send(pc_ref.at[:, 1 - zh, from_right], pc_ref.at[:, 1 - zh, from_right], (s2c, r2c), 5, left),
    ]
    for cp in fwd2:
        cp.start()

    for cp in stage1[0] + stage1[1]:
        cp.wait_send()
    for pair in halves:
        for cp in pair:
            cp.wait_send()
    halves[0][1].wait_recv()
    halves[0][3].wait_recv()
    halves[1][0].wait_recv()
    halves[1][2].wait_recv()
    for cp in fwd + fwd2:
        cp.wait()
    own_sum.wait()
    for cp in sums:
        cp.wait()


def _row_panel(activations, codes, colsum, n_row, n_col):
    tokens = activations.shape[0]
    width = activations.shape[1] // n_row
    n_x = n_col // Z_HI
    assert n_x == 4
    group = Z_HI * n_row
    any_spec = pl.BlockSpec(memory_space=pl.ANY)
    return pl.pallas_call(
        functools.partial(_row_panel_kernel, n_row, n_x),
        out_shape=(
            jax.ShapeDtypeStruct((n_row, Z_HI, n_x, tokens, width), activations.dtype),
            jax.ShapeDtypeStruct((n_row, Z_HI, n_x, 1, tokens), jnp.int32),
            jax.ShapeDtypeStruct((n_row,) + colsum.shape, colsum.dtype),
        ),
        in_specs=[any_spec, any_spec, any_spec],
        out_specs=(any_spec, any_spec, any_spec),
        scratch_shapes=[
            pltpu.SemaphoreType.DMA((group - 1,)),
            pltpu.SemaphoreType.DMA((group - 1,)),
            pltpu.SemaphoreType.DMA((group - 1,)),
            pltpu.SemaphoreType.DMA((group - 1,)),
            pltpu.SemaphoreType.DMA((6,)),
            pltpu.SemaphoreType.DMA((6,)),
            pltpu.SemaphoreType.DMA((6,)),
            pltpu.SemaphoreType.DMA((6,)),
            pltpu.SemaphoreType.DMA((n_row - 1,)),
            pltpu.SemaphoreType.DMA((n_row - 1,)),
            pltpu.SemaphoreType.DMA((3,)),
        ],
        compiler_params=pltpu.CompilerParams(collective_id=0, has_side_effects=True),
    )(activations, codes, colsum)


def _col_piece_kernel(n_col, x_ref, code_ref, o_ref, code_out, send_sem, recv_sem, lsem):
    r = lax.axis_index("row")
    c = lax.axis_index("col")
    width = o_ref.shape[-1]
    barrier = pltpu.get_barrier_semaphore()
    for k in range(1, n_col):
        pl.semaphore_signal(barrier, 1, device_id=(r, lax.rem(c + k, n_col)), device_id_type=MESH)
    pl.semaphore_wait(barrier, n_col - 1)
    own = pltpu.make_async_copy(
        x_ref.at[:, pl.ds(pl.multiple_of(c * width, width), width)], o_ref.at[c], lsem.at[0])
    own.start()
    copies = []
    for k in range(1, n_col):
        dst = lax.rem(c + k, n_col)
        cp = pltpu.make_async_remote_copy(
            src_ref=x_ref.at[:, pl.ds(pl.multiple_of(dst * width, width), width)],
            dst_ref=o_ref.at[c],
            send_sem=send_sem.at[k - 1],
            recv_sem=recv_sem.at[k - 1],
            device_id=(r, dst),
            device_id_type=MESH,
        )
        cp.start()
        copies.append(cp)
    keep = pltpu.make_async_copy(code_ref, code_out, lsem.at[1])
    keep.start()
    own.wait()
    keep.wait()
    for cp in copies:
        cp.wait()


def _col_piece(activations, codes, n_col):
    tokens = activations.shape[0]
    width = activations.shape[1] // n_col
    any_spec = pl.BlockSpec(memory_space=pl.ANY)
    return pl.pallas_call(
        functools.partial(_col_piece_kernel, n_col),
        out_shape=(
            jax.ShapeDtypeStruct((n_col, tokens, width), activations.dtype),
            jax.ShapeDtypeStruct(codes.shape, codes.dtype),
        ),
        in_specs=[any_spec, any_spec],
        out_specs=(any_spec, any_spec),
        scratch_shapes=[
            pltpu.SemaphoreType.DMA((n_col - 1,)),
            pltpu.SemaphoreType.DMA((n_col - 1,)),
            pltpu.SemaphoreType.DMA((2,)),
        ],
        compiler_params=pltpu.CompilerParams(collective_id=1, has_side_effects=True),
    )(activations, codes)


def _column_sum(panel):
    ones = jnp.ones((8, panel.shape[0]), panel.dtype)
    return jnp.dot(ones, panel, preferred_element_type=jnp.float32)[0]


def shards(activations, tenant_ids, concept_labels):
    local_tokens = activations.shape[0]
    width = activations.shape[1]
    row_count = lax.axis_size("row")
    col_count = lax.axis_size("col")
    n_x = col_count // Z_HI
    groups = TENANTS * LABELS
    codes = tenant_ids * LABELS + concept_labels
    col_piece, codes = _col_piece(activations, codes.reshape(1, local_tokens), col_count)
    col_piece = col_piece.reshape(col_count * local_tokens, col_piece.shape[-1])
    col_panel = lax.all_gather(col_piece, "row", axis=0, tiled=True)
    colsum = jnp.sum(col_piece, axis=0, dtype=jnp.float32, keepdims=True)
    row_slots, code_slots, col_sums = _row_panel(activations, codes, colsum, row_count, col_count)
    total = col_panel.shape[0]
    row_width = row_slots.shape[-1]
    row_panel = row_slots.reshape(total, row_width)
    gram = jnp.einsum("tf,tg->fg", row_panel, col_panel, preferred_element_type=jnp.float32)
    mean_row = _column_sum(row_panel) / total
    mean_col = jnp.sum(col_sums, axis=(0, 1)) / total
    covariance = gram / total - mean_row[:, None] * mean_col[None, :]
    slice_width = width // (row_count * col_count)
    slice_start = lax.axis_index("col") * slice_width
    mean_slice = lax.dynamic_slice_in_dim(mean_row, slice_start, slice_width)
    group_ids = jnp.arange(groups, dtype=jnp.int32)
    onehot_all = code_slots[..., None] == group_ids
    counts = jnp.sum(onehot_all.astype(jnp.float32), axis=(0, 1, 2, 3, 4))
    panel_slice = lax.dynamic_slice_in_dim(row_slots, slice_start, slice_width, 4)
    sums = jnp.einsum(
        "rhxotg,rhxtf->gf",
        onehot_all.astype(jnp.bfloat16),
        panel_slice,
        preferred_element_type=jnp.float32,
    )
    cross = groups / total * (sums - counts[:, None] * mean_slice[None, :])
    return (covariance, cross)


def solution(mesh):
    placed = (P(("row", "col"), None), P(("row", "col")), P(("row", "col")))
    return jax.shard_map(
        shards,
        mesh=mesh,
        in_specs=placed,
        out_specs=(P("row", "col"), P(None, ("row", "col"))),
        check_vma=False,
    )
```

```python
import functools

import jax
import jax.numpy as jnp
from jax import lax
from jax.experimental import pallas as pl
from jax.experimental.pallas import tpu as pltpu
from jax.sharding import PartitionSpec as P

TENANTS = 64
LABELS = 2
MESH = pl.DeviceIdType.MESH
Z_HI = 2


def _row_panel_kernel(n_row, n_x, x_ref, code_ref, cs_ref, p_ref, pc_ref, cs_out,
                      s1, r1, s1c, r1c, s2, r2, s2c, r2c, s3, r3, lsem):
    r = lax.axis_index("row")
    c = lax.axis_index("col")
    zh = c // n_x
    x = lax.rem(c, n_x)
    width = p_ref.shape[-1]
    left = zh * n_x + lax.rem(x + n_x - 1, n_x)
    right = zh * n_x + lax.rem(x + 1, n_x)
    sources = [(dz, dr) for dz in range(Z_HI - 1, -1, -1) for dr in range(n_row) if dz or dr]

    def peer(dz, dr):
        return lax.rem(r + dr, n_row), lax.rem(zh + dz, Z_HI) * n_x + x

    barrier = pltpu.get_barrier_semaphore()
    for dz, dr in sources:
        pl.semaphore_signal(barrier, 1, device_id=peer(dz, dr), device_id_type=MESH)
    pl.semaphore_signal(barrier, 1, device_id=(r, left), device_id_type=MESH)
    pl.semaphore_signal(barrier, 1, device_id=(r, right), device_id_type=MESH)
    pl.semaphore_wait(barrier, len(sources) + 2)

    own = pltpu.make_async_copy(
        x_ref.at[:, pl.ds(pl.multiple_of(r * width, width), width)], p_ref.at[r, zh, x], lsem.at[0])
    own_codes = pltpu.make_async_copy(code_ref, pc_ref.at[r, zh, x], lsem.at[1])
    own_sum = pltpu.make_async_copy(cs_ref, cs_out.at[r], lsem.at[2])
    own.start()
    own_codes.start()
    own_sum.start()
    stage1 = {0: [], 1: []}
    sums = []
    for i, (dz, dr) in enumerate(sources):
        pr, pc = peer(dz, dr)
        cp = pltpu.make_async_remote_copy(
            src_ref=x_ref.at[:, pl.ds(pl.multiple_of(pr * width, width), width)],
            dst_ref=p_ref.at[r, zh, x],
            send_sem=s1.at[i],
            recv_sem=r1.at[i],
            device_id=(pr, pc),
            device_id_type=MESH,
        )
        cc = pltpu.make_async_remote_copy(
            src_ref=code_ref,
            dst_ref=pc_ref.at[r, zh, x],
            send_sem=s1c.at[i],
            recv_sem=r1c.at[i],
            device_id=(pr, pc),
            device_id_type=MESH,
        )
        cp.start()
        cc.start()
        stage1[1 - min(dz, 1)] += [cp, cc]
        if dz == 0:
            cs = pltpu.make_async_remote_copy(
                src_ref=cs_ref,
                dst_ref=cs_out.at[r],
                send_sem=s3.at[dr - 1],
                recv_sem=r3.at[dr - 1],
                device_id=(pr, pc),
                device_id_type=MESH,
            )
            cs.start()
            sums.append(cs)

    def send(src, dst, sems, idx, target):
        return pltpu.make_async_remote_copy(
            src_ref=src, dst_ref=dst, send_sem=sems[0].at[idx], recv_sem=sems[1].at[idx],
            device_id=(r, target), device_id_type=MESH)

    own.wait()
    own_codes.wait()
    halves = []
    for h, plane in enumerate((1 - zh, zh)):
        for cp in stage1[h]:
            cp.wait_recv()
        pair = [
            send(p_ref.at[:, plane, x], p_ref.at[:, plane, x], (s2, r2), 2 * h, right),
            send(p_ref.at[:, plane, x], p_ref.at[:, plane, x], (s2, r2), 2 * h + 1, left),
            send(pc_ref.at[:, plane, x], pc_ref.at[:, plane, x], (s2c, r2c), 2 * h, right),
            send(pc_ref.at[:, plane, x], pc_ref.at[:, plane, x], (s2c, r2c), 2 * h + 1, left),
        ]
        for cp in pair:
            cp.start()
        halves.append(pair)

    from_left = lax.rem(x + n_x - 1, n_x)
    from_right = lax.rem(x + 1, n_x)
    halves[0][1].wait_recv()
    halves[0][3].wait_recv()
    fwd2 = [
        send(p_ref.at[:, 1 - zh, from_right], p_ref.at[:, 1 - zh, from_right], (s2, r2), 5, left),
        send(pc_ref.at[:, 1 - zh, from_right], pc_ref.at[:, 1 - zh, from_right], (s2c, r2c), 5, left),
    ]
    for cp in fwd2:
        cp.start()
    halves[1][0].wait_recv()
    halves[1][2].wait_recv()
    fwd = [
        send(p_ref.at[:, zh, from_left], p_ref.at[:, zh, from_left], (s2, r2), 4, right),
        send(pc_ref.at[:, zh, from_left], pc_ref.at[:, zh, from_left], (s2c, r2c), 4, right),
    ]
    for cp in fwd:
        cp.start()

    for cp in stage1[0] + stage1[1]:
        cp.wait_send()
    for pair in halves:
        for cp in pair:
            cp.wait_send()
    halves[0][0].wait_recv()
    halves[0][2].wait_recv()
    halves[1][1].wait_recv()
    halves[1][3].wait_recv()
    for cp in fwd + fwd2:
        cp.wait()
    own_sum.wait()
    for cp in sums:
        cp.wait()


def _row_panel(activations, codes, colsum, n_row, n_col):
    tokens = activations.shape[0]
    width = activations.shape[1] // n_row
    n_x = n_col // Z_HI
    assert n_x == 4
    group = Z_HI * n_row
    any_spec = pl.BlockSpec(memory_space=pl.ANY)
    return pl.pallas_call(
        functools.partial(_row_panel_kernel, n_row, n_x),
        out_shape=(
            jax.ShapeDtypeStruct((n_row, Z_HI, n_x, tokens, width), activations.dtype),
            jax.ShapeDtypeStruct((n_row, Z_HI, n_x, 1, tokens), jnp.int32),
            jax.ShapeDtypeStruct((n_row,) + colsum.shape, colsum.dtype),
        ),
        in_specs=[any_spec, any_spec, any_spec],
        out_specs=(any_spec, any_spec, any_spec),
        scratch_shapes=[
            pltpu.SemaphoreType.DMA((group - 1,)),
            pltpu.SemaphoreType.DMA((group - 1,)),
            pltpu.SemaphoreType.DMA((group - 1,)),
            pltpu.SemaphoreType.DMA((group - 1,)),
            pltpu.SemaphoreType.DMA((6,)),
            pltpu.SemaphoreType.DMA((6,)),
            pltpu.SemaphoreType.DMA((6,)),
            pltpu.SemaphoreType.DMA((6,)),
            pltpu.SemaphoreType.DMA((n_row - 1,)),
            pltpu.SemaphoreType.DMA((n_row - 1,)),
            pltpu.SemaphoreType.DMA((3,)),
        ],
        compiler_params=pltpu.CompilerParams(collective_id=0, has_side_effects=True),
    )(activations, codes, colsum)


def _col_piece_kernel(n_col, x_ref, code_ref, o_ref, code_out, send_sem, recv_sem, lsem):
    r = lax.axis_index("row")
    c = lax.axis_index("col")
    width = o_ref.shape[-1]
    barrier = pltpu.get_barrier_semaphore()
    for k in range(1, n_col):
        pl.semaphore_signal(barrier, 1, device_id=(r, lax.rem(c + k, n_col)), device_id_type=MESH)
    pl.semaphore_wait(barrier, n_col - 1)
    own = pltpu.make_async_copy(
        x_ref.at[:, pl.ds(pl.multiple_of(c * width, width), width)], o_ref.at[c], lsem.at[0])
    own.start()
    copies = []
    for k in range(1, n_col):
        dst = lax.rem(c + k, n_col)
        cp = pltpu.make_async_remote_copy(
            src_ref=x_ref.at[:, pl.ds(pl.multiple_of(dst * width, width), width)],
            dst_ref=o_ref.at[c],
            send_sem=send_sem.at[k - 1],
            recv_sem=recv_sem.at[k - 1],
            device_id=(r, dst),
            device_id_type=MESH,
        )
        cp.start()
        copies.append(cp)
    keep = pltpu.make_async_copy(code_ref, code_out, lsem.at[1])
    keep.start()
    own.wait()
    keep.wait()
    for cp in copies:
        cp.wait()


def _col_piece(activations, codes, n_col):
    tokens = activations.shape[0]
    width = activations.shape[1] // n_col
    any_spec = pl.BlockSpec(memory_space=pl.ANY)
    return pl.pallas_call(
        functools.partial(_col_piece_kernel, n_col),
        out_shape=(
            jax.ShapeDtypeStruct((n_col, tokens, width), activations.dtype),
            jax.ShapeDtypeStruct(codes.shape, codes.dtype),
        ),
        in_specs=[any_spec, any_spec],
        out_specs=(any_spec, any_spec),
        scratch_shapes=[
            pltpu.SemaphoreType.DMA((n_col - 1,)),
            pltpu.SemaphoreType.DMA((n_col - 1,)),
            pltpu.SemaphoreType.DMA((2,)),
        ],
        compiler_params=pltpu.CompilerParams(collective_id=1, has_side_effects=True),
    )(activations, codes)


def _column_sum(panel):
    ones = jnp.ones((8, panel.shape[0]), panel.dtype)
    return jnp.dot(ones, panel, preferred_element_type=jnp.float32)[0]


def shards(activations, tenant_ids, concept_labels):
    local_tokens = activations.shape[0]
    width = activations.shape[1]
    row_count = lax.axis_size("row")
    col_count = lax.axis_size("col")
    n_x = col_count // Z_HI
    groups = TENANTS * LABELS
    codes = tenant_ids * LABELS + concept_labels
    col_piece, codes = _col_piece(activations, codes.reshape(1, local_tokens), col_count)
    col_piece = col_piece.reshape(col_count * local_tokens, col_piece.shape[-1])
    col_panel = lax.all_gather(col_piece, "row", axis=0, tiled=True)
    colsum = jnp.sum(col_piece, axis=0, dtype=jnp.float32, keepdims=True)
    row_slots, code_slots, col_sums = _row_panel(activations, codes, colsum, row_count, col_count)
    total = col_panel.shape[0]
    row_width = row_slots.shape[-1]
    row_panel = row_slots.reshape(total, row_width)
    gram = jnp.einsum("tf,tg->fg", row_panel, col_panel, preferred_element_type=jnp.float32)
    mean_row = _column_sum(row_panel) / total
    mean_col = jnp.sum(col_sums, axis=(0, 1)) / total
    covariance = gram / total - mean_row[:, None] * mean_col[None, :]
    slice_width = width // (row_count * col_count)
    slice_start = lax.axis_index("col") * slice_width
    mean_slice = lax.dynamic_slice_in_dim(mean_row, slice_start, slice_width)
    group_ids = jnp.arange(groups, dtype=jnp.int32)
    onehot_all = code_slots[..., None] == group_ids
    counts = jnp.sum(onehot_all.astype(jnp.float32), axis=(0, 1, 2, 3, 4))
    panel_slice = lax.dynamic_slice_in_dim(row_slots, slice_start, slice_width, 4)
    sums = jnp.einsum(
        "rhxotg,rhxtf->gf",
        onehot_all.astype(jnp.bfloat16),
        panel_slice,
        preferred_element_type=jnp.float32,
    )
    cross = groups / total * (sums - counts[:, None] * mean_slice[None, :])
    return (covariance, cross)


def solution(mesh):
    placed = (P(("row", "col"), None), P(("row", "col")), P(("row", "col")))
    return jax.shard_map(
        shards,
        mesh=mesh,
        in_specs=placed,
        out_specs=(P("row", "col"), P(None, ("row", "col"))),
        check_vma=False,
    )
```

```python
import functools

import jax
import jax.numpy as jnp
from jax import lax
from jax.experimental import pallas as pl
from jax.experimental.pallas import tpu as pltpu
from jax.sharding import PartitionSpec as P

TENANTS = 64
LABELS = 2
MESH = pl.DeviceIdType.MESH
Z_HI = 2


def _row_panel_kernel(n_row, n_x, x_ref, code_ref, cs_ref, p_ref, pc_ref, cs_out,
                      s1, r1, s1c, r1c, s2, r2, s2c, r2c, s3, r3, lsem):
    r = lax.axis_index("row")
    c = lax.axis_index("col")
    zh = c // n_x
    x = lax.rem(c, n_x)
    width = p_ref.shape[-1]
    left = zh * n_x + lax.rem(x + n_x - 1, n_x)
    right = zh * n_x + lax.rem(x + 1, n_x)
    sources = [(dz, dr) for dz in range(Z_HI - 1, -1, -1) for dr in range(n_row) if dz or dr]

    def peer(dz, dr):
        return lax.rem(r + dr, n_row), lax.rem(zh + dz, Z_HI) * n_x + x

    barrier = pltpu.get_barrier_semaphore()
    for dz, dr in sources:
        pl.semaphore_signal(barrier, 1, device_id=peer(dz, dr), device_id_type=MESH)
    pl.semaphore_signal(barrier, 1, device_id=(r, left), device_id_type=MESH)
    pl.semaphore_signal(barrier, 1, device_id=(r, right), device_id_type=MESH)
    pl.semaphore_wait(barrier, len(sources) + 2)

    own = pltpu.make_async_copy(
        x_ref.at[:, pl.ds(pl.multiple_of(r * width, width), width)], p_ref.at[r, zh, x], lsem.at[0])
    own_codes = pltpu.make_async_copy(code_ref, pc_ref.at[r, zh, x], lsem.at[1])
    own_sum = pltpu.make_async_copy(cs_ref, cs_out.at[r], lsem.at[2])
    own.start()
    own_codes.start()
    own_sum.start()
    stage1 = {0: [], 1: []}
    sums = []
    for i, (dz, dr) in enumerate(sources):
        pr, pc = peer(dz, dr)
        cp = pltpu.make_async_remote_copy(
            src_ref=x_ref.at[:, pl.ds(pl.multiple_of(pr * width, width), width)],
            dst_ref=p_ref.at[r, zh, x],
            send_sem=s1.at[i],
            recv_sem=r1.at[i],
            device_id=(pr, pc),
            device_id_type=MESH,
        )
        cc = pltpu.make_async_remote_copy(
            src_ref=code_ref,
            dst_ref=pc_ref.at[r, zh, x],
            send_sem=s1c.at[i],
            recv_sem=r1c.at[i],
            device_id=(pr, pc),
            device_id_type=MESH,
        )
        cp.start()
        cc.start()
        stage1[1 - min(dz, 1)] += [cp, cc]
        if dz == 0:
            cs = pltpu.make_async_remote_copy(
                src_ref=cs_ref,
                dst_ref=cs_out.at[r],
                send_sem=s3.at[dr - 1],
                recv_sem=r3.at[dr - 1],
                device_id=(pr, pc),
                device_id_type=MESH,
            )
            cs.start()
            sums.append(cs)

    def send(src, dst, sems, idx, target):
        return pltpu.make_async_remote_copy(
            src_ref=src, dst_ref=dst, send_sem=sems[0].at[idx], recv_sem=sems[1].at[idx],
            device_id=(r, target), device_id_type=MESH)

    own.wait()
    own_codes.wait()
    halves = []
    for h, plane in enumerate((1 - zh, zh)):
        for cp in stage1[h]:
            cp.wait_recv()
        pair = [
            send(p_ref.at[:, plane, x], p_ref.at[:, plane, x], (s2, r2), 2 * h, right),
            send(p_ref.at[:, plane, x], p_ref.at[:, plane, x], (s2, r2), 2 * h + 1, left),
            send(pc_ref.at[:, plane, x], pc_ref.at[:, plane, x], (s2c, r2c), 2 * h, right),
            send(pc_ref.at[:, plane, x], pc_ref.at[:, plane, x], (s2c, r2c), 2 * h + 1, left),
        ]
        for cp in pair:
            cp.start()
        halves.append(pair)

    from_left = lax.rem(x + n_x - 1, n_x)
    from_right = lax.rem(x + 1, n_x)
    halves[0][1].wait_recv()
    halves[0][3].wait_recv()
    fwd2 = [
        send(p_ref.at[:, 1 - zh, from_right], p_ref.at[:, 1 - zh, from_right], (s2, r2), 5, left),
        send(pc_ref.at[:, 1 - zh, from_right], pc_ref.at[:, 1 - zh, from_right], (s2c, r2c), 5, left),
    ]
    for cp in fwd2:
        cp.start()
    halves[1][0].wait_recv()
    halves[1][2].wait_recv()
    fwd = [
        send(p_ref.at[:, zh, from_left], p_ref.at[:, zh, from_left], (s2, r2), 4, right),
        send(pc_ref.at[:, zh, from_left], pc_ref.at[:, zh, from_left], (s2c, r2c), 4, right),
    ]
    for cp in fwd:
        cp.start()

    for cp in stage1[0] + stage1[1]:
        cp.wait_send()
    for pair in halves:
        for cp in pair:
            cp.wait_send()
    halves[0][0].wait_recv()
    halves[0][2].wait_recv()
    halves[1][1].wait_recv()
    halves[1][3].wait_recv()
    for cp in fwd + fwd2:
        cp.wait()
    own_sum.wait()
    for cp in sums:
        cp.wait()


def _row_panel(activations, codes, colsum, n_row, n_col):
    tokens = activations.shape[0]
    width = activations.shape[1] // n_row
    n_x = n_col // Z_HI
    assert n_x == 4
    group = Z_HI * n_row
    any_spec = pl.BlockSpec(memory_space=pl.ANY)
    return pl.pallas_call(
        functools.partial(_row_panel_kernel, n_row, n_x),
        out_shape=(
            jax.ShapeDtypeStruct((n_row, Z_HI, n_x, tokens, width), activations.dtype),
            jax.ShapeDtypeStruct((n_row, Z_HI, n_x, 1, tokens), jnp.int32),
            jax.ShapeDtypeStruct((n_row,) + colsum.shape, colsum.dtype),
        ),
        in_specs=[any_spec, any_spec, any_spec],
        out_specs=(any_spec, any_spec, any_spec),
        scratch_shapes=[
            pltpu.SemaphoreType.DMA((group - 1,)),
            pltpu.SemaphoreType.DMA((group - 1,)),
            pltpu.SemaphoreType.DMA((group - 1,)),
            pltpu.SemaphoreType.DMA((group - 1,)),
            pltpu.SemaphoreType.DMA((6,)),
            pltpu.SemaphoreType.DMA((6,)),
            pltpu.SemaphoreType.DMA((6,)),
            pltpu.SemaphoreType.DMA((6,)),
            pltpu.SemaphoreType.DMA((n_row - 1,)),
            pltpu.SemaphoreType.DMA((n_row - 1,)),
            pltpu.SemaphoreType.DMA((3,)),
        ],
        compiler_params=pltpu.CompilerParams(collective_id=0, has_side_effects=True),
    )(activations, codes, colsum)


def _col_piece_kernel(n_col, x_ref, tenant_ref, label_ref, o_ref, code_out, send_sem, recv_sem, lsem):
    r = lax.axis_index("row")
    c = lax.axis_index("col")
    width = o_ref.shape[-1]
    barrier = pltpu.get_barrier_semaphore()
    for k in range(1, n_col):
        pl.semaphore_signal(barrier, 1, device_id=(r, lax.rem(c + k, n_col)), device_id_type=MESH)
    code_out[...] = tenant_ref[...] * LABELS + label_ref[...]
    pl.semaphore_wait(barrier, n_col - 1)
    own = pltpu.make_async_copy(
        x_ref.at[:, pl.ds(pl.multiple_of(c * width, width), width)], o_ref.at[c], lsem.at[0])
    own.start()
    copies = []
    for k in range(1, n_col):
        dst = lax.rem(c + k, n_col)
        cp = pltpu.make_async_remote_copy(
            src_ref=x_ref.at[:, pl.ds(pl.multiple_of(dst * width, width), width)],
            dst_ref=o_ref.at[c],
            send_sem=send_sem.at[k - 1],
            recv_sem=recv_sem.at[k - 1],
            device_id=(r, dst),
            device_id_type=MESH,
        )
        cp.start()
        copies.append(cp)
    own.wait()
    for cp in copies:
        cp.wait()


def _col_piece(activations, tenant_ids, concept_labels, n_col):
    tokens = activations.shape[0]
    width = activations.shape[1] // n_col
    any_spec = pl.BlockSpec(memory_space=pl.ANY)
    vmem_spec = pl.BlockSpec(memory_space=pltpu.VMEM)
    return pl.pallas_call(
        functools.partial(_col_piece_kernel, n_col),
        out_shape=(
            jax.ShapeDtypeStruct((n_col, tokens, width), activations.dtype),
            jax.ShapeDtypeStruct((1, tokens), jnp.int32),
        ),
        in_specs=[any_spec, vmem_spec, vmem_spec],
        out_specs=(any_spec, vmem_spec),
        scratch_shapes=[
            pltpu.SemaphoreType.DMA((n_col - 1,)),
            pltpu.SemaphoreType.DMA((n_col - 1,)),
            pltpu.SemaphoreType.DMA((1,)),
        ],
        compiler_params=pltpu.CompilerParams(collective_id=1, has_side_effects=True),
    )(activations, tenant_ids.reshape(1, tokens), concept_labels.reshape(1, tokens))


def _column_sum(panel):
    ones = jnp.ones((8, panel.shape[0]), panel.dtype)
    return jnp.dot(ones, panel, preferred_element_type=jnp.float32)[0]


def shards(activations, tenant_ids, concept_labels):
    local_tokens = activations.shape[0]
    width = activations.shape[1]
    row_count = lax.axis_size("row")
    col_count = lax.axis_size("col")
    n_x = col_count // Z_HI
    groups = TENANTS * LABELS
    col_piece, codes = _col_piece(activations, tenant_ids, concept_labels, col_count)
    col_piece = col_piece.reshape(col_count * local_tokens, col_piece.shape[-1])
    col_panel = lax.all_gather(col_piece, "row", axis=0, tiled=True)
    colsum = jnp.sum(col_piece, axis=0, dtype=jnp.float32, keepdims=True)
    row_slots, code_slots, col_sums = _row_panel(activations, codes, colsum, row_count, col_count)
    total = col_panel.shape[0]
    row_width = row_slots.shape[-1]
    row_panel = row_slots.reshape(total, row_width)
    gram = jnp.einsum("tf,tg->fg", row_panel, col_panel, preferred_element_type=jnp.float32)
    mean_row = _column_sum(row_panel) / total
    mean_col = jnp.sum(col_sums, axis=(0, 1)) / total
    covariance = gram / total - mean_row[:, None] * mean_col[None, :]
    slice_width = width // (row_count * col_count)
    slice_start = lax.axis_index("col") * slice_width
    mean_slice = lax.dynamic_slice_in_dim(mean_row, slice_start, slice_width)
    group_ids = jnp.arange(groups, dtype=jnp.int32)
    onehot_all = code_slots[..., None] == group_ids
    counts = jnp.sum(onehot_all.astype(jnp.float32), axis=(0, 1, 2, 3, 4))
    panel_slice = lax.dynamic_slice_in_dim(row_slots, slice_start, slice_width, 4)
    sums = jnp.einsum(
        "rhxotg,rhxtf->gf",
        onehot_all.astype(jnp.bfloat16),
        panel_slice,
        preferred_element_type=jnp.float32,
    )
    cross = groups / total * (sums - counts[:, None] * mean_slice[None, :])
    return (covariance, cross)


def solution(mesh):
    placed = (P(("row", "col"), None), P(("row", "col")), P(("row", "col")))
    return jax.shard_map(
        shards,
        mesh=mesh,
        in_specs=placed,
        out_specs=(P("row", "col"), P(None, ("row", "col"))),
        check_vma=False,
    )
```

```python
import functools

import jax
import jax.numpy as jnp
from jax import lax
from jax.experimental import pallas as pl
from jax.experimental.pallas import tpu as pltpu
from jax.sharding import PartitionSpec as P

TENANTS = 64
LABELS = 2
MESH = pl.DeviceIdType.MESH
Z_HI = 2


def _row_panel_kernel(n_row, n_x, x_ref, code_ref, cs_ref, p_ref, pc_ref, cs_out,
                      s1, r1, s1c, r1c, s2, r2, s2c, r2c, s3, r3, lsem):
    r = lax.axis_index("row")
    c = lax.axis_index("col")
    zh = c // n_x
    x = lax.rem(c, n_x)
    width = p_ref.shape[-1]
    left = zh * n_x + lax.rem(x + n_x - 1, n_x)
    right = zh * n_x + lax.rem(x + 1, n_x)
    sources = [(dz, dr) for dz in range(Z_HI - 1, -1, -1) for dr in range(n_row) if dz or dr]

    def peer(dz, dr):
        return lax.rem(r + dr, n_row), lax.rem(zh + dz, Z_HI) * n_x + x

    barrier = pltpu.get_barrier_semaphore()
    for dz, dr in sources:
        pl.semaphore_signal(barrier, 1, device_id=peer(dz, dr), device_id_type=MESH)
    pl.semaphore_signal(barrier, 1, device_id=(r, left), device_id_type=MESH)
    pl.semaphore_signal(barrier, 1, device_id=(r, right), device_id_type=MESH)
    pl.semaphore_wait(barrier, len(sources) + 2)

    own = pltpu.make_async_copy(
        x_ref.at[:, pl.ds(pl.multiple_of(r * width, width), width)], p_ref.at[r, zh, x], lsem.at[0])
    own_codes = pltpu.make_async_copy(code_ref, pc_ref.at[r, zh, x], lsem.at[1])
    own_sum = pltpu.make_async_copy(cs_ref, cs_out.at[r], lsem.at[2])
    own.start()
    own_codes.start()
    own_sum.start()
    group = Z_HI * n_row
    half_rows = n_row // 2
    stage1 = []
    sums = []
    for i, (dz, dr) in enumerate(sources):
        pr, pc = peer(dz, dr)
        cp = pltpu.make_async_remote_copy(
            src_ref=x_ref.at[:, pl.ds(pl.multiple_of(pr * width, width), width)],
            dst_ref=p_ref.at[r, zh, x],
            send_sem=s1.at[i],
            recv_sem=r1.at[zh * n_row + r],
            device_id=(pr, pc),
            device_id_type=MESH,
        )
        cc = pltpu.make_async_remote_copy(
            src_ref=code_ref,
            dst_ref=pc_ref.at[r, zh, x],
            send_sem=s1c.at[i],
            recv_sem=r1c.at[zh * n_row + r],
            device_id=(pr, pc),
            device_id_type=MESH,
        )
        cp.start()
        cc.start()
        stage1 += [cp, cc]
        if dz == 0:
            cs = pltpu.make_async_remote_copy(
                src_ref=cs_ref,
                dst_ref=cs_out.at[r],
                send_sem=s3.at[dr - 1],
                recv_sem=r3.at[dr - 1],
                device_id=(pr, pc),
                device_id_type=MESH,
            )
            cs.start()
            sums.append(cs)

    def send(src, dst, sems, idx, target):
        return pltpu.make_async_remote_copy(
            src_ref=src, dst_ref=dst, send_sem=sems[0].at[idx], recv_sem=sems[1].at[idx],
            device_id=(r, target), device_id_type=MESH)

    def arrived(plane, row):
        for ref, sems in ((p_ref, (s1, r1)), (pc_ref, (s1c, r1c))):
            pltpu.make_async_remote_copy(
                src_ref=ref.at[row, plane, x], dst_ref=ref.at[row, plane, x],
                send_sem=sems[0].at[0], recv_sem=sems[1].at[plane * n_row + row],
                device_id=(r, right), device_id_type=MESH).wait_recv()

    own.wait()
    own_codes.wait()
    parts = [(1 - zh, 0), (1 - zh, half_rows), (zh, 0), (zh, half_rows)]
    ring = []
    for k, (plane, row0) in enumerate(parts):
        for row in range(row0, row0 + half_rows):
            if k < 2:
                arrived(plane, row)
            else:
                @pl.when(r != row)
                def _(row=row, plane=plane):
                    arrived(plane, row)
        rows = pl.ds(row0, half_rows)
        pair = [
            send(p_ref.at[rows, plane, x], p_ref.at[rows, plane, x], (s2, r2), 2 * k, right),
            send(p_ref.at[rows, plane, x], p_ref.at[rows, plane, x], (s2, r2), 2 * k + 1, left),
            send(pc_ref.at[rows, plane, x], pc_ref.at[rows, plane, x], (s2c, r2c), 2 * k, right),
            send(pc_ref.at[rows, plane, x], pc_ref.at[rows, plane, x], (s2c, r2c), 2 * k + 1, left),
        ]
        for cp in pair:
            cp.start()
        ring.append(pair)

    from_left = lax.rem(x + n_x - 1, n_x)
    from_right = lax.rem(x + 1, n_x)
    fwd = []
    for k, (plane, row0) in enumerate(parts):
        rows = pl.ds(row0, half_rows)
        if k < 2:
            ring[k][1].wait_recv()
            ring[k][3].wait_recv()
            src, target, idx = from_right, left, 8 + k
        else:
            ring[k][0].wait_recv()
            ring[k][2].wait_recv()
            src, target, idx = from_left, right, 8 + k
        pair = [
            send(p_ref.at[rows, plane, src], p_ref.at[rows, plane, src], (s2, r2), idx, target),
            send(pc_ref.at[rows, plane, src], pc_ref.at[rows, plane, src], (s2c, r2c), idx, target),
        ]
        for cp in pair:
            cp.start()
        fwd += pair

    for cp in stage1:
        cp.wait_send()
    for k, pair in enumerate(ring):
        for cp in pair:
            cp.wait_send()
        if k < 2:
            pair[0].wait_recv()
            pair[2].wait_recv()
        else:
            pair[1].wait_recv()
            pair[3].wait_recv()
    for cp in fwd:
        cp.wait()
    own_sum.wait()
    for cp in sums:
        cp.wait()


def _row_panel(activations, codes, colsum, n_row, n_col):
    tokens = activations.shape[0]
    width = activations.shape[1] // n_row
    n_x = n_col // Z_HI
    assert n_x == 4
    group = Z_HI * n_row
    any_spec = pl.BlockSpec(memory_space=pl.ANY)
    return pl.pallas_call(
        functools.partial(_row_panel_kernel, n_row, n_x),
        out_shape=(
            jax.ShapeDtypeStruct((n_row, Z_HI, n_x, tokens, width), activations.dtype),
            jax.ShapeDtypeStruct((n_row, Z_HI, n_x, 1, tokens), jnp.int32),
            jax.ShapeDtypeStruct((n_row,) + colsum.shape, colsum.dtype),
        ),
        in_specs=[any_spec, any_spec, any_spec],
        out_specs=(any_spec, any_spec, any_spec),
        scratch_shapes=[
            pltpu.SemaphoreType.DMA((group - 1,)),
            pltpu.SemaphoreType.DMA((group,)),
            pltpu.SemaphoreType.DMA((group - 1,)),
            pltpu.SemaphoreType.DMA((group,)),
            pltpu.SemaphoreType.DMA((12,)),
            pltpu.SemaphoreType.DMA((12,)),
            pltpu.SemaphoreType.DMA((12,)),
            pltpu.SemaphoreType.DMA((12,)),
            pltpu.SemaphoreType.DMA((n_row - 1,)),
            pltpu.SemaphoreType.DMA((n_row - 1,)),
            pltpu.SemaphoreType.DMA((3,)),
        ],
        compiler_params=pltpu.CompilerParams(collective_id=0, has_side_effects=True),
    )(activations, codes, colsum)


def _col_piece_kernel(n_col, x_ref, code_ref, o_ref, code_out, send_sem, recv_sem, lsem):
    r = lax.axis_index("row")
    c = lax.axis_index("col")
    width = o_ref.shape[-1]
    barrier = pltpu.get_barrier_semaphore()
    for k in range(1, n_col):
        pl.semaphore_signal(barrier, 1, device_id=(r, lax.rem(c + k, n_col)), device_id_type=MESH)
    pl.semaphore_wait(barrier, n_col - 1)
    own = pltpu.make_async_copy(
        x_ref.at[:, pl.ds(pl.multiple_of(c * width, width), width)], o_ref.at[c], lsem.at[0])
    own.start()
    copies = []
    for k in range(1, n_col):
        dst = lax.rem(c + k, n_col)
        cp = pltpu.make_async_remote_copy(
            src_ref=x_ref.at[:, pl.ds(pl.multiple_of(dst * width, width), width)],
            dst_ref=o_ref.at[c],
            send_sem=send_sem.at[k - 1],
            recv_sem=recv_sem.at[k - 1],
            device_id=(r, dst),
            device_id_type=MESH,
        )
        cp.start()
        copies.append(cp)
    keep = pltpu.make_async_copy(code_ref, code_out, lsem.at[1])
    keep.start()
    own.wait()
    keep.wait()
    for cp in copies:
        cp.wait()


def _col_piece(activations, codes, n_col):
    tokens = activations.shape[0]
    width = activations.shape[1] // n_col
    any_spec = pl.BlockSpec(memory_space=pl.ANY)
    return pl.pallas_call(
        functools.partial(_col_piece_kernel, n_col),
        out_shape=(
            jax.ShapeDtypeStruct((n_col, tokens, width), activations.dtype),
            jax.ShapeDtypeStruct(codes.shape, codes.dtype),
        ),
        in_specs=[any_spec, any_spec],
        out_specs=(any_spec, any_spec),
        scratch_shapes=[
            pltpu.SemaphoreType.DMA((n_col - 1,)),
            pltpu.SemaphoreType.DMA((n_col - 1,)),
            pltpu.SemaphoreType.DMA((2,)),
        ],
        compiler_params=pltpu.CompilerParams(collective_id=1, has_side_effects=True),
    )(activations, codes)


def _column_sum(panel):
    ones = jnp.ones((8, panel.shape[0]), panel.dtype)
    return jnp.dot(ones, panel, preferred_element_type=jnp.float32)[0]


def shards(activations, tenant_ids, concept_labels):
    local_tokens = activations.shape[0]
    width = activations.shape[1]
    row_count = lax.axis_size("row")
    col_count = lax.axis_size("col")
    n_x = col_count // Z_HI
    groups = TENANTS * LABELS
    codes = tenant_ids * LABELS + concept_labels
    col_piece, codes = _col_piece(activations, codes.reshape(1, local_tokens), col_count)
    col_piece = col_piece.reshape(col_count * local_tokens, col_piece.shape[-1])
    col_panel = lax.all_gather(col_piece, "row", axis=0, tiled=True)
    colsum = jnp.sum(col_piece, axis=0, dtype=jnp.float32, keepdims=True)
    row_slots, code_slots, col_sums = _row_panel(activations, codes, colsum, row_count, col_count)
    total = col_panel.shape[0]
    row_width = row_slots.shape[-1]
    row_panel = row_slots.reshape(total, row_width)
    gram = jnp.einsum("tf,tg->fg", row_panel, col_panel, preferred_element_type=jnp.float32)
    mean_row = _column_sum(row_panel) / total
    mean_col = jnp.sum(col_sums, axis=(0, 1)) / total
    covariance = gram / total - mean_row[:, None] * mean_col[None, :]
    slice_width = width // (row_count * col_count)
    slice_start = lax.axis_index("col") * slice_width
    mean_slice = lax.dynamic_slice_in_dim(mean_row, slice_start, slice_width)
    group_ids = jnp.arange(groups, dtype=jnp.int32)
    onehot_all = code_slots[..., None] == group_ids
    counts = jnp.sum(onehot_all.astype(jnp.float32), axis=(0, 1, 2, 3, 4))
    panel_slice = lax.dynamic_slice_in_dim(row_slots, slice_start, slice_width, 4)
    sums = jnp.einsum(
        "rhxotg,rhxtf->gf",
        onehot_all.astype(jnp.bfloat16),
        panel_slice,
        preferred_element_type=jnp.float32,
    )
    cross = groups / total * (sums - counts[:, None] * mean_slice[None, :])
    return (covariance, cross)


def solution(mesh):
    placed = (P(("row", "col"), None), P(("row", "col")), P(("row", "col")))
    return jax.shard_map(
        shards,
        mesh=mesh,
        in_specs=placed,
        out_specs=(P("row", "col"), P(None, ("row", "col"))),
        check_vma=False,
    )
```

```python
import functools

import jax
import jax.numpy as jnp
from jax import lax
from jax.experimental import pallas as pl
from jax.experimental.pallas import tpu as pltpu
from jax.sharding import PartitionSpec as P

TENANTS = 64
LABELS = 2
MESH = pl.DeviceIdType.MESH
Z_HI = 2


def _row_panel_kernel(n_row, n_x, x_ref, code_ref, cs_ref, p_ref, pc_ref, cs_out, cs_total,
                      s1, r1, s1c, r1c, s2, r2, s2c, r2c, s3, r3, lsem, cs_buf):
    r = lax.axis_index("row")
    c = lax.axis_index("col")
    zh = c // n_x
    x = lax.rem(c, n_x)
    width = p_ref.shape[-1]
    left = zh * n_x + lax.rem(x + n_x - 1, n_x)
    right = zh * n_x + lax.rem(x + 1, n_x)
    sources = [(dz, dr) for dz in range(Z_HI - 1, -1, -1) for dr in range(n_row) if dz or dr]

    def peer(dz, dr):
        return lax.rem(r + dr, n_row), lax.rem(zh + dz, Z_HI) * n_x + x

    barrier = pltpu.get_barrier_semaphore()
    for dz, dr in sources:
        pl.semaphore_signal(barrier, 1, device_id=peer(dz, dr), device_id_type=MESH)
    pl.semaphore_signal(barrier, 1, device_id=(r, left), device_id_type=MESH)
    pl.semaphore_signal(barrier, 1, device_id=(r, right), device_id_type=MESH)
    pl.semaphore_wait(barrier, len(sources) + 2)

    own = pltpu.make_async_copy(
        x_ref.at[:, pl.ds(pl.multiple_of(r * width, width), width)], p_ref.at[r, zh, x], lsem.at[0])
    own_codes = pltpu.make_async_copy(code_ref, pc_ref.at[r, zh, x], lsem.at[1])
    own_sum = pltpu.make_async_copy(cs_ref, cs_out.at[r], lsem.at[2])
    own.start()
    own_codes.start()
    own_sum.start()
    group = Z_HI * n_row
    half_rows = n_row // 2
    stage1 = []
    sums = []
    for i, (dz, dr) in enumerate(sources):
        pr, pc = peer(dz, dr)
        cp = pltpu.make_async_remote_copy(
            src_ref=x_ref.at[:, pl.ds(pl.multiple_of(pr * width, width), width)],
            dst_ref=p_ref.at[r, zh, x],
            send_sem=s1.at[i],
            recv_sem=r1.at[zh * n_row + r],
            device_id=(pr, pc),
            device_id_type=MESH,
        )
        cc = pltpu.make_async_remote_copy(
            src_ref=code_ref,
            dst_ref=pc_ref.at[r, zh, x],
            send_sem=s1c.at[i],
            recv_sem=r1c.at[zh * n_row + r],
            device_id=(pr, pc),
            device_id_type=MESH,
        )
        cp.start()
        cc.start()
        stage1 += [cp, cc]
        if dz == 0:
            cs = pltpu.make_async_remote_copy(
                src_ref=cs_ref,
                dst_ref=cs_out.at[r],
                send_sem=s3.at[dr - 1],
                recv_sem=r3.at[dr - 1],
                device_id=(pr, pc),
                device_id_type=MESH,
            )
            cs.start()
            sums.append(cs)

    def send(src, dst, sems, idx, target):
        return pltpu.make_async_remote_copy(
            src_ref=src, dst_ref=dst, send_sem=sems[0].at[idx], recv_sem=sems[1].at[idx],
            device_id=(r, target), device_id_type=MESH)

    def arrived(plane, row):
        for ref, sems in ((p_ref, (s1, r1)), (pc_ref, (s1c, r1c))):
            pltpu.make_async_remote_copy(
                src_ref=ref.at[row, plane, x], dst_ref=ref.at[row, plane, x],
                send_sem=sems[0].at[0], recv_sem=sems[1].at[plane * n_row + row],
                device_id=(r, right), device_id_type=MESH).wait_recv()

    own.wait()
    own_codes.wait()
    parts = [(1 - zh, 0), (1 - zh, half_rows), (zh, 0), (zh, half_rows)]
    ring = []
    for k, (plane, row0) in enumerate(parts):
        for row in range(row0, row0 + half_rows):
            if k < 2:
                arrived(plane, row)
            else:
                @pl.when(r != row)
                def _(row=row, plane=plane):
                    arrived(plane, row)
        rows = pl.ds(row0, half_rows)
        pair = [
            send(p_ref.at[rows, plane, x], p_ref.at[rows, plane, x], (s2, r2), 2 * k, right),
            send(p_ref.at[rows, plane, x], p_ref.at[rows, plane, x], (s2, r2), 2 * k + 1, left),
            send(pc_ref.at[rows, plane, x], pc_ref.at[rows, plane, x], (s2c, r2c), 2 * k, right),
            send(pc_ref.at[rows, plane, x], pc_ref.at[rows, plane, x], (s2c, r2c), 2 * k + 1, left),
        ]
        for cp in pair:
            cp.start()
        ring.append(pair)

    own_sum.wait()
    for cp in sums:
        cp.wait_recv()
    load = pltpu.make_async_copy(cs_out, cs_buf, lsem.at[3])
    load.start()
    load.wait()
    cs_total[...] = jnp.sum(cs_buf[...], axis=0)

    from_left = lax.rem(x + n_x - 1, n_x)
    from_right = lax.rem(x + 1, n_x)
    fwd = []
    for k, (plane, row0) in enumerate(parts):
        rows = pl.ds(row0, half_rows)
        if k < 2:
            ring[k][1].wait_recv()
            ring[k][3].wait_recv()
            src, target, idx = from_right, left, 8 + k
        else:
            ring[k][0].wait_recv()
            ring[k][2].wait_recv()
            src, target, idx = from_left, right, 8 + k
        pair = [
            send(p_ref.at[rows, plane, src], p_ref.at[rows, plane, src], (s2, r2), idx, target),
            send(pc_ref.at[rows, plane, src], pc_ref.at[rows, plane, src], (s2c, r2c), idx, target),
        ]
        for cp in pair:
            cp.start()
        fwd += pair

    for cp in stage1:
        cp.wait_send()
    for k, pair in enumerate(ring):
        for cp in pair:
            cp.wait_send()
        if k < 2:
            pair[0].wait_recv()
            pair[2].wait_recv()
        else:
            pair[1].wait_recv()
            pair[3].wait_recv()
    for cp in fwd:
        cp.wait()
    for cp in sums:
        cp.wait_send()


def _row_panel(activations, codes, colsum, n_row, n_col):
    tokens = activations.shape[0]
    width = activations.shape[1] // n_row
    n_x = n_col // Z_HI
    assert n_x == 4
    group = Z_HI * n_row
    any_spec = pl.BlockSpec(memory_space=pl.ANY)
    return pl.pallas_call(
        functools.partial(_row_panel_kernel, n_row, n_x),
        out_shape=(
            jax.ShapeDtypeStruct((n_row, Z_HI, n_x, tokens, width), activations.dtype),
            jax.ShapeDtypeStruct((n_row, Z_HI, n_x, 1, tokens), jnp.int32),
            jax.ShapeDtypeStruct((n_row,) + colsum.shape, colsum.dtype),
            jax.ShapeDtypeStruct(colsum.shape, colsum.dtype),
        ),
        in_specs=[any_spec, any_spec, any_spec],
        out_specs=(any_spec, any_spec, any_spec, pl.BlockSpec(memory_space=pltpu.VMEM)),
        scratch_shapes=[
            pltpu.SemaphoreType.DMA((group - 1,)),
            pltpu.SemaphoreType.DMA((group,)),
            pltpu.SemaphoreType.DMA((group - 1,)),
            pltpu.SemaphoreType.DMA((group,)),
            pltpu.SemaphoreType.DMA((12,)),
            pltpu.SemaphoreType.DMA((12,)),
            pltpu.SemaphoreType.DMA((12,)),
            pltpu.SemaphoreType.DMA((12,)),
            pltpu.SemaphoreType.DMA((n_row - 1,)),
            pltpu.SemaphoreType.DMA((n_row - 1,)),
            pltpu.SemaphoreType.DMA((4,)),
            pltpu.VMEM((n_row,) + colsum.shape, colsum.dtype),
        ],
        compiler_params=pltpu.CompilerParams(collective_id=0, has_side_effects=True),
    )(activations, codes, colsum)


def _col_piece_kernel(n_col, x_ref, code_ref, o_ref, code_out, send_sem, recv_sem, lsem):
    r = lax.axis_index("row")
    c = lax.axis_index("col")
    width = o_ref.shape[-1]
    barrier = pltpu.get_barrier_semaphore()
    for k in range(1, n_col):
        pl.semaphore_signal(barrier, 1, device_id=(r, lax.rem(c + k, n_col)), device_id_type=MESH)
    pl.semaphore_wait(barrier, n_col - 1)
    own = pltpu.make_async_copy(
        x_ref.at[:, pl.ds(pl.multiple_of(c * width, width), width)], o_ref.at[c], lsem.at[0])
    own.start()
    copies = []
    for k in range(1, n_col):
        dst = lax.rem(c + k, n_col)
        cp = pltpu.make_async_remote_copy(
            src_ref=x_ref.at[:, pl.ds(pl.multiple_of(dst * width, width), width)],
            dst_ref=o_ref.at[c],
            send_sem=send_sem.at[k - 1],
            recv_sem=recv_sem.at[k - 1],
            device_id=(r, dst),
            device_id_type=MESH,
        )
        cp.start()
        copies.append(cp)
    keep = pltpu.make_async_copy(code_ref, code_out, lsem.at[1])
    keep.start()
    own.wait()
    keep.wait()
    for cp in copies:
        cp.wait()


def _col_piece(activations, codes, n_col):
    tokens = activations.shape[0]
    width = activations.shape[1] // n_col
    any_spec = pl.BlockSpec(memory_space=pl.ANY)
    return pl.pallas_call(
        functools.partial(_col_piece_kernel, n_col),
        out_shape=(
            jax.ShapeDtypeStruct((n_col, tokens, width), activations.dtype),
            jax.ShapeDtypeStruct(codes.shape, codes.dtype),
        ),
        in_specs=[any_spec, any_spec],
        out_specs=(any_spec, any_spec),
        scratch_shapes=[
            pltpu.SemaphoreType.DMA((n_col - 1,)),
            pltpu.SemaphoreType.DMA((n_col - 1,)),
            pltpu.SemaphoreType.DMA((2,)),
        ],
        compiler_params=pltpu.CompilerParams(collective_id=1, has_side_effects=True),
    )(activations, codes)


def _column_sum(panel):
    ones = jnp.ones((8, panel.shape[0]), panel.dtype)
    return jnp.dot(ones, panel, preferred_element_type=jnp.float32)[0]


def shards(activations, tenant_ids, concept_labels):
    local_tokens = activations.shape[0]
    width = activations.shape[1]
    row_count = lax.axis_size("row")
    col_count = lax.axis_size("col")
    n_x = col_count // Z_HI
    groups = TENANTS * LABELS
    codes = tenant_ids * LABELS + concept_labels
    col_piece, codes = _col_piece(activations, codes.reshape(1, local_tokens), col_count)
    col_piece = col_piece.reshape(col_count * local_tokens, col_piece.shape[-1])
    col_panel = lax.all_gather(col_piece, "row", axis=0, tiled=True)
    colsum = jnp.sum(col_piece, axis=0, dtype=jnp.float32, keepdims=True)
    row_slots, code_slots, _, col_total = _row_panel(activations, codes, colsum, row_count, col_count)
    total = col_panel.shape[0]
    row_width = row_slots.shape[-1]
    row_panel = row_slots.reshape(total, row_width)
    gram = jnp.einsum("tf,tg->fg", row_panel, col_panel, preferred_element_type=jnp.float32)
    mean_row = _column_sum(row_panel) / total
    mean_col = col_total[0] / total
    covariance = gram / total - mean_row[:, None] * mean_col[None, :]
    slice_width = width // (row_count * col_count)
    slice_start = lax.axis_index("col") * slice_width
    mean_slice = lax.dynamic_slice_in_dim(mean_row, slice_start, slice_width)
    group_ids = jnp.arange(groups, dtype=jnp.int32)
    onehot_all = code_slots[..., None] == group_ids
    counts = jnp.sum(onehot_all.astype(jnp.float32), axis=(0, 1, 2, 3, 4))
    panel_slice = lax.dynamic_slice_in_dim(row_slots, slice_start, slice_width, 4)
    sums = jnp.einsum(
        "rhxotg,rhxtf->gf",
        onehot_all.astype(jnp.bfloat16),
        panel_slice,
        preferred_element_type=jnp.float32,
    )
    cross = groups / total * (sums - counts[:, None] * mean_slice[None, :])
    return (covariance, cross)


def solution(mesh):
    placed = (P(("row", "col"), None), P(("row", "col")), P(("row", "col")))
    return jax.shard_map(
        shards,
        mesh=mesh,
        in_specs=placed,
        out_specs=(P("row", "col"), P(None, ("row", "col"))),
        check_vma=False,
    )
```

```python
import functools

import jax
import jax.numpy as jnp
from jax import lax
from jax.experimental import pallas as pl
from jax.experimental.pallas import tpu as pltpu
from jax.sharding import PartitionSpec as P

TENANTS = 64
LABELS = 2
MESH = pl.DeviceIdType.MESH
Z_HI = 2


def _row_panel_kernel(n_row, n_x, x_ref, code_ref, cs_ref, p_ref, pc_ref, cs_out, cs_total,
                      s1, r1, s1c, r1c, s2, r2, s2c, r2c, s3, r3, lsem, cs_buf):
    r = lax.axis_index("row")
    c = lax.axis_index("col")
    zh = c // n_x
    x = lax.rem(c, n_x)
    width = p_ref.shape[-1]
    left = zh * n_x + lax.rem(x + n_x - 1, n_x)
    right = zh * n_x + lax.rem(x + 1, n_x)
    sources = [(dz, dr) for dz in range(Z_HI - 1, -1, -1) for dr in range(n_row) if dz or dr]

    def peer(dz, dr):
        return lax.rem(r + dr, n_row), lax.rem(zh + dz, Z_HI) * n_x + x

    barrier = pltpu.get_barrier_semaphore()
    for dz, dr in sources:
        pl.semaphore_signal(barrier, 1, device_id=peer(dz, dr), device_id_type=MESH)
    pl.semaphore_signal(barrier, 1, device_id=(r, left), device_id_type=MESH)
    pl.semaphore_signal(barrier, 1, device_id=(r, right), device_id_type=MESH)
    pl.semaphore_wait(barrier, len(sources) + 2)

    own = pltpu.make_async_copy(
        x_ref.at[:, pl.ds(pl.multiple_of(r * width, width), width)], p_ref.at[r, zh, x], lsem.at[0])
    own_codes = pltpu.make_async_copy(code_ref, pc_ref.at[r, zh, x], lsem.at[1])
    own_sum = pltpu.make_async_copy(cs_ref, cs_out.at[r], lsem.at[2])
    own.start()
    own_codes.start()
    own_sum.start()
    group = Z_HI * n_row
    half_rows = n_row // 2
    stage1 = []
    sums = []
    for i, (dz, dr) in enumerate(sources):
        pr, pc = peer(dz, dr)
        cp = pltpu.make_async_remote_copy(
            src_ref=x_ref.at[:, pl.ds(pl.multiple_of(pr * width, width), width)],
            dst_ref=p_ref.at[r, zh, x],
            send_sem=s1.at[i],
            recv_sem=r1.at[zh * n_row + r],
            device_id=(pr, pc),
            device_id_type=MESH,
        )
        cc = pltpu.make_async_remote_copy(
            src_ref=code_ref,
            dst_ref=pc_ref.at[r, zh, x],
            send_sem=s1c.at[i],
            recv_sem=r1c.at[zh * n_row + r],
            device_id=(pr, pc),
            device_id_type=MESH,
        )
        cp.start()
        cc.start()
        stage1 += [cp, cc]
        if dz == 0:
            cs = pltpu.make_async_remote_copy(
                src_ref=cs_ref,
                dst_ref=cs_out.at[r],
                send_sem=s3.at[dr - 1],
                recv_sem=r3.at[dr - 1],
                device_id=(pr, pc),
                device_id_type=MESH,
            )
            cs.start()
            sums.append(cs)

    def send(src, dst, sems, idx, target):
        return pltpu.make_async_remote_copy(
            src_ref=src, dst_ref=dst, send_sem=sems[0].at[idx], recv_sem=sems[1].at[idx],
            device_id=(r, target), device_id_type=MESH)

    def arrived(plane, row):
        for ref, sems in ((p_ref, (s1, r1)), (pc_ref, (s1c, r1c))):
            pltpu.make_async_remote_copy(
                src_ref=ref.at[row, plane, x], dst_ref=ref.at[row, plane, x],
                send_sem=sems[0].at[0], recv_sem=sems[1].at[plane * n_row + row],
                device_id=(r, right), device_id_type=MESH).wait_recv()

    own.wait()
    own_codes.wait()
    parts = [(1 - zh, 0), (1 - zh, half_rows), (zh, 0), (zh, half_rows)]
    ring = []
    for k, (plane, row0) in enumerate(parts):
        for row in range(row0, row0 + half_rows):
            if k < 2:
                arrived(plane, row)
            else:
                @pl.when(r != row)
                def _(row=row, plane=plane):
                    arrived(plane, row)
        rows = pl.ds(row0, half_rows)
        pair = [
            send(p_ref.at[rows, plane, x], p_ref.at[rows, plane, x], (s2, r2), 2 * k, right),
            send(p_ref.at[rows, plane, x], p_ref.at[rows, plane, x], (s2, r2), 2 * k + 1, left),
            send(pc_ref.at[rows, plane, x], pc_ref.at[rows, plane, x], (s2c, r2c), 2 * k, right),
            send(pc_ref.at[rows, plane, x], pc_ref.at[rows, plane, x], (s2c, r2c), 2 * k + 1, left),
        ]
        for cp in pair:
            cp.start()
        ring.append(pair)

    own_sum.wait()
    for cp in sums:
        cp.wait_recv()
    load = pltpu.make_async_copy(cs_out, cs_buf, lsem.at[3])
    load.start()
    load.wait()
    cs_total[...] = jnp.sum(cs_buf[...], axis=0)

    from_left = lax.rem(x + n_x - 1, n_x)
    from_right = lax.rem(x + 1, n_x)
    fwd = []
    for k, (plane, row0) in enumerate(parts):
        rows = pl.ds(row0, half_rows)
        if k < 2:
            ring[k][1].wait_recv()
            ring[k][3].wait_recv()
            src, target, idx = from_right, left, 8 + k
        else:
            ring[k][0].wait_recv()
            ring[k][2].wait_recv()
            src, target, idx = from_left, right, 8 + k
        pair = [
            send(p_ref.at[rows, plane, src], p_ref.at[rows, plane, src], (s2, r2), idx, target),
            send(pc_ref.at[rows, plane, src], pc_ref.at[rows, plane, src], (s2c, r2c), idx, target),
        ]
        for cp in pair:
            cp.start()
        fwd += pair

    for cp in stage1:
        cp.wait_send()
    for k, pair in enumerate(ring):
        for cp in pair:
            cp.wait_send()
        if k < 2:
            pair[0].wait_recv()
            pair[2].wait_recv()
        else:
            pair[1].wait_recv()
            pair[3].wait_recv()
    for cp in fwd:
        cp.wait()
    for cp in sums:
        cp.wait_send()


def _row_panel(activations, codes, colsum, n_row, n_col):
    tokens = activations.shape[0]
    width = activations.shape[1] // n_row
    n_x = n_col // Z_HI
    assert n_x == 4
    group = Z_HI * n_row
    any_spec = pl.BlockSpec(memory_space=pl.ANY)
    return pl.pallas_call(
        functools.partial(_row_panel_kernel, n_row, n_x),
        out_shape=(
            jax.ShapeDtypeStruct((n_row, Z_HI, n_x, tokens, width), activations.dtype),
            jax.ShapeDtypeStruct((n_row, Z_HI, n_x, 1, tokens), jnp.int32),
            jax.ShapeDtypeStruct((n_row,) + colsum.shape, colsum.dtype),
            jax.ShapeDtypeStruct(colsum.shape, colsum.dtype),
        ),
        in_specs=[any_spec, any_spec, any_spec],
        out_specs=(any_spec, any_spec, any_spec, pl.BlockSpec(memory_space=pltpu.VMEM)),
        scratch_shapes=[
            pltpu.SemaphoreType.DMA((group - 1,)),
            pltpu.SemaphoreType.DMA((group,)),
            pltpu.SemaphoreType.DMA((group - 1,)),
            pltpu.SemaphoreType.DMA((group,)),
            pltpu.SemaphoreType.DMA((12,)),
            pltpu.SemaphoreType.DMA((12,)),
            pltpu.SemaphoreType.DMA((12,)),
            pltpu.SemaphoreType.DMA((12,)),
            pltpu.SemaphoreType.DMA((n_row - 1,)),
            pltpu.SemaphoreType.DMA((n_row - 1,)),
            pltpu.SemaphoreType.DMA((4,)),
            pltpu.VMEM((n_row,) + colsum.shape, colsum.dtype),
        ],
        compiler_params=pltpu.CompilerParams(collective_id=0, has_side_effects=True),
    )(activations, codes, colsum)


def _col_piece_kernel(n_col, x_ref, o_ref, send_sem, recv_sem, lsem):
    r = lax.axis_index("row")
    c = lax.axis_index("col")
    width = o_ref.shape[-1]
    barrier = pltpu.get_barrier_semaphore()
    for k in range(1, n_col):
        pl.semaphore_signal(barrier, 1, device_id=(r, lax.rem(c + k, n_col)), device_id_type=MESH)
    pl.semaphore_wait(barrier, n_col - 1)
    own = pltpu.make_async_copy(
        x_ref.at[:, pl.ds(pl.multiple_of(c * width, width), width)], o_ref.at[c], lsem.at[0])
    own.start()
    copies = []
    for k in range(1, n_col):
        dst = lax.rem(c + k, n_col)
        cp = pltpu.make_async_remote_copy(
            src_ref=x_ref.at[:, pl.ds(pl.multiple_of(dst * width, width), width)],
            dst_ref=o_ref.at[c],
            send_sem=send_sem.at[k - 1],
            recv_sem=recv_sem.at[k - 1],
            device_id=(r, dst),
            device_id_type=MESH,
        )
        cp.start()
        copies.append(cp)
    own.wait()
    for cp in copies:
        cp.wait()


def _col_piece(activations, n_col):
    tokens = activations.shape[0]
    width = activations.shape[1] // n_col
    any_spec = pl.BlockSpec(memory_space=pl.ANY)
    return pl.pallas_call(
        functools.partial(_col_piece_kernel, n_col),
        out_shape=jax.ShapeDtypeStruct((n_col, tokens, width), activations.dtype),
        in_specs=[any_spec],
        out_specs=any_spec,
        scratch_shapes=[
            pltpu.SemaphoreType.DMA((n_col - 1,)),
            pltpu.SemaphoreType.DMA((n_col - 1,)),
            pltpu.SemaphoreType.DMA((2,)),
        ],
        compiler_params=pltpu.CompilerParams(collective_id=1, has_side_effects=True),
    )(activations)


def _column_sum(panel):
    ones = jnp.ones((8, panel.shape[0]), panel.dtype)
    return jnp.dot(ones, panel, preferred_element_type=jnp.float32)[0]


def shards(activations, tenant_ids, concept_labels):
    local_tokens = activations.shape[0]
    width = activations.shape[1]
    row_count = lax.axis_size("row")
    col_count = lax.axis_size("col")
    n_x = col_count // Z_HI
    groups = TENANTS * LABELS
    codes = tenant_ids * LABELS + concept_labels
    codes = codes.reshape(1, local_tokens)
    col_piece = _col_piece(activations, col_count)
    col_piece = col_piece.reshape(col_count * local_tokens, col_piece.shape[-1])
    col_panel = lax.all_gather(col_piece, "row", axis=0, tiled=True)
    colsum = jnp.sum(col_piece, axis=0, dtype=jnp.float32, keepdims=True)
    row_slots, code_slots, _, col_total = _row_panel(activations, codes, colsum, row_count, col_count)
    total = col_panel.shape[0]
    row_width = row_slots.shape[-1]
    row_panel = row_slots.reshape(total, row_width)
    gram = jnp.einsum("tf,tg->fg", row_panel, col_panel, preferred_element_type=jnp.float32)
    mean_row = _column_sum(row_panel) / total
    mean_col = col_total[0] / total
    covariance = gram / total - mean_row[:, None] * mean_col[None, :]
    slice_width = width // (row_count * col_count)
    slice_start = lax.axis_index("col") * slice_width
    mean_slice = lax.dynamic_slice_in_dim(mean_row, slice_start, slice_width)
    group_ids = jnp.arange(groups, dtype=jnp.int32)
    onehot_all = code_slots[..., None] == group_ids
    counts = jnp.sum(onehot_all.astype(jnp.float32), axis=(0, 1, 2, 3, 4))
    panel_slice = lax.dynamic_slice_in_dim(row_slots, slice_start, slice_width, 4)
    sums = jnp.einsum(
        "rhxotg,rhxtf->gf",
        onehot_all.astype(jnp.bfloat16),
        panel_slice,
        preferred_element_type=jnp.float32,
    )
    cross = groups / total * (sums - counts[:, None] * mean_slice[None, :])
    return (covariance, cross)


def solution(mesh):
    placed = (P(("row", "col"), None), P(("row", "col")), P(("row", "col")))
    return jax.shard_map(
        shards,
        mesh=mesh,
        in_specs=placed,
        out_specs=(P("row", "col"), P(None, ("row", "col"))),
        check_vma=False,
    )
```

```python
import functools

import jax
import jax.numpy as jnp
from jax import lax
from jax.experimental import pallas as pl
from jax.experimental.pallas import tpu as pltpu
from jax.sharding import PartitionSpec as P

TENANTS = 64
LABELS = 2
MESH = pl.DeviceIdType.MESH
Z_HI = 2


def _row_panel_kernel(n_row, n_x, x_ref, code_ref, cs_ref, p_ref, pc_ref, cs_out, cs_total,
                      s1, r1, s1c, r1c, s2, r2, s2c, r2c, s3, r3, lsem, cs_buf):
    r = lax.axis_index("row")
    c = lax.axis_index("col")
    zh = c // n_x
    x = lax.rem(c, n_x)
    width = p_ref.shape[-1]
    left = zh * n_x + lax.rem(x + n_x - 1, n_x)
    right = zh * n_x + lax.rem(x + 1, n_x)
    sources = [(dz, dr) for dz in range(Z_HI - 1, -1, -1) for dr in range(n_row) if dz or dr]

    def peer(dz, dr):
        return lax.rem(r + dr, n_row), lax.rem(zh + dz, Z_HI) * n_x + x

    barrier = pltpu.get_barrier_semaphore()
    for dz, dr in sources:
        pl.semaphore_signal(barrier, 1, device_id=peer(dz, dr), device_id_type=MESH)
    pl.semaphore_signal(barrier, 1, device_id=(r, left), device_id_type=MESH)
    pl.semaphore_signal(barrier, 1, device_id=(r, right), device_id_type=MESH)
    pl.semaphore_wait(barrier, len(sources) + 2)

    own = pltpu.make_async_copy(
        x_ref.at[:, pl.ds(pl.multiple_of(r * width, width), width)], p_ref.at[r, zh, x], lsem.at[0])
    own_codes = pltpu.make_async_copy(code_ref, pc_ref.at[r, zh, x], lsem.at[1])
    own_sum = pltpu.make_async_copy(cs_ref, cs_out.at[r], lsem.at[2])
    own.start()
    own_codes.start()
    own_sum.start()
    group = Z_HI * n_row
    half_rows = n_row // 2
    stage1 = []
    sums = []
    for i, (dz, dr) in enumerate(sources):
        pr, pc = peer(dz, dr)
        cp = pltpu.make_async_remote_copy(
            src_ref=x_ref.at[:, pl.ds(pl.multiple_of(pr * width, width), width)],
            dst_ref=p_ref.at[r, zh, x],
            send_sem=s1.at[i],
            recv_sem=r1.at[zh * n_row + r],
            device_id=(pr, pc),
            device_id_type=MESH,
        )
        cc = pltpu.make_async_remote_copy(
            src_ref=code_ref,
            dst_ref=pc_ref.at[r, zh, x],
            send_sem=s1c.at[i],
            recv_sem=r1c.at[zh * n_row + r],
            device_id=(pr, pc),
            device_id_type=MESH,
        )
        cp.start()
        cc.start()
        stage1 += [cp, cc]
        if dz == 0:
            cs = pltpu.make_async_remote_copy(
                src_ref=cs_ref,
                dst_ref=cs_out.at[r],
                send_sem=s3.at[dr - 1],
                recv_sem=r3.at[dr - 1],
                device_id=(pr, pc),
                device_id_type=MESH,
            )
            cs.start()
            sums.append(cs)

    def send(src, dst, sems, idx, target):
        return pltpu.make_async_remote_copy(
            src_ref=src, dst_ref=dst, send_sem=sems[0].at[idx], recv_sem=sems[1].at[idx],
            device_id=(r, target), device_id_type=MESH)

    def arrived(plane, row):
        for ref, sems in ((p_ref, (s1, r1)), (pc_ref, (s1c, r1c))):
            pltpu.make_async_remote_copy(
                src_ref=ref.at[row, plane, x], dst_ref=ref.at[row, plane, x],
                send_sem=sems[0].at[0], recv_sem=sems[1].at[plane * n_row + row],
                device_id=(r, right), device_id_type=MESH).wait_recv()

    own.wait()
    own_codes.wait()
    parts = [(1 - zh, 0), (1 - zh, half_rows), (zh, 0), (zh, half_rows)]
    ring = []
    for k, (plane, row0) in enumerate(parts):
        for row in range(row0, row0 + half_rows):
            if k < 2:
                arrived(plane, row)
            else:
                @pl.when(r != row)
                def _(row=row, plane=plane):
                    arrived(plane, row)
        rows = pl.ds(row0, half_rows)
        pair = [
            send(p_ref.at[rows, plane, x], p_ref.at[rows, plane, x], (s2, r2), 2 * k, right),
            send(p_ref.at[rows, plane, x], p_ref.at[rows, plane, x], (s2, r2), 2 * k + 1, left),
            send(pc_ref.at[rows, plane, x], pc_ref.at[rows, plane, x], (s2c, r2c), 2 * k, right),
            send(pc_ref.at[rows, plane, x], pc_ref.at[rows, plane, x], (s2c, r2c), 2 * k + 1, left),
        ]
        for cp in pair:
            cp.start()
        ring.append(pair)

    from_left = lax.rem(x + n_x - 1, n_x)
    from_right = lax.rem(x + 1, n_x)
    fwd = []
    for k, (plane, row0) in enumerate(parts):
        rows = pl.ds(row0, half_rows)
        if k < 2:
            ring[k][1].wait_recv()
            ring[k][3].wait_recv()
            src, target, idx = from_right, left, 8 + k
        else:
            ring[k][0].wait_recv()
            ring[k][2].wait_recv()
            src, target, idx = from_left, right, 8 + k
        pair = [
            send(p_ref.at[rows, plane, src], p_ref.at[rows, plane, src], (s2, r2), idx, target),
            send(pc_ref.at[rows, plane, src], pc_ref.at[rows, plane, src], (s2c, r2c), idx, target),
        ]
        for cp in pair:
            cp.start()
        fwd += pair

    own_sum.wait()
    for cp in sums:
        cp.wait_recv()
    load = pltpu.make_async_copy(cs_out, cs_buf, lsem.at[3])
    load.start()
    load.wait()
    cs_total[...] = jnp.sum(cs_buf[...], axis=0)

    for cp in stage1:
        cp.wait_send()
    for k, pair in enumerate(ring):
        for cp in pair:
            cp.wait_send()
        if k < 2:
            pair[0].wait_recv()
            pair[2].wait_recv()
        else:
            pair[1].wait_recv()
            pair[3].wait_recv()
    for cp in fwd:
        cp.wait()
    for cp in sums:
        cp.wait_send()


def _row_panel(activations, codes, colsum, n_row, n_col):
    tokens = activations.shape[0]
    width = activations.shape[1] // n_row
    n_x = n_col // Z_HI
    assert n_x == 4
    group = Z_HI * n_row
    any_spec = pl.BlockSpec(memory_space=pl.ANY)
    return pl.pallas_call(
        functools.partial(_row_panel_kernel, n_row, n_x),
        out_shape=(
            jax.ShapeDtypeStruct((n_row, Z_HI, n_x, tokens, width), activations.dtype),
            jax.ShapeDtypeStruct((n_row, Z_HI, n_x, 1, tokens), jnp.int32),
            jax.ShapeDtypeStruct((n_row,) + colsum.shape, colsum.dtype),
            jax.ShapeDtypeStruct(colsum.shape, colsum.dtype),
        ),
        in_specs=[any_spec, any_spec, any_spec],
        out_specs=(any_spec, any_spec, any_spec, pl.BlockSpec(memory_space=pltpu.VMEM)),
        scratch_shapes=[
            pltpu.SemaphoreType.DMA((group - 1,)),
            pltpu.SemaphoreType.DMA((group,)),
            pltpu.SemaphoreType.DMA((group - 1,)),
            pltpu.SemaphoreType.DMA((group,)),
            pltpu.SemaphoreType.DMA((12,)),
            pltpu.SemaphoreType.DMA((12,)),
            pltpu.SemaphoreType.DMA((12,)),
            pltpu.SemaphoreType.DMA((12,)),
            pltpu.SemaphoreType.DMA((n_row - 1,)),
            pltpu.SemaphoreType.DMA((n_row - 1,)),
            pltpu.SemaphoreType.DMA((4,)),
            pltpu.VMEM((n_row,) + colsum.shape, colsum.dtype),
        ],
        compiler_params=pltpu.CompilerParams(collective_id=0, has_side_effects=True),
    )(activations, codes, colsum)


def _col_piece_kernel(n_col, x_ref, code_ref, o_ref, code_out, send_sem, recv_sem, lsem):
    r = lax.axis_index("row")
    c = lax.axis_index("col")
    width = o_ref.shape[-1]
    barrier = pltpu.get_barrier_semaphore()
    for k in range(1, n_col):
        pl.semaphore_signal(barrier, 1, device_id=(r, lax.rem(c + k, n_col)), device_id_type=MESH)
    pl.semaphore_wait(barrier, n_col - 1)
    own = pltpu.make_async_copy(
        x_ref.at[:, pl.ds(pl.multiple_of(c * width, width), width)], o_ref.at[c], lsem.at[0])
    own.start()
    copies = []
    for k in range(1, n_col):
        dst = lax.rem(c + k, n_col)
        cp = pltpu.make_async_remote_copy(
            src_ref=x_ref.at[:, pl.ds(pl.multiple_of(dst * width, width), width)],
            dst_ref=o_ref.at[c],
            send_sem=send_sem.at[k - 1],
            recv_sem=recv_sem.at[k - 1],
            device_id=(r, dst),
            device_id_type=MESH,
        )
        cp.start()
        copies.append(cp)
    keep = pltpu.make_async_copy(code_ref, code_out, lsem.at[1])
    keep.start()
    own.wait()
    keep.wait()
    for cp in copies:
        cp.wait()


def _col_piece(activations, codes, n_col):
    tokens = activations.shape[0]
    width = activations.shape[1] // n_col
    any_spec = pl.BlockSpec(memory_space=pl.ANY)
    return pl.pallas_call(
        functools.partial(_col_piece_kernel, n_col),
        out_shape=(
            jax.ShapeDtypeStruct((n_col, tokens, width), activations.dtype),
            jax.ShapeDtypeStruct(codes.shape, codes.dtype),
        ),
        in_specs=[any_spec, any_spec],
        out_specs=(any_spec, any_spec),
        scratch_shapes=[
            pltpu.SemaphoreType.DMA((n_col - 1,)),
            pltpu.SemaphoreType.DMA((n_col - 1,)),
            pltpu.SemaphoreType.DMA((2,)),
        ],
        compiler_params=pltpu.CompilerParams(collective_id=1, has_side_effects=True),
    )(activations, codes)


def _column_sum(panel):
    ones = jnp.ones((8, panel.shape[0]), panel.dtype)
    return jnp.dot(ones, panel, preferred_element_type=jnp.float32)[0]


def shards(activations, tenant_ids, concept_labels):
    local_tokens = activations.shape[0]
    width = activations.shape[1]
    row_count = lax.axis_size("row")
    col_count = lax.axis_size("col")
    n_x = col_count // Z_HI
    groups = TENANTS * LABELS
    codes = tenant_ids * LABELS + concept_labels
    col_piece, codes = _col_piece(activations, codes.reshape(1, local_tokens), col_count)
    col_piece = col_piece.reshape(col_count * local_tokens, col_piece.shape[-1])
    col_panel = lax.all_gather(col_piece, "row", axis=0, tiled=True)
    colsum = jnp.sum(col_piece, axis=0, dtype=jnp.float32, keepdims=True)
    row_slots, code_slots, _, col_total = _row_panel(activations, codes, colsum, row_count, col_count)
    total = col_panel.shape[0]
    row_width = row_slots.shape[-1]
    row_panel = row_slots.reshape(total, row_width)
    gram = jnp.einsum("tf,tg->fg", row_panel, col_panel, preferred_element_type=jnp.float32)
    mean_row = _column_sum(row_panel) / total
    mean_col = col_total[0] / total
    covariance = gram / total - mean_row[:, None] * mean_col[None, :]
    slice_width = width // (row_count * col_count)
    slice_start = lax.axis_index("col") * slice_width
    mean_slice = lax.dynamic_slice_in_dim(mean_row, slice_start, slice_width)
    group_ids = jnp.arange(groups, dtype=jnp.int32)
    onehot_all = code_slots[..., None] == group_ids
    counts = jnp.sum(onehot_all.astype(jnp.float32), axis=(0, 1, 2, 3, 4))
    panel_slice = lax.dynamic_slice_in_dim(row_slots, slice_start, slice_width, 4)
    sums = jnp.einsum(
        "rhxotg,rhxtf->gf",
        onehot_all.astype(jnp.bfloat16),
        panel_slice,
        preferred_element_type=jnp.float32,
    )
    cross = groups / total * (sums - counts[:, None] * mean_slice[None, :])
    return (covariance, cross)


def solution(mesh):
    placed = (P(("row", "col"), None), P(("row", "col")), P(("row", "col")))
    return jax.shard_map(
        shards,
        mesh=mesh,
        in_specs=placed,
        out_specs=(P("row", "col"), P(None, ("row", "col"))),
        check_vma=False,
    )
```
